256 devices in a mesh: layer: 4 (over x_lo, core), row: 64 (over y, z, x_hi).
Axes of the slice: x: 4 (x_hi: 2, x_lo: 2; x = x_hi * 2 + x_lo), y: 4, z: 8, core: 2. Of those that a mesh axis runs over, the one named last changes fastest.
Arguments:
- density: bfloat16 [40960, 2048], P('row', 'layer'), may hold values from -1 to 1, as said below
- pattern: int32 [640, 32], P('row', 'layer'), may hold values 0 or 1
Outputs:
- purified: float32 [40960, 2048], P('row', 'layer')
The draws below stay inside these ranges and needn't reach their ends.
Inputs may be any that keep to these rules, and one draw needn't show every extreme that they name: `density`: entry (r, o * 64 + c) is P's entry in row r and column ((r // 64 + o - 16) mod 640) * 64 + c.
All inputs are finite; a program needn't handle non-finite values. No bound on the sum of `pattern` on one device may be relied on, other than what follows from the above.
Results may differ from the reference program's by a relative error of at most 0.0065.
Values may be sent and summed in bfloat16 or wider, within the bound.
A program may use at most 192 MiB of HBM per device.

```python
import jax
import jax.numpy as jnp
from jax import lax

BS = 64
NOFF = 32
HALF = 16
NB = 640


def draw_density(key, part):
    rows_all = NB * BS
    cols_all = NOFF * BS
    key_noise, key_diag = jax.random.split(key, 2)
    noise = jax.random.truncated_normal(key_noise, -4.0, 4.0, (rows_all, cols_all), jnp.float32) * 0.05
    diagonal = jax.random.uniform(key_diag, (rows_all, 1), jnp.float32, 0.3, 0.7)
    row_ids = jnp.arange(rows_all, dtype=jnp.int32)[:, None]
    col_ids = jnp.arange(cols_all, dtype=jnp.int32)[None, :]
    on_diag = (col_ids // BS == NOFF // 2) & (col_ids % BS == row_ids % BS)
    return jnp.where(on_diag, diagonal, noise).astype(jnp.bfloat16)


def plant(drawn, rng, least, top_value):
    longest = drawn.shape.index(max(drawn.shape))
    spots = []
    for shift in (0, 1):
        where = [jax.random.randint(jax.random.fold_in(rng, axis), (), 0, length) for axis, length in enumerate(drawn.shape)]
        where[longest] = (where[longest] + shift) % drawn.shape[longest]
        spots.append(tuple(where))
    return drawn.at[spots[0]].set(least).at[spots[1]].set(top_value)


def setup_inputs(seed: int = 0) -> dict:
    splits = jax.random.split(jax.random.key(seed), 3)
    return {
        "density": draw_density(jax.random.fold_in(splits[2], 71), 0),
        "pattern": plant((jax.random.randint(splits[1], (NB, NOFF), 0, 5) < 4).astype(jnp.int32), jax.random.fold_in(splits[1], 1), 0, 1),
    }


def multiply(left, right):
    doubled = jnp.concatenate([right, right], axis=0)

    def advance(running, offset_idx):
        column_blocks = lax.dynamic_index_in_dim(left, offset_idx, 2, keepdims=False)
        first_row = jnp.mod(offset_idx - HALF, NB).astype(jnp.int32)
        near_rows = lax.dynamic_slice_in_dim(doubled, first_row, NB, 0)
        product = jnp.einsum('ixy,iybz->ixbz', column_blocks.astype(jnp.float32), near_rows.astype(jnp.float32), precision=lax.Precision.HIGHEST)
        padded = jnp.pad(product, ((0, 0), (0, 0), (NOFF, NOFF), (0, 0)))
        moved = lax.dynamic_slice_in_dim(padded, (NOFF - offset_idx + HALF).astype(jnp.int32), NOFF, 2)
        return running + moved, None

    initial = jnp.zeros((NB, BS, NOFF, BS), jnp.float32)
    running, unused = lax.scan(advance, initial, jnp.arange(NOFF, dtype=jnp.int32))
    return running


def reference(density, pattern):
    keep = pattern.astype(jnp.bfloat16)[:, None, :, None]
    blocks = density.reshape(NB, BS, NOFF, BS) * keep
    pattern_f = pattern.astype(jnp.float32)[:, None, :, None]
    square = (multiply(blocks, blocks) * pattern_f).astype(jnp.bfloat16)
    cubic = multiply(square, blocks) * pattern_f
    purified = 3.0 * square.astype(jnp.float32) - 2.0 * cubic
    return purified.reshape(NB * BS, NOFF * BS)
```

```python
import jax
import jax.numpy as jnp
from jax import lax
from jax.sharding import PartitionSpec as P


def shifted(value, axis, steps):
    count = lax.axis_size(axis)
    pairs = [(source, (source + steps) % count) for source in range(count)]
    return lax.ppermute(value, axis, pairs)


def skew_rows(band, shift_total):
    n, bs, width = band.shape
    pieces = [
        jnp.pad(band[i], ((0, 0), (i * bs, (shift_total - i) * bs))) for i in range(n)
    ]
    return jnp.stack(pieces, axis=0)


def body(density, pattern):
    rows_dev, slab_cols = density.shape
    block_rows, slab_offsets = pattern.shape
    bs = rows_dev // block_rows
    layers = lax.axis_size("layer")
    offsets = slab_offsets * layers
    half = offsets // 2
    layer_id = lax.axis_index("layer")

    keep = pattern.astype(jnp.bfloat16)[:, None, :, None]
    masked = (density.reshape(block_rows, bs, slab_offsets, bs) * keep).reshape(rows_dev, slab_cols)
    own_band = lax.all_gather(masked, "layer", axis=1, tiled=True)

    total_rows = block_rows + offsets - 1
    below = half
    above = total_rows - half - block_rows
    lower_parts = []
    dist = 1
    need = below
    while need > 0:
        take = min(block_rows, need)
        lower_parts.insert(0, shifted(own_band[(block_rows - take) * bs:], "row", dist))
        need -= take
        dist += 1
    upper_parts = []
    dist = 1
    need = above
    while need > 0:
        take = min(block_rows, need)
        upper_parts.append(shifted(own_band[: take * bs], "row", -dist))
        need -= take
        dist += 1
    halo = jnp.concatenate(lower_parts + [own_band] + upper_parts, axis=0)
    halo = halo.reshape(total_rows, bs, offsets * bs)

    width = slab_offsets + block_rows - 1
    pad_l = total_rows - 1 - half
    pad_r = max(0, slab_offsets * (layers - 1) + half + width - offsets)
    halo_pad = jnp.pad(halo, ((0, 0), (0, 0), (pad_l * bs, pad_r * bs)))
    base = layer_id * slab_offsets
    right_rows = []
    for t in range(total_rows):
        start = (base + (half + pad_l - t)) * bs
        right_rows.append(lax.dynamic_slice_in_dim(halo_pad[t], start, width * bs, axis=1))
    right = jnp.stack(right_rows, axis=0).reshape(total_rows * bs, width * bs)

    pattern_f = pattern.astype(jnp.float32)[:, None, :, None]

    def product(left_band):
        left = skew_rows(left_band.reshape(block_rows, bs, offsets * bs), block_rows - 1)
        left = left.reshape(rows_dev, total_rows * bs)
        dense = jnp.dot(left, right, preferred_element_type=jnp.float32)
        dense = dense.reshape(block_rows, bs, width * bs)
        out = jnp.stack(
            [dense[i, :, i * bs: (i + slab_offsets) * bs] for i in range(block_rows)], axis=0
        )
        return out.reshape(block_rows, bs, slab_offsets, bs) * pattern_f

    square = product(own_band).astype(jnp.bfloat16)
    square_full = lax.all_gather(square.reshape(rows_dev, slab_cols), "layer", axis=1, tiled=True)
    cubic = product(square_full)
    purified = 3.0 * square.astype(jnp.float32) - 2.0 * cubic
    return purified.reshape(rows_dev, slab_cols)


def solution(mesh):
    placed = (P("row", "layer"), P("row", "layer"))
    return jax.shard_map(
        body, mesh=mesh, in_specs=placed, out_specs=P("row", "layer"), check_vma=False
    )
```

```python
import jax
import jax.numpy as jnp
from jax import lax
from jax.sharding import PartitionSpec as P


def shifted(value, axis, steps):
    count = lax.axis_size(axis)
    pairs = [(source, (source + steps) % count) for source in range(count)]
    return lax.ppermute(value, axis, pairs)


def skew_rows(band, shift_total):
    n, bs, width = band.shape
    pieces = [
        jnp.pad(band[i], ((0, 0), (i * bs, (shift_total - i) * bs))) for i in range(n)
    ]
    return jnp.stack(pieces, axis=0)


def body(density, pattern):
    rows_dev, slab_cols = density.shape
    block_rows, slab_offsets = pattern.shape
    bs = rows_dev // block_rows
    layers = lax.axis_size("layer")
    offsets = slab_offsets * layers
    half = offsets // 2
    layer_id = lax.axis_index("layer")

    keep = pattern.astype(jnp.bfloat16)[:, None, :, None]
    masked = (density.reshape(block_rows, bs, slab_offsets, bs) * keep).reshape(rows_dev, slab_cols)
    own_band = lax.all_gather(masked, "layer", axis=1, tiled=True)

    total_rows = block_rows + offsets - 1
    width = slab_offsets + block_rows - 1
    pad_l = total_rows - 1 - half
    pad_r = max(0, slab_offsets * (layers - 1) + half + width - offsets)
    band_pad = jnp.pad(
        own_band.reshape(block_rows, bs, offsets * bs), ((0, 0), (0, 0), (pad_l * bs, pad_r * bs))
    )
    base = layer_id * slab_offsets

    def windows(shift, first, last):
        rows = []
        for j in range(first, last):
            start = (base + block_rows * shift - j + pad_l) * bs
            rows.append(lax.dynamic_slice_in_dim(band_pad[j], start, width * bs, axis=1))
        return jnp.stack(rows, axis=0)

    below = half
    above = total_rows - half - block_rows
    lower_parts = []
    dist = 1
    need = below
    while need > 0:
        take = min(block_rows, need)
        lower_parts.insert(0, shifted(windows(dist, block_rows - take, block_rows), "row", dist))
        need -= take
        dist += 1
    upper_parts = []
    dist = 1
    need = above
    while need > 0:
        take = min(block_rows, need)
        upper_parts.append(shifted(windows(-dist, 0, take), "row", -dist))
        need -= take
        dist += 1
    right = jnp.concatenate(lower_parts + [windows(0, 0, block_rows)] + upper_parts, axis=0)
    right = right.reshape(total_rows * bs, width * bs)

    pattern_f = pattern.astype(jnp.float32)[:, None, :, None]

    def product(left_band):
        left = skew_rows(left_band.reshape(block_rows, bs, offsets * bs), block_rows - 1)
        left = left.reshape(rows_dev, total_rows * bs)
        dense = jnp.dot(left, right, preferred_element_type=jnp.float32)
        dense = dense.reshape(block_rows, bs, width * bs)
        out = jnp.stack(
            [dense[i, :, i * bs: (i + slab_offsets) * bs] for i in range(block_rows)], axis=0
        )
        return out.reshape(block_rows, bs, slab_offsets, bs) * pattern_f

    square = product(own_band).astype(jnp.bfloat16)
    square_full = lax.all_gather(square.reshape(rows_dev, slab_cols), "layer", axis=1, tiled=True)
    cubic = product(square_full)
    purified = 3.0 * square.astype(jnp.float32) - 2.0 * cubic
    return purified.reshape(rows_dev, slab_cols)


def solution(mesh):
    placed = (P("row", "layer"), P("row", "layer"))
    return jax.shard_map(
        body, mesh=mesh, in_specs=placed, out_specs=P("row", "layer"), check_vma=False
    )
```

```python
import jax
import jax.numpy as jnp
from jax import lax
from jax.sharding import PartitionSpec as P
from jax.experimental import pallas as pl
from jax.experimental.pallas import tpu as pltpu

MESH_AXES = ("layer", "row")


def _peer(axis, sizes, step):
    coords = [lax.axis_index(name) for name in MESH_AXES]
    k = MESH_AXES.index(axis)
    coords[k] = lax.rem(coords[k] + step + sizes[k], sizes[k])
    return tuple(coords)


def _greet(axis, sizes, steps):
    k = MESH_AXES.index(axis)
    peers = sorted({(s % sizes[k]) for s in steps} | {(-s) % sizes[k] for s in steps})
    barrier = pltpu.get_barrier_semaphore()
    for p in peers:
        pl.semaphore_signal(barrier, inc=1, device_id=_peer(axis, sizes, p),
                            device_id_type=pl.DeviceIdType.MESH)
    pl.semaphore_wait(barrier, len(peers))


def _row_exchange_kernel(sizes, steps, row_starts, own_start, *refs):
    n = len(steps)
    srcs = refs[:n]
    own_ref = refs[n]
    out_ref = refs[n + 1]
    send_sem, recv_sem, local_sem = refs[n + 2:]
    _greet("row", sizes, steps)
    copies = []
    for k, step in enumerate(steps):
        rows = srcs[k].shape[0]
        copy = pltpu.make_async_remote_copy(
            src_ref=srcs[k],
            dst_ref=out_ref.at[pl.ds(row_starts[k], rows)],
            send_sem=send_sem.at[k],
            recv_sem=recv_sem.at[k],
            device_id=_peer("row", sizes, step),
            device_id_type=pl.DeviceIdType.MESH,
        )
        copy.start()
        copies.append(copy)
    local = pltpu.make_async_copy(
        own_ref, out_ref.at[pl.ds(own_start, own_ref.shape[0])], local_sem.at[0]
    )
    local.start()
    local.wait()
    for copy in copies:
        copy.wait()


def row_exchange(sizes, steps, row_starts, own_start, total_rows, sends, own):
    n = len(steps)
    shape = (total_rows,) + own.shape[1:]
    any_spec = pl.BlockSpec(memory_space=pl.ANY)
    return pl.pallas_call(
        lambda *refs: _row_exchange_kernel(sizes, steps, row_starts, own_start, *refs),
        out_shape=jax.ShapeDtypeStruct(shape, own.dtype),
        in_specs=[any_spec] * (n + 1),
        out_specs=any_spec,
        scratch_shapes=[
            pltpu.SemaphoreType.DMA((n,)),
            pltpu.SemaphoreType.DMA((n,)),
            pltpu.SemaphoreType.DMA((1,)),
        ],
        compiler_params=pltpu.CompilerParams(collective_id=0, has_side_effects=True),
        name="row_exchange",
    )(*sends, own)


def _layer_gather_kernel(sizes, *refs):
    src_ref, out_ref, send_sem, recv_sem, local_sem = refs
    k = MESH_AXES.index("layer")
    count = sizes[k]
    steps = list(range(1, count))
    me = lax.axis_index("layer")
    width = src_ref.shape[1]
    _greet("layer", sizes, steps)
    mine = out_ref.at[:, pl.ds(pl.multiple_of(me * width, width), width)]
    copies = []
    for j, step in enumerate(steps):
        copy = pltpu.make_async_remote_copy(
            src_ref=src_ref,
            dst_ref=mine,
            send_sem=send_sem.at[j],
            recv_sem=recv_sem.at[j],
            device_id=_peer("layer", sizes, step),
            device_id_type=pl.DeviceIdType.MESH,
        )
        copy.start()
        copies.append(copy)
    local = pltpu.make_async_copy(src_ref, mine, local_sem.at[0])
    local.start()
    local.wait()
    for copy in copies:
        copy.wait()


def layer_gather(sizes, slab, collective_id):
    count = sizes[MESH_AXES.index("layer")]
    any_spec = pl.BlockSpec(memory_space=pl.ANY)
    return pl.pallas_call(
        lambda *refs: _layer_gather_kernel(sizes, *refs),
        out_shape=jax.ShapeDtypeStruct((slab.shape[0], slab.shape[1] * count), slab.dtype),
        in_specs=[any_spec],
        out_specs=any_spec,
        scratch_shapes=[
            pltpu.SemaphoreType.DMA((count - 1,)),
            pltpu.SemaphoreType.DMA((count - 1,)),
            pltpu.SemaphoreType.DMA((1,)),
        ],
        compiler_params=pltpu.CompilerParams(collective_id=collective_id, has_side_effects=True),
        name="layer_gather",
    )(slab)


def shifted(value, axis, steps):
    count = lax.axis_size(axis)
    pairs = [(source, (source + steps) % count) for source in range(count)]
    return lax.ppermute(value, axis, pairs)


def skew_rows(band, shift_total):
    n, bs, width = band.shape
    pieces = [
        jnp.pad(band[i], ((0, 0), (i * bs, (shift_total - i) * bs))) for i in range(n)
    ]
    return jnp.stack(pieces, axis=0)


def body(density, pattern):
    rows_dev, slab_cols = density.shape
    block_rows, slab_offsets = pattern.shape
    bs = rows_dev // block_rows
    layers = lax.axis_size("layer")
    offsets = slab_offsets * layers
    half = offsets // 2
    layer_id = lax.axis_index("layer")
    sizes = tuple(lax.axis_size(name) for name in MESH_AXES)

    keep = pattern.astype(jnp.bfloat16)[:, None, :, None]
    masked = (density.reshape(block_rows, bs, slab_offsets, bs) * keep).reshape(rows_dev, slab_cols)
    own_band = layer_gather(sizes, masked, 1)

    total_rows = block_rows + offsets - 1
    width = slab_offsets + block_rows - 1
    pad_l = total_rows - 1 - half
    pad_r = max(0, slab_offsets * (layers - 1) + half + width - offsets)
    band_pad = jnp.pad(
        own_band.reshape(block_rows, bs, offsets * bs), ((0, 0), (0, 0), (pad_l * bs, pad_r * bs))
    )
    base = layer_id * slab_offsets

    def windows(shift, first, last):
        rows = []
        for j in range(first, last):
            start = (base + block_rows * shift - j + pad_l) * bs
            rows.append(lax.dynamic_slice_in_dim(band_pad[j], start, width * bs, axis=1))
        return jnp.stack(rows, axis=0)

    below = half
    above = total_rows - half - block_rows
    steps, sends, row_starts = [], [], []
    dist, need = 1, below
    while need > 0:
        take = min(block_rows, need)
        sends.append(windows(dist, block_rows - take, block_rows))
        steps.append(dist)
        row_starts.append(need - take)
        need -= take
        dist += 1
    dist, need = 1, above
    while need > 0:
        take = min(block_rows, need)
        sends.append(windows(-dist, 0, take))
        steps.append(-dist)
        row_starts.append(below + block_rows + (above - need))
        need -= take
        dist += 1
    right = row_exchange(sizes, steps, row_starts, below, total_rows, sends, windows(0, 0, block_rows))
    right = right.reshape(total_rows * bs, width * bs)

    pattern_f = pattern.astype(jnp.float32)[:, None, :, None]

    def product(left_band):
        left = skew_rows(left_band.reshape(block_rows, bs, offsets * bs), block_rows - 1)
        left = left.reshape(rows_dev, total_rows * bs)
        dense = jnp.dot(left, right, preferred_element_type=jnp.float32)
        dense = dense.reshape(block_rows, bs, width * bs)
        out = jnp.stack(
            [dense[i, :, i * bs: (i + slab_offsets) * bs] for i in range(block_rows)], axis=0
        )
        return out.reshape(block_rows, bs, slab_offsets, bs) * pattern_f

    square = product(own_band).astype(jnp.bfloat16)
    square_full = layer_gather(sizes, square.reshape(rows_dev, slab_cols), 1)
    cubic = product(square_full)
    purified = 3.0 * square.astype(jnp.float32) - 2.0 * cubic
    return purified.reshape(rows_dev, slab_cols)


def solution(mesh):
    placed = (P("row", "layer"), P("row", "layer"))
    return jax.shard_map(
        body, mesh=mesh, in_specs=placed, out_specs=P("row", "layer"), check_vma=False
    )
```

```python
import jax
import jax.numpy as jnp
from jax import lax
from jax.sharding import PartitionSpec as P
from jax.experimental import pallas as pl
from jax.experimental.pallas import tpu as pltpu

MESH_AXES = ("layer", "row")


def _peer(sizes, layer_shift, row_shift):
    layer = lax.axis_index("layer")
    row = lax.axis_index("row")
    return (
        lax.rem(layer + layer_shift + sizes[0], sizes[0]),
        lax.rem(row + row_shift + sizes[1], sizes[1]),
    )


def _greet(sizes, shifts):
    barrier = pltpu.get_barrier_semaphore()
    for layer_shift, row_shift in shifts:
        pl.semaphore_signal(barrier, inc=1, device_id=_peer(sizes, layer_shift, row_shift),
                            device_id_type=pl.DeviceIdType.MESH)
    pl.semaphore_wait(barrier, len(shifts))


def _row_exchange_kernel(sizes, shifts, row_starts, own_start, *refs):
    n = len(shifts)
    srcs = refs[:n]
    own_ref = refs[n]
    out_ref = refs[n + 1]
    send_sem, recv_sem, local_sem = refs[n + 2:]
    _greet(sizes, shifts)
    copies = []
    for k, (layer_shift, row_shift) in enumerate(shifts):
        rows = srcs[k].shape[0]
        copy = pltpu.make_async_remote_copy(
            src_ref=srcs[k],
            dst_ref=out_ref.at[pl.ds(row_starts[k], rows)],
            send_sem=send_sem.at[k],
            recv_sem=recv_sem.at[k],
            device_id=_peer(sizes, layer_shift, row_shift),
            device_id_type=pl.DeviceIdType.MESH,
        )
        copy.start()
        copies.append(copy)
    local = pltpu.make_async_copy(
        own_ref, out_ref.at[pl.ds(own_start, own_ref.shape[0])], local_sem.at[0]
    )
    local.start()
    local.wait()
    for copy in copies:
        copy.wait()


def row_exchange(sizes, shifts, row_starts, own_start, total_rows, sends, own):
    n = len(shifts)
    shape = (total_rows,) + own.shape[1:]
    any_spec = pl.BlockSpec(memory_space=pl.ANY)
    return pl.pallas_call(
        lambda *refs: _row_exchange_kernel(sizes, shifts, row_starts, own_start, *refs),
        out_shape=jax.ShapeDtypeStruct(shape, own.dtype),
        in_specs=[any_spec] * (n + 1),
        out_specs=any_spec,
        scratch_shapes=[
            pltpu.SemaphoreType.DMA((n,)),
            pltpu.SemaphoreType.DMA((n,)),
            pltpu.SemaphoreType.DMA((1,)),
        ],
        compiler_params=pltpu.CompilerParams(collective_id=0, has_side_effects=True),
        name="row_exchange",
    )(*sends, own)


def _layer_gather_kernel(sizes, *refs):
    src_ref, out_ref, send_sem, recv_sem, local_sem = refs
    count = sizes[0]
    me = lax.axis_index("layer")
    width = src_ref.shape[1]
    core_shift = 1 - 2 * lax.rem(me, 2)
    far = count // 2
    _greet(sizes, [(far, 0), (core_shift, 0)])

    def cols(layer):
        return out_ref.at[:, pl.ds(pl.multiple_of(layer * width, width), width)]

    mine = cols(me)
    to_far = pltpu.make_async_remote_copy(
        src_ref=src_ref, dst_ref=mine, send_sem=send_sem.at[0], recv_sem=recv_sem.at[0],
        device_id=_peer(sizes, far, 0), device_id_type=pl.DeviceIdType.MESH,
    )
    to_core = pltpu.make_async_remote_copy(
        src_ref=src_ref, dst_ref=mine, send_sem=send_sem.at[1], recv_sem=recv_sem.at[1],
        device_id=_peer(sizes, core_shift, 0), device_id_type=pl.DeviceIdType.MESH,
    )
    to_far.start()
    to_core.start()
    local = pltpu.make_async_copy(src_ref, mine, local_sem.at[0])
    local.start()
    far_layer = lax.rem(me + far, count)
    to_far.wait_recv()
    forward = pltpu.make_async_remote_copy(
        src_ref=cols(far_layer), dst_ref=cols(far_layer), send_sem=send_sem.at[2],
        recv_sem=recv_sem.at[2], device_id=_peer(sizes, core_shift, 0),
        device_id_type=pl.DeviceIdType.MESH,
    )
    forward.start()
    local.wait()
    to_far.wait_send()
    to_core.wait()
    forward.wait()


def layer_gather(sizes, slab, collective_id):
    count = sizes[0]
    any_spec = pl.BlockSpec(memory_space=pl.ANY)
    return pl.pallas_call(
        lambda *refs: _layer_gather_kernel(sizes, *refs),
        out_shape=jax.ShapeDtypeStruct((slab.shape[0], slab.shape[1] * count), slab.dtype),
        in_specs=[any_spec],
        out_specs=any_spec,
        scratch_shapes=[
            pltpu.SemaphoreType.DMA((3,)),
            pltpu.SemaphoreType.DMA((3,)),
            pltpu.SemaphoreType.DMA((1,)),
        ],
        compiler_params=pltpu.CompilerParams(collective_id=collective_id, has_side_effects=True),
        name="layer_gather",
    )(slab)


def shifted(value, axis, steps):
    count = lax.axis_size(axis)
    pairs = [(source, (source + steps) % count) for source in range(count)]
    return lax.ppermute(value, axis, pairs)


def skew_rows(band, shift_total):
    n, bs, width = band.shape
    pieces = [
        jnp.pad(band[i], ((0, 0), (i * bs, (shift_total - i) * bs))) for i in range(n)
    ]
    return jnp.stack(pieces, axis=0)


def body(density, pattern):
    rows_dev, slab_cols = density.shape
    block_rows, slab_offsets = pattern.shape
    bs = rows_dev // block_rows
    layers = lax.axis_size("layer")
    offsets = slab_offsets * layers
    half = offsets // 2
    layer_id = lax.axis_index("layer")
    sizes = tuple(lax.axis_size(name) for name in MESH_AXES)

    keep = pattern.astype(jnp.bfloat16)[:, None, :, None]
    masked = (density.reshape(block_rows, bs, slab_offsets, bs) * keep).reshape(rows_dev, slab_cols)
    own_band = layer_gather(sizes, masked, 1)

    total_rows = block_rows + offsets - 1
    width = slab_offsets + block_rows - 1
    pad_l = total_rows - 1 - half
    pad_r = max(0, slab_offsets * (layers - 1) + half + width - offsets)
    band_pad = jnp.pad(
        own_band.reshape(block_rows, bs, offsets * bs), ((0, 0), (0, 0), (pad_l * bs, pad_r * bs))
    )
    base = layer_id * slab_offsets

    far = layers // 2

    def windows(shift, first, last, layer_shift=0):
        rows = []
        target = lax.rem(layer_id + layer_shift, layers) * slab_offsets
        for j in range(first, last):
            start = (target + block_rows * shift - j + pad_l) * bs
            rows.append(lax.dynamic_slice_in_dim(band_pad[j], start, width * bs, axis=1))
        return jnp.stack(rows, axis=0)

    below = half
    above = total_rows - half - block_rows
    steps, sends, row_starts = [], [], []
    dist, need = 1, below
    while need > 0:
        take = min(block_rows, need)
        layer_shift = far if dist == 1 else 0
        sends.append(windows(dist, block_rows - take, block_rows, layer_shift))
        steps.append((layer_shift, dist))
        row_starts.append(need - take)
        need -= take
        dist += 1
    dist, need = 1, above
    while need > 0:
        take = min(block_rows, need)
        layer_shift = far if dist == 1 else 0
        sends.append(windows(-dist, 0, take, layer_shift))
        steps.append((layer_shift, -dist))
        row_starts.append(below + block_rows + (above - need))
        need -= take
        dist += 1
    right = row_exchange(sizes, steps, row_starts, below, total_rows, sends, windows(0, 0, block_rows))
    right = right.reshape(total_rows * bs, width * bs)

    pattern_f = pattern.astype(jnp.float32)[:, None, :, None]

    def product(left_band):
        left = skew_rows(left_band.reshape(block_rows, bs, offsets * bs), block_rows - 1)
        left = left.reshape(rows_dev, total_rows * bs)
        dense = jnp.dot(left, right, preferred_element_type=jnp.float32)
        dense = dense.reshape(block_rows, bs, width * bs)
        out = jnp.stack(
            [dense[i, :, i * bs: (i + slab_offsets) * bs] for i in range(block_rows)], axis=0
        )
        return out.reshape(block_rows, bs, slab_offsets, bs) * pattern_f

    square = product(own_band).astype(jnp.bfloat16)
    square_full = layer_gather(sizes, square.reshape(rows_dev, slab_cols), 1)
    cubic = product(square_full)
    purified = 3.0 * square.astype(jnp.float32) - 2.0 * cubic
    return purified.reshape(rows_dev, slab_cols)


def solution(mesh):
    placed = (P("row", "layer"), P("row", "layer"))
    return jax.shard_map(
        body, mesh=mesh, in_specs=placed, out_specs=P("row", "layer"), check_vma=False
    )
```

```python
import jax
import jax.numpy as jnp
from jax import lax
from jax.sharding import PartitionSpec as P
from jax.experimental import pallas as pl
from jax.experimental.pallas import tpu as pltpu

MESH_AXES = ("layer", "row")


def _peer(sizes, layer_shift, row_shift):
    layer = lax.axis_index("layer")
    row = lax.axis_index("row")
    return (
        lax.rem(layer + layer_shift + sizes[0], sizes[0]),
        lax.rem(row + row_shift + sizes[1], sizes[1]),
    )


def _greet(sizes, shifts):
    barrier = pltpu.get_barrier_semaphore()
    for layer_shift, row_shift in shifts:
        pl.semaphore_signal(barrier, inc=1, device_id=_peer(sizes, layer_shift, row_shift),
                            device_id_type=pl.DeviceIdType.MESH)
    pl.semaphore_wait(barrier, len(shifts))


def _row_exchange_kernel(sizes, shifts, row_starts, own_start, pair_shifts, pair_starts, *refs):
    n = len(shifts)
    m = len(pair_shifts)
    srcs = refs[:n]
    own_ref = refs[n]
    pair_srcs = refs[n + 1:n + 1 + m]
    out_ref, pair_ref = refs[n + 1 + m:n + 3 + m]
    send_sem, recv_sem, pair_send, pair_recv, fwd_send, fwd_recv, local_sem = refs[n + 3 + m:]
    me = lax.axis_index("layer")
    core = lax.rem(me, 2)
    core_shift = 1 - 2 * core
    _greet(sizes, list(shifts) + list(pair_shifts) + [(core_shift, 0)])
    copies = []
    for k, (layer_shift, row_shift) in enumerate(shifts):
        rows = srcs[k].shape[0]
        copy = pltpu.make_async_remote_copy(
            src_ref=srcs[k],
            dst_ref=out_ref.at[pl.ds(row_starts[k], rows)],
            send_sem=send_sem.at[k],
            recv_sem=recv_sem.at[k],
            device_id=_peer(sizes, layer_shift, row_shift),
            device_id_type=pl.DeviceIdType.MESH,
        )
        copy.start()
        copies.append(copy)
    pair_copies = []
    for k, (layer_shift, row_shift) in enumerate(pair_shifts):
        rows = pair_srcs[k].shape[0]
        copy = pltpu.make_async_remote_copy(
            src_ref=pair_srcs[k],
            dst_ref=pair_ref.at[pl.ds(pair_starts[k] + core * rows, rows)],
            send_sem=pair_send.at[k],
            recv_sem=pair_recv.at[k],
            device_id=_peer(sizes, layer_shift, row_shift),
            device_id_type=pl.DeviceIdType.MESH,
        )
        copy.start()
        pair_copies.append(copy)
    local = pltpu.make_async_copy(
        own_ref, out_ref.at[pl.ds(own_start, own_ref.shape[0])], local_sem.at[0]
    )
    local.start()
    forwards = []
    for k in range(m):
        rows = pair_srcs[k].shape[0]
        pair_copies[k].wait_recv()
        held = pair_ref.at[pl.ds(pair_starts[k] + core * rows, rows)]
        forward = pltpu.make_async_remote_copy(
            src_ref=held,
            dst_ref=held,
            send_sem=fwd_send.at[k],
            recv_sem=fwd_recv.at[k],
            device_id=_peer(sizes, core_shift, 0),
            device_id_type=pl.DeviceIdType.MESH,
        )
        forward.start()
        forwards.append(forward)
    local.wait()
    for copy in copies:
        copy.wait()
    for k in range(m):
        pair_copies[k].wait_send()
        forwards[k].wait()


def row_exchange(sizes, shifts, row_starts, own_start, total_rows, sends, own,
                 pair_shifts, pair_starts, pair_rows, pair_sends):
    n = len(shifts)
    m = len(pair_shifts)
    shape = (total_rows,) + own.shape[1:]
    pair_shape = (pair_rows,) + pair_sends[0].shape[1:]
    any_spec = pl.BlockSpec(memory_space=pl.ANY)
    return pl.pallas_call(
        lambda *refs: _row_exchange_kernel(
            sizes, shifts, row_starts, own_start, pair_shifts, pair_starts, *refs),
        out_shape=(jax.ShapeDtypeStruct(shape, own.dtype),
                   jax.ShapeDtypeStruct(pair_shape, own.dtype)),
        in_specs=[any_spec] * (n + 1 + m),
        out_specs=(any_spec, any_spec),
        scratch_shapes=[
            pltpu.SemaphoreType.DMA((n,)),
            pltpu.SemaphoreType.DMA((n,)),
            pltpu.SemaphoreType.DMA((m,)),
            pltpu.SemaphoreType.DMA((m,)),
            pltpu.SemaphoreType.DMA((m,)),
            pltpu.SemaphoreType.DMA((m,)),
            pltpu.SemaphoreType.DMA((1,)),
        ],
        compiler_params=pltpu.CompilerParams(collective_id=0, has_side_effects=True),
        name="row_exchange",
    )(*sends, own, *pair_sends)


def _layer_gather_kernel(sizes, *refs):
    src_ref, out_ref, send_sem, recv_sem, local_sem = refs
    count = sizes[0]
    me = lax.axis_index("layer")
    width = src_ref.shape[1]
    core_shift = 1 - 2 * lax.rem(me, 2)
    far = count // 2
    _greet(sizes, [(far, 0), (core_shift, 0)])

    def cols(layer):
        return out_ref.at[:, pl.ds(pl.multiple_of(layer * width, width), width)]

    mine = cols(me)
    to_far = pltpu.make_async_remote_copy(
        src_ref=src_ref, dst_ref=mine, send_sem=send_sem.at[0], recv_sem=recv_sem.at[0],
        device_id=_peer(sizes, far, 0), device_id_type=pl.DeviceIdType.MESH,
    )
    to_core = pltpu.make_async_remote_copy(
        src_ref=src_ref, dst_ref=mine, send_sem=send_sem.at[1], recv_sem=recv_sem.at[1],
        device_id=_peer(sizes, core_shift, 0), device_id_type=pl.DeviceIdType.MESH,
    )
    to_far.start()
    to_core.start()
    local = pltpu.make_async_copy(src_ref, mine, local_sem.at[0])
    local.start()
    far_layer = lax.rem(me + far, count)
    to_far.wait_recv()
    forward = pltpu.make_async_remote_copy(
        src_ref=cols(far_layer), dst_ref=cols(far_layer), send_sem=send_sem.at[2],
        recv_sem=recv_sem.at[2], device_id=_peer(sizes, core_shift, 0),
        device_id_type=pl.DeviceIdType.MESH,
    )
    forward.start()
    local.wait()
    to_far.wait_send()
    to_core.wait()
    forward.wait()


def layer_gather(sizes, slab, collective_id):
    count = sizes[0]
    any_spec = pl.BlockSpec(memory_space=pl.ANY)
    return pl.pallas_call(
        lambda *refs: _layer_gather_kernel(sizes, *refs),
        out_shape=jax.ShapeDtypeStruct((slab.shape[0], slab.shape[1] * count), slab.dtype),
        in_specs=[any_spec],
        out_specs=any_spec,
        scratch_shapes=[
            pltpu.SemaphoreType.DMA((3,)),
            pltpu.SemaphoreType.DMA((3,)),
            pltpu.SemaphoreType.DMA((1,)),
        ],
        compiler_params=pltpu.CompilerParams(collective_id=collective_id, has_side_effects=True),
        name="layer_gather",
    )(slab)


def shifted(value, axis, steps):
    count = lax.axis_size(axis)
    pairs = [(source, (source + steps) % count) for source in range(count)]
    return lax.ppermute(value, axis, pairs)


def skew_rows(band, shift_total):
    n, bs, width = band.shape
    pieces = [
        jnp.pad(band[i], ((0, 0), (i * bs, (shift_total - i) * bs))) for i in range(n)
    ]
    return jnp.stack(pieces, axis=0)


def body(density, pattern):
    rows_dev, slab_cols = density.shape
    block_rows, slab_offsets = pattern.shape
    bs = rows_dev // block_rows
    layers = lax.axis_size("layer")
    offsets = slab_offsets * layers
    half = offsets // 2
    layer_id = lax.axis_index("layer")
    sizes = tuple(lax.axis_size(name) for name in MESH_AXES)

    keep = pattern.astype(jnp.bfloat16)[:, None, :, None]
    masked = (density.reshape(block_rows, bs, slab_offsets, bs) * keep).reshape(rows_dev, slab_cols)
    own_band = layer_gather(sizes, masked, 1)

    total_rows = block_rows + offsets - 1
    width = slab_offsets + block_rows - 1
    pad_l = total_rows - 1 - half
    pad_r = max(0, slab_offsets * (layers - 1) + half + width - offsets)
    band_pad = jnp.pad(
        own_band.reshape(block_rows, bs, offsets * bs), ((0, 0), (0, 0), (pad_l * bs, pad_r * bs))
    )
    base = layer_id * slab_offsets

    far = layers // 2

    def windows(shift, first, last, layer_shift=0):
        rows = []
        target = lax.rem(layer_id + layer_shift, layers) * slab_offsets
        for j in range(first, last):
            start = (target + block_rows * shift - j + pad_l) * bs
            rows.append(lax.dynamic_slice_in_dim(band_pad[j], start, width * bs, axis=1))
        return jnp.stack(rows, axis=0)

    core = lax.rem(layer_id, 2)
    pair_width = width + slab_offsets
    half_rows = block_rows // 2

    def pair_windows(shift):
        target = (lax.rem(layer_id + far, layers) - core) * slab_offsets
        rows = []
        for jj in range(half_rows):
            j = core * half_rows + jj
            row = lax.dynamic_index_in_dim(band_pad, j, 0, keepdims=False)
            start = (target + block_rows * shift - j + pad_l) * bs
            rows.append(lax.dynamic_slice_in_dim(row, start, pair_width * bs, axis=1))
        return jnp.stack(rows, axis=0)

    below = half
    above = total_rows - half - block_rows
    steps, sends, row_starts = [], [], []
    pair_sends = []
    dist, need = 1, below
    while need > 0:
        take = min(block_rows, need)
        if dist == 1:
            lower_start = need - take
            pair_sends.append(pair_windows(dist))
        else:
            sends.append(windows(dist, block_rows - take, block_rows))
            steps.append((0, dist))
            row_starts.append(need - take)
        need -= take
        dist += 1
    dist, need = 1, above
    while need > 0:
        take = min(block_rows, need)
        if dist == 1:
            upper_start = below + block_rows
            pair_sends.append(pair_windows(-dist))
        else:
            sends.append(windows(-dist, 0, take))
            steps.append((0, -dist))
            row_starts.append(below + block_rows + (above - need))
        need -= take
        dist += 1
    right, pair_buf = row_exchange(
        sizes, steps, row_starts, below, total_rows, sends, windows(0, 0, block_rows),
        [(far, 1), (far, -1)], [0, block_rows], 2 * block_rows, pair_sends,
    )
    pair_part = lax.dynamic_slice_in_dim(pair_buf, core * slab_offsets * bs, width * bs, axis=2)
    right = lax.dynamic_update_slice_in_dim(right, pair_part[:block_rows], lower_start, axis=0)
    right = lax.dynamic_update_slice_in_dim(right, pair_part[block_rows:], upper_start, axis=0)
    right = right.reshape(total_rows * bs, width * bs)

    pattern_f = pattern.astype(jnp.float32)[:, None, :, None]

    def product(left_band):
        left = skew_rows(left_band.reshape(block_rows, bs, offsets * bs), block_rows - 1)
        left = left.reshape(rows_dev, total_rows * bs)
        dense = jnp.dot(left, right, preferred_element_type=jnp.float32)
        dense = dense.reshape(block_rows, bs, width * bs)
        out = jnp.stack(
            [dense[i, :, i * bs: (i + slab_offsets) * bs] for i in range(block_rows)], axis=0
        )
        return out.reshape(block_rows, bs, slab_offsets, bs) * pattern_f

    square = product(own_band).astype(jnp.bfloat16)
    square_full = layer_gather(sizes, square.reshape(rows_dev, slab_cols), 1)
    cubic = product(square_full)
    purified = 3.0 * square.astype(jnp.float32) - 2.0 * cubic
    return purified.reshape(rows_dev, slab_cols)


def solution(mesh):
    placed = (P("row", "layer"), P("row", "layer"))
    return jax.shard_map(
        body, mesh=mesh, in_specs=placed, out_specs=P("row", "layer"), check_vma=False
    )
```

```python
import jax
import jax.numpy as jnp
from jax import lax
from jax.sharding import PartitionSpec as P
from jax.experimental import pallas as pl
from jax.experimental.pallas import tpu as pltpu

MESH_AXES = ("layer", "row")


def _peer(sizes, layer_shift, row_shift):
    layer = lax.axis_index("layer")
    row = lax.axis_index("row")
    return (
        lax.rem(layer + layer_shift + sizes[0], sizes[0]),
        lax.rem(row + row_shift + sizes[1], sizes[1]),
    )


def _greet(sizes, shifts):
    barrier = pltpu.get_barrier_semaphore()
    for layer_shift, row_shift in shifts:
        pl.semaphore_signal(barrier, inc=1, device_id=_peer(sizes, layer_shift, row_shift),
                            device_id_type=pl.DeviceIdType.MESH)
    pl.semaphore_wait(barrier, len(shifts))


def _row_exchange_kernel(sizes, shifts, row_starts, own_start, pair_shifts, pair_starts, *refs):
    n = len(shifts)
    m = len(pair_shifts)
    srcs = refs[:n]
    own_ref = refs[n]
    pair_srcs = refs[n + 1:n + 1 + m]
    out_ref, pair_ref = refs[n + 1 + m:n + 3 + m]
    send_sem, recv_sem, pair_send, pair_recv, fwd_send, fwd_recv, local_sem = refs[n + 3 + m:]
    me = lax.axis_index("layer")
    core = lax.rem(me, 2)
    core_shift = 1 - 2 * core
    _greet(sizes, list(shifts) + list(pair_shifts) + [(core_shift, 0)])
    copies = []
    for k, (layer_shift, row_shift) in enumerate(shifts):
        rows = srcs[k].shape[0]
        copy = pltpu.make_async_remote_copy(
            src_ref=srcs[k],
            dst_ref=out_ref.at[pl.ds(row_starts[k], rows)],
            send_sem=send_sem.at[k],
            recv_sem=recv_sem.at[k],
            device_id=_peer(sizes, layer_shift, row_shift),
            device_id_type=pl.DeviceIdType.MESH,
        )
        copy.start()
        copies.append(copy)
    pair_copies = []
    for k, (layer_shift, row_shift) in enumerate(pair_shifts):
        rows = pair_srcs[k].shape[0]
        copy = pltpu.make_async_remote_copy(
            src_ref=pair_srcs[k],
            dst_ref=pair_ref.at[pl.ds(pair_starts[k] + core * rows, rows)],
            send_sem=pair_send.at[k],
            recv_sem=pair_recv.at[k],
            device_id=_peer(sizes, layer_shift, row_shift),
            device_id_type=pl.DeviceIdType.MESH,
        )
        copy.start()
        pair_copies.append(copy)
    local = pltpu.make_async_copy(
        own_ref, out_ref.at[pl.ds(own_start, own_ref.shape[0])], local_sem.at[0]
    )
    local.start()
    forwards = []
    for k in range(m):
        rows = pair_srcs[k].shape[0]
        pair_copies[k].wait_recv()
        held = pair_ref.at[pl.ds(pair_starts[k] + core * rows, rows)]
        forward = pltpu.make_async_remote_copy(
            src_ref=held,
            dst_ref=held,
            send_sem=fwd_send.at[k],
            recv_sem=fwd_recv.at[k],
            device_id=_peer(sizes, core_shift, 0),
            device_id_type=pl.DeviceIdType.MESH,
        )
        forward.start()
        forwards.append(forward)
    local.wait()
    for copy in copies:
        copy.wait()
    for k in range(m):
        pair_copies[k].wait_send()
        forwards[k].wait()


def row_exchange(sizes, shifts, row_starts, own_start, total_rows, sends, own,
                 pair_shifts, pair_starts, pair_rows, pair_sends):
    n = len(shifts)
    m = len(pair_shifts)
    shape = (total_rows,) + own.shape[1:]
    pair_shape = (pair_rows,) + pair_sends[0].shape[1:]
    any_spec = pl.BlockSpec(memory_space=pl.ANY)
    return pl.pallas_call(
        lambda *refs: _row_exchange_kernel(
            sizes, shifts, row_starts, own_start, pair_shifts, pair_starts, *refs),
        out_shape=(jax.ShapeDtypeStruct(shape, own.dtype),
                   jax.ShapeDtypeStruct(pair_shape, own.dtype)),
        in_specs=[any_spec] * (n + 1 + m),
        out_specs=(any_spec, any_spec),
        scratch_shapes=[
            pltpu.SemaphoreType.DMA((n,)),
            pltpu.SemaphoreType.DMA((n,)),
            pltpu.SemaphoreType.DMA((m,)),
            pltpu.SemaphoreType.DMA((m,)),
            pltpu.SemaphoreType.DMA((m,)),
            pltpu.SemaphoreType.DMA((m,)),
            pltpu.SemaphoreType.DMA((1,)),
        ],
        compiler_params=pltpu.CompilerParams(collective_id=0, has_side_effects=True),
        name="row_exchange",
    )(*sends, own, *pair_sends)


def _layer_gather_kernel(sizes, *refs):
    src_ref, out_ref, send_sem, recv_sem, local_sem = refs
    count = sizes[0]
    me = lax.axis_index("layer")
    width = src_ref.shape[1]
    core_shift = 1 - 2 * lax.rem(me, 2)
    far = count // 2
    _greet(sizes, [(far, 0), (core_shift, 0)])

    def cols(layer):
        return out_ref.at[:, pl.ds(pl.multiple_of(layer * width, width), width)]

    mine = cols(me)
    to_far = pltpu.make_async_remote_copy(
        src_ref=src_ref, dst_ref=mine, send_sem=send_sem.at[0], recv_sem=recv_sem.at[0],
        device_id=_peer(sizes, far, 0), device_id_type=pl.DeviceIdType.MESH,
    )
    to_core = pltpu.make_async_remote_copy(
        src_ref=src_ref, dst_ref=mine, send_sem=send_sem.at[1], recv_sem=recv_sem.at[1],
        device_id=_peer(sizes, core_shift, 0), device_id_type=pl.DeviceIdType.MESH,
    )
    to_far.start()
    to_core.start()
    local = pltpu.make_async_copy(src_ref, mine, local_sem.at[0])
    local.start()
    far_layer = lax.rem(me + far, count)
    to_far.wait_recv()
    forward = pltpu.make_async_remote_copy(
        src_ref=cols(far_layer), dst_ref=cols(far_layer), send_sem=send_sem.at[2],
        recv_sem=recv_sem.at[2], device_id=_peer(sizes, core_shift, 0),
        device_id_type=pl.DeviceIdType.MESH,
    )
    forward.start()
    local.wait()
    to_far.wait_send()
    to_core.wait()
    forward.wait()


def layer_gather(sizes, slab, collective_id):
    count = sizes[0]
    any_spec = pl.BlockSpec(memory_space=pl.ANY)
    return pl.pallas_call(
        lambda *refs: _layer_gather_kernel(sizes, *refs),
        out_shape=jax.ShapeDtypeStruct((slab.shape[0], slab.shape[1] * count), slab.dtype),
        in_specs=[any_spec],
        out_specs=any_spec,
        scratch_shapes=[
            pltpu.SemaphoreType.DMA((3,)),
            pltpu.SemaphoreType.DMA((3,)),
            pltpu.SemaphoreType.DMA((1,)),
        ],
        compiler_params=pltpu.CompilerParams(collective_id=collective_id, has_side_effects=True),
        name="layer_gather",
    )(slab)


def shifted(value, axis, steps):
    count = lax.axis_size(axis)
    pairs = [(source, (source + steps) % count) for source in range(count)]
    return lax.ppermute(value, axis, pairs)


def skew_rows(band, shift_total):
    n, bs, width = band.shape
    pieces = [
        jnp.pad(band[i], ((0, 0), (i * bs, (shift_total - i) * bs))) for i in range(n)
    ]
    return jnp.stack(pieces, axis=0)


def body(density, pattern):
    rows_dev, slab_cols = density.shape
    block_rows, slab_offsets = pattern.shape
    bs = rows_dev // block_rows
    layers = lax.axis_size("layer")
    offsets = slab_offsets * layers
    half = offsets // 2
    layer_id = lax.axis_index("layer")
    sizes = tuple(lax.axis_size(name) for name in MESH_AXES)

    keep = pattern.astype(jnp.bfloat16)[:, None, :, None]
    masked = (density.reshape(block_rows, bs, slab_offsets, bs) * keep).reshape(rows_dev, slab_cols)
    own_band = layer_gather(sizes, masked, 1)

    total_rows = block_rows + offsets - 1
    width = slab_offsets + block_rows - 1
    pad_l = total_rows - 1 - half
    core = lax.rem(layer_id, 2)
    pair_width = width + slab_offsets
    half_rows = block_rows // 2
    far = layers // 2
    span = pad_l + 2 * block_rows + pair_width
    pad_r = max(0, slab_offsets * (layers - 1) + span - offsets - pad_l)
    band_pad = jnp.pad(
        own_band.reshape(block_rows, bs, offsets * bs), ((0, 0), (0, 0), (pad_l * bs, pad_r * bs))
    )

    def relative(target_layer):
        start = target_layer * slab_offsets * bs
        return lax.dynamic_slice_in_dim(band_pad, start, span * bs, axis=2)

    own_rel = relative(layer_id)
    pair_rel = relative(lax.rem(layer_id + far, layers) - core)

    def cut(rel, shift, first, last, w):
        rows = []
        for j in range(first, last):
            start = (block_rows * shift - j + pad_l) * bs
            rows.append(rel[j, :, start:start + w * bs])
        return jnp.stack(rows, axis=0)

    def windows(shift, first, last):
        return cut(own_rel, shift, first, last, width)

    def pair_windows(shift):
        both = cut(pair_rel, shift, 0, block_rows, pair_width)
        return lax.dynamic_slice_in_dim(both, core * half_rows, half_rows, axis=0)

    below = half
    above = total_rows - half - block_rows
    steps, sends, row_starts = [], [], []
    pair_sends = []
    dist, need = 1, below
    while need > 0:
        take = min(block_rows, need)
        if dist == 1:
            lower_start = need - take
            pair_sends.append(pair_windows(dist))
        else:
            sends.append(windows(dist, block_rows - take, block_rows))
            steps.append((0, dist))
            row_starts.append(need - take)
        need -= take
        dist += 1
    dist, need = 1, above
    while need > 0:
        take = min(block_rows, need)
        if dist == 1:
            upper_start = below + block_rows
            pair_sends.append(pair_windows(-dist))
        else:
            sends.append(windows(-dist, 0, take))
            steps.append((0, -dist))
            row_starts.append(below + block_rows + (above - need))
        need -= take
        dist += 1
    right, pair_buf = row_exchange(
        sizes, steps, row_starts, below, total_rows, sends, windows(0, 0, block_rows),
        [(far, 1), (far, -1)], [0, block_rows], 2 * block_rows, pair_sends,
    )
    pair_part = lax.dynamic_slice_in_dim(pair_buf, core * slab_offsets * bs, width * bs, axis=2)
    right = lax.dynamic_update_slice_in_dim(right, pair_part[:block_rows], lower_start, axis=0)
    right = lax.dynamic_update_slice_in_dim(right, pair_part[block_rows:], upper_start, axis=0)
    right = right.reshape(total_rows * bs, width * bs)

    pattern_f = pattern.astype(jnp.float32)[:, None, :, None]

    def product(left_band):
        left = skew_rows(left_band.reshape(block_rows, bs, offsets * bs), block_rows - 1)
        left = left.reshape(rows_dev, total_rows * bs)
        dense = jnp.dot(left, right, preferred_element_type=jnp.float32)
        dense = dense.reshape(block_rows, bs, width * bs)
        out = jnp.stack(
            [dense[i, :, i * bs: (i + slab_offsets) * bs] for i in range(block_rows)], axis=0
        )
        return out.reshape(block_rows, bs, slab_offsets, bs) * pattern_f

    square = product(own_band).astype(jnp.bfloat16)
    square_full = layer_gather(sizes, square.reshape(rows_dev, slab_cols), 1)
    cubic = product(square_full)
    purified = 3.0 * square.astype(jnp.float32) - 2.0 * cubic
    return purified.reshape(rows_dev, slab_cols)


def solution(mesh):
    placed = (P("row", "layer"), P("row", "layer"))
    return jax.shard_map(
        body, mesh=mesh, in_specs=placed, out_specs=P("row", "layer"), check_vma=False
    )
```

```python
import jax
import jax.numpy as jnp
from jax import lax
from jax.sharding import PartitionSpec as P
from jax.experimental import pallas as pl
from jax.experimental.pallas import tpu as pltpu

MESH_AXES = ("layer", "row")


def _peer(sizes, layer_shift, row_shift):
    layer = lax.axis_index("layer")
    row = lax.axis_index("row")
    return (
        lax.rem(layer + layer_shift + sizes[0], sizes[0]),
        lax.rem(row + row_shift + sizes[1], sizes[1]),
    )


def _greet(sizes, shifts):
    barrier = pltpu.get_barrier_semaphore()
    for layer_shift, row_shift in shifts:
        pl.semaphore_signal(barrier, inc=1, device_id=_peer(sizes, layer_shift, row_shift),
                            device_id_type=pl.DeviceIdType.MESH)
    pl.semaphore_wait(barrier, len(shifts))


def _row_exchange_kernel(sizes, plan, *refs):
    (slab_offsets, block_rows, pad_l, width, pair_width, far, own_start,
     steps, pair_steps) = plan
    band_ref, out_ref, pair_ref = refs[:3]
    send_sem, recv_sem, pair_send, pair_recv, fwd_send, fwd_recv, local_sem = refs[3:]
    me = lax.axis_index("layer")
    core = lax.rem(me, 2)
    core_shift = 1 - 2 * core
    half_rows = block_rows // 2
    shifts = [(0, shift) for shift, _, _, _ in steps]
    shifts += [(far, shift) for shift, _ in pair_steps]
    _greet(sizes, shifts + [(core_shift, 0)])
    mesh = pl.DeviceIdType.MESH

    def row_copy(j, start, count, dst, send, recv, target):
        return pltpu.make_async_remote_copy(
            src_ref=band_ref.at[j, pl.ds(start, count)], dst_ref=dst,
            send_sem=send, recv_sem=recv, device_id=target, device_id_type=mesh,
        )

    def group(dst_rows, count, send, recv, target):
        return pltpu.make_async_remote_copy(
            src_ref=band_ref.at[pl.ds(0, dst_rows.shape[0]), pl.ds(0, count)], dst_ref=dst_rows,
            send_sem=send, recv_sem=recv, device_id=target, device_id_type=mesh,
        )

    waits = []
    for k, (shift, first, last, row_start) in enumerate(steps):
        target = _peer(sizes, 0, shift)
        for j in range(first, last):
            start = me * slab_offsets + block_rows * shift - j + pad_l
            row_copy(j, start, width, out_ref.at[row_start + j - first],
                     send_sem.at[k], recv_sem.at[k], target).start()
        waits.append(group(out_ref.at[pl.ds(row_start, last - first)], width,
                           send_sem.at[k], recv_sem.at[k], target))
    pair_groups = []
    pair_base = (lax.rem(me + far, sizes[0]) - core) * slab_offsets
    for k, (shift, pair_start) in enumerate(pair_steps):
        target = _peer(sizes, far, shift)
        for jj in range(half_rows):
            j = core * half_rows + jj
            start = pair_base + block_rows * shift - j + pad_l
            row_copy(j, start, pair_width, pair_ref.at[pair_start + j],
                     pair_send.at[k], pair_recv.at[k], target).start()
        held = pair_ref.at[pl.ds(pair_start + core * half_rows, half_rows)]
        pair_groups.append((held, group(held, pair_width, pair_send.at[k], pair_recv.at[k], target)))
    for j in range(block_rows):
        start = me * slab_offsets - j + pad_l
        pltpu.make_async_copy(band_ref.at[j, pl.ds(start, width)],
                              out_ref.at[own_start + j], local_sem.at[0]).start()
    forwards = []
    for k, (held, grp) in enumerate(pair_groups):
        grp.wait_recv()
        forward = pltpu.make_async_remote_copy(
            src_ref=held, dst_ref=held, send_sem=fwd_send.at[k], recv_sem=fwd_recv.at[k],
            device_id=_peer(sizes, core_shift, 0), device_id_type=mesh,
        )
        forward.start()
        forwards.append(forward)
    pltpu.make_async_copy(band_ref.at[pl.ds(0, block_rows), pl.ds(0, width)],
                          out_ref.at[pl.ds(own_start, block_rows)], local_sem.at[0]).wait()
    for grp in waits:
        grp.wait()
    for k, (held, grp) in enumerate(pair_groups):
        grp.wait_send()
        forwards[k].wait()


def row_exchange(sizes, plan, total_rows, pair_rows, band):
    (slab_offsets, block_rows, pad_l, width, pair_width, far, own_start,
     steps, pair_steps) = plan
    blk = band.shape[2:]
    any_spec = pl.BlockSpec(memory_space=pl.ANY)
    n, m = len(steps), len(pair_steps)
    return pl.pallas_call(
        lambda *refs: _row_exchange_kernel(sizes, plan, *refs),
        out_shape=(jax.ShapeDtypeStruct((total_rows, width) + blk, band.dtype),
                   jax.ShapeDtypeStruct((pair_rows, pair_width) + blk, band.dtype)),
        in_specs=[any_spec],
        out_specs=(any_spec, any_spec),
        scratch_shapes=[
            pltpu.SemaphoreType.DMA((n,)),
            pltpu.SemaphoreType.DMA((n,)),
            pltpu.SemaphoreType.DMA((m,)),
            pltpu.SemaphoreType.DMA((m,)),
            pltpu.SemaphoreType.DMA((m,)),
            pltpu.SemaphoreType.DMA((m,)),
            pltpu.SemaphoreType.DMA((1,)),
        ],
        compiler_params=pltpu.CompilerParams(collective_id=0, has_side_effects=True),
        name="row_exchange",
    )(band)


def _layer_gather_kernel(sizes, *refs):
    src_ref, out_ref, send_sem, recv_sem, local_sem = refs
    count = sizes[0]
    me = lax.axis_index("layer")
    width = src_ref.shape[1]
    core_shift = 1 - 2 * lax.rem(me, 2)
    far = count // 2
    _greet(sizes, [(far, 0), (core_shift, 0)])

    def cols(layer):
        return out_ref.at[:, pl.ds(pl.multiple_of(layer * width, width), width)]

    mine = cols(me)
    to_far = pltpu.make_async_remote_copy(
        src_ref=src_ref, dst_ref=mine, send_sem=send_sem.at[0], recv_sem=recv_sem.at[0],
        device_id=_peer(sizes, far, 0), device_id_type=pl.DeviceIdType.MESH,
    )
    to_core = pltpu.make_async_remote_copy(
        src_ref=src_ref, dst_ref=mine, send_sem=send_sem.at[1], recv_sem=recv_sem.at[1],
        device_id=_peer(sizes, core_shift, 0), device_id_type=pl.DeviceIdType.MESH,
    )
    to_far.start()
    to_core.start()
    local = pltpu.make_async_copy(src_ref, mine, local_sem.at[0])
    local.start()
    far_layer = lax.rem(me + far, count)
    to_far.wait_recv()
    forward = pltpu.make_async_remote_copy(
        src_ref=cols(far_layer), dst_ref=cols(far_layer), send_sem=send_sem.at[2],
        recv_sem=recv_sem.at[2], device_id=_peer(sizes, core_shift, 0),
        device_id_type=pl.DeviceIdType.MESH,
    )
    forward.start()
    local.wait()
    to_far.wait_send()
    to_core.wait()
    forward.wait()


def layer_gather(sizes, slab, collective_id):
    count = sizes[0]
    any_spec = pl.BlockSpec(memory_space=pl.ANY)
    return pl.pallas_call(
        lambda *refs: _layer_gather_kernel(sizes, *refs),
        out_shape=jax.ShapeDtypeStruct((slab.shape[0], slab.shape[1] * count), slab.dtype),
        in_specs=[any_spec],
        out_specs=any_spec,
        scratch_shapes=[
            pltpu.SemaphoreType.DMA((3,)),
            pltpu.SemaphoreType.DMA((3,)),
            pltpu.SemaphoreType.DMA((1,)),
        ],
        compiler_params=pltpu.CompilerParams(collective_id=collective_id, has_side_effects=True),
        name="layer_gather",
    )(slab)


def shifted(value, axis, steps):
    count = lax.axis_size(axis)
    pairs = [(source, (source + steps) % count) for source in range(count)]
    return lax.ppermute(value, axis, pairs)


def skew_rows(band, shift_total):
    n, bs, width = band.shape
    pieces = [
        jnp.pad(band[i], ((0, 0), (i * bs, (shift_total - i) * bs))) for i in range(n)
    ]
    return jnp.stack(pieces, axis=0)


def body(density, pattern):
    rows_dev, slab_cols = density.shape
    block_rows, slab_offsets = pattern.shape
    bs = rows_dev // block_rows
    layers = lax.axis_size("layer")
    offsets = slab_offsets * layers
    half = offsets // 2
    layer_id = lax.axis_index("layer")
    sizes = tuple(lax.axis_size(name) for name in MESH_AXES)

    keep = pattern.astype(jnp.bfloat16)[:, None, :, None]
    masked = (density.reshape(block_rows, bs, slab_offsets, bs) * keep).reshape(rows_dev, slab_cols)
    own_band = layer_gather(sizes, masked, 1)

    total_rows = block_rows + offsets - 1
    width = slab_offsets + block_rows - 1
    pad_l = total_rows - 1 - half
    far = layers // 2
    pair_width = width + slab_offsets
    span = pad_l + 2 * block_rows + pair_width
    pad_r = max(0, slab_offsets * (layers - 1) + span - offsets - pad_l)
    band = own_band.reshape(block_rows, bs, offsets, bs).transpose(0, 2, 1, 3)
    band = jnp.pad(band, ((0, 0), (pad_l, pad_r), (0, 0), (0, 0)))
    core = lax.rem(layer_id, 2)

    below = half
    above = total_rows - half - block_rows
    steps = []
    dist, need = 1, below
    while need > 0:
        take = min(block_rows, need)
        if dist == 1:
            lower_start = need - take
        else:
            steps.append((dist, block_rows - take, block_rows, need - take))
        need -= take
        dist += 1
    dist, need = 1, above
    while need > 0:
        take = min(block_rows, need)
        if dist == 1:
            upper_start = below + block_rows
        else:
            steps.append((-dist, 0, take, below + block_rows + (above - need)))
        need -= take
        dist += 1
    pair_steps = ((1, 0), (-1, block_rows))
    plan = (slab_offsets, block_rows, pad_l, width, pair_width, far, below,
            tuple(steps), pair_steps)
    right, pair_buf = row_exchange(sizes, plan, total_rows, 2 * block_rows, band)
    pair_part = lax.dynamic_slice_in_dim(pair_buf, core * slab_offsets, width, axis=1)
    right = jnp.concatenate([
        right[:lower_start], pair_part[:block_rows], right[below:below + block_rows],
        pair_part[block_rows:], right[upper_start + block_rows:],
    ], axis=0)
    right = right.transpose(0, 2, 1, 3).reshape(total_rows * bs, width * bs)

    pattern_f = pattern.astype(jnp.float32)[:, None, :, None]

    def product(left_band):
        left = skew_rows(left_band.reshape(block_rows, bs, offsets * bs), block_rows - 1)
        left = left.reshape(rows_dev, total_rows * bs)
        dense = jnp.dot(left, right, preferred_element_type=jnp.float32)
        dense = dense.reshape(block_rows, bs, width * bs)
        out = jnp.stack(
            [dense[i, :, i * bs: (i + slab_offsets) * bs] for i in range(block_rows)], axis=0
        )
        return out.reshape(block_rows, bs, slab_offsets, bs) * pattern_f

    square = product(own_band).astype(jnp.bfloat16)
    square_full = layer_gather(sizes, square.reshape(rows_dev, slab_cols), 1)
    cubic = product(square_full)
    purified = 3.0 * square.astype(jnp.float32) - 2.0 * cubic
    return purified.reshape(rows_dev, slab_cols)


def solution(mesh):
    placed = (P("row", "layer"), P("row", "layer"))
    return jax.shard_map(
        body, mesh=mesh, in_specs=placed, out_specs=P("row", "layer"), check_vma=False
    )
```

```python
import jax
import jax.numpy as jnp
from jax import lax
from jax.sharding import PartitionSpec as P
from jax.experimental import pallas as pl
from jax.experimental.pallas import tpu as pltpu

MESH_AXES = ("layer", "row")


def _peer(sizes, layer_shift, row_shift):
    layer = lax.axis_index("layer")
    row = lax.axis_index("row")
    return (
        lax.rem(layer + layer_shift + sizes[0], sizes[0]),
        lax.rem(row + row_shift + sizes[1], sizes[1]),
    )


def _greet(sizes, shifts):
    barrier = pltpu.get_barrier_semaphore()
    for layer_shift, row_shift in shifts:
        pl.semaphore_signal(barrier, inc=1, device_id=_peer(sizes, layer_shift, row_shift),
                            device_id_type=pl.DeviceIdType.MESH)
    pl.semaphore_wait(barrier, len(shifts))


def _row_exchange_kernel(sizes, plan, *refs):
    (slab_offsets, block_rows, pad_l, width, pair_width, far, own_start,
     steps, pair_steps) = plan
    band_ref, out_ref, pair_ref = refs[:3]
    send_sem, recv_sem, pair_send, pair_recv, fwd_send, fwd_recv, local_sem = refs[3:]
    me = lax.axis_index("layer")
    core = lax.rem(me, 2)
    core_shift = 1 - 2 * core
    half_rows = block_rows // 2
    shifts = [(0, shift) for shift, _, _, _ in steps]
    shifts += [(far, shift) for shift, _ in pair_steps]
    _greet(sizes, shifts + [(core_shift, 0)])
    mesh = pl.DeviceIdType.MESH

    bs = band_ref.shape[2]

    def window(j, start, count):
        odd = lax.rem(start, 2)
        first = pl.multiple_of((start - odd) * bs, 2 * bs)
        return band_ref.at[odd, j, :, pl.ds(first, count * bs)]

    def row_copy(j, start, count, dst, send, recv, target):
        return pltpu.make_async_remote_copy(
            src_ref=window(j, start, count), dst_ref=dst,
            send_sem=send, recv_sem=recv, device_id=target, device_id_type=mesh,
        )

    def group(dst_rows, count, send, recv, target):
        return pltpu.make_async_remote_copy(
            src_ref=band_ref.at[0, pl.ds(0, dst_rows.shape[0]), :, pl.ds(0, count * bs)],
            dst_ref=dst_rows, send_sem=send, recv_sem=recv, device_id=target,
            device_id_type=mesh,
        )

    waits = []
    for k, (shift, first, last, row_start) in enumerate(steps):
        target = _peer(sizes, 0, shift)
        for j in range(first, last):
            start = me * slab_offsets + block_rows * shift - j + pad_l
            row_copy(j, start, width, out_ref.at[row_start + j - first],
                     send_sem.at[k], recv_sem.at[k], target).start()
        waits.append(group(out_ref.at[pl.ds(row_start, last - first)], width,
                           send_sem.at[k], recv_sem.at[k], target))
    pair_groups = []
    pair_base = (lax.rem(me + far, sizes[0]) - core) * slab_offsets
    for k, (shift, pair_start) in enumerate(pair_steps):
        target = _peer(sizes, far, shift)
        for jj in range(half_rows):
            j = core * half_rows + jj
            start = pair_base + block_rows * shift - j + pad_l
            row_copy(j, start, pair_width, pair_ref.at[pair_start + j],
                     pair_send.at[k], pair_recv.at[k], target).start()
        held = pair_ref.at[pl.ds(pair_start + core * half_rows, half_rows)]
        pair_groups.append((held, group(held, pair_width, pair_send.at[k], pair_recv.at[k], target)))
    for j in range(block_rows):
        start = me * slab_offsets - j + pad_l
        pltpu.make_async_copy(window(j, start, width),
                              out_ref.at[own_start + j], local_sem.at[0]).start()
    forwards = []
    for k, (held, grp) in enumerate(pair_groups):
        grp.wait_recv()
        forward = pltpu.make_async_remote_copy(
            src_ref=held, dst_ref=held, send_sem=fwd_send.at[k], recv_sem=fwd_recv.at[k],
            device_id=_peer(sizes, core_shift, 0), device_id_type=mesh,
        )
        forward.start()
        forwards.append(forward)
    pltpu.make_async_copy(band_ref.at[0, pl.ds(0, block_rows), :, pl.ds(0, width * bs)],
                          out_ref.at[pl.ds(own_start, block_rows)], local_sem.at[0]).wait()
    for grp in waits:
        grp.wait()
    for k, (held, grp) in enumerate(pair_groups):
        grp.wait_send()
        forwards[k].wait()


def row_exchange(sizes, plan, total_rows, pair_rows, band):
    (slab_offsets, block_rows, pad_l, width, pair_width, far, own_start,
     steps, pair_steps) = plan
    bs = band.shape[2]
    any_spec = pl.BlockSpec(memory_space=pl.ANY)
    n, m = len(steps), len(pair_steps)
    return pl.pallas_call(
        lambda *refs: _row_exchange_kernel(sizes, plan, *refs),
        out_shape=(jax.ShapeDtypeStruct((total_rows, bs, width * bs), band.dtype),
                   jax.ShapeDtypeStruct((pair_rows, bs, pair_width * bs), band.dtype)),
        in_specs=[any_spec],
        out_specs=(any_spec, any_spec),
        scratch_shapes=[
            pltpu.SemaphoreType.DMA((n,)),
            pltpu.SemaphoreType.DMA((n,)),
            pltpu.SemaphoreType.DMA((m,)),
            pltpu.SemaphoreType.DMA((m,)),
            pltpu.SemaphoreType.DMA((m,)),
            pltpu.SemaphoreType.DMA((m,)),
            pltpu.SemaphoreType.DMA((1,)),
        ],
        compiler_params=pltpu.CompilerParams(collective_id=0, has_side_effects=True),
        name="row_exchange",
    )(band)


def _layer_gather_kernel(sizes, *refs):
    src_ref, out_ref, send_sem, recv_sem, local_sem = refs
    count = sizes[0]
    me = lax.axis_index("layer")
    width = src_ref.shape[1]
    core_shift = 1 - 2 * lax.rem(me, 2)
    far = count // 2
    _greet(sizes, [(far, 0), (core_shift, 0)])

    def cols(layer):
        return out_ref.at[:, pl.ds(pl.multiple_of(layer * width, width), width)]

    mine = cols(me)
    to_far = pltpu.make_async_remote_copy(
        src_ref=src_ref, dst_ref=mine, send_sem=send_sem.at[0], recv_sem=recv_sem.at[0],
        device_id=_peer(sizes, far, 0), device_id_type=pl.DeviceIdType.MESH,
    )
    to_core = pltpu.make_async_remote_copy(
        src_ref=src_ref, dst_ref=mine, send_sem=send_sem.at[1], recv_sem=recv_sem.at[1],
        device_id=_peer(sizes, core_shift, 0), device_id_type=pl.DeviceIdType.MESH,
    )
    to_far.start()
    to_core.start()
    local = pltpu.make_async_copy(src_ref, mine, local_sem.at[0])
    local.start()
    far_layer = lax.rem(me + far, count)
    to_far.wait_recv()
    forward = pltpu.make_async_remote_copy(
        src_ref=cols(far_layer), dst_ref=cols(far_layer), send_sem=send_sem.at[2],
        recv_sem=recv_sem.at[2], device_id=_peer(sizes, core_shift, 0),
        device_id_type=pl.DeviceIdType.MESH,
    )
    forward.start()
    local.wait()
    to_far.wait_send()
    to_core.wait()
    forward.wait()


def layer_gather(sizes, slab, collective_id):
    count = sizes[0]
    any_spec = pl.BlockSpec(memory_space=pl.ANY)
    return pl.pallas_call(
        lambda *refs: _layer_gather_kernel(sizes, *refs),
        out_shape=jax.ShapeDtypeStruct((slab.shape[0], slab.shape[1] * count), slab.dtype),
        in_specs=[any_spec],
        out_specs=any_spec,
        scratch_shapes=[
            pltpu.SemaphoreType.DMA((3,)),
            pltpu.SemaphoreType.DMA((3,)),
            pltpu.SemaphoreType.DMA((1,)),
        ],
        compiler_params=pltpu.CompilerParams(collective_id=collective_id, has_side_effects=True),
        name="layer_gather",
    )(slab)


def shifted(value, axis, steps):
    count = lax.axis_size(axis)
    pairs = [(source, (source + steps) % count) for source in range(count)]
    return lax.ppermute(value, axis, pairs)


def skew_rows(band, shift_total):
    n, bs, width = band.shape
    pieces = [
        jnp.pad(band[i], ((0, 0), (i * bs, (shift_total - i) * bs))) for i in range(n)
    ]
    return jnp.stack(pieces, axis=0)


def body(density, pattern):
    rows_dev, slab_cols = density.shape
    block_rows, slab_offsets = pattern.shape
    bs = rows_dev // block_rows
    layers = lax.axis_size("layer")
    offsets = slab_offsets * layers
    half = offsets // 2
    layer_id = lax.axis_index("layer")
    sizes = tuple(lax.axis_size(name) for name in MESH_AXES)

    keep = pattern.astype(jnp.bfloat16)[:, None, :, None]
    masked = (density.reshape(block_rows, bs, slab_offsets, bs) * keep).reshape(rows_dev, slab_cols)
    own_band = layer_gather(sizes, masked, 1)

    total_rows = block_rows + offsets - 1
    width = slab_offsets + block_rows - 1
    pad_l = total_rows - 1 - half
    far = layers // 2
    width = width + width % 2
    pair_width = width + slab_offsets
    span = pad_l + 2 * block_rows + pair_width + 2
    total_blocks = slab_offsets * (layers - 1) + span
    total_blocks += total_blocks % 2
    pad_r = total_blocks - offsets - pad_l
    band = jnp.pad(own_band.reshape(block_rows, bs, offsets * bs),
                   ((0, 0), (0, 0), (pad_l * bs, pad_r * bs)))
    moved = jnp.pad(band[:, :, bs:], ((0, 0), (0, 0), (0, bs)))
    band = jnp.stack([band, moved], axis=0)
    core = lax.rem(layer_id, 2)

    below = half
    above = total_rows - half - block_rows
    steps = []
    dist, need = 1, below
    while need > 0:
        take = min(block_rows, need)
        if dist == 1:
            lower_start = need - take
        else:
            steps.append((dist, block_rows - take, block_rows, need - take))
        need -= take
        dist += 1
    dist, need = 1, above
    while need > 0:
        take = min(block_rows, need)
        if dist == 1:
            upper_start = below + block_rows
        else:
            steps.append((-dist, 0, take, below + block_rows + (above - need)))
        need -= take
        dist += 1
    pair_steps = ((1, 0), (-1, block_rows))
    plan = (slab_offsets, block_rows, pad_l, width, pair_width, far, below,
            tuple(steps), pair_steps)
    right, pair_buf = row_exchange(sizes, plan, total_rows, 2 * block_rows, band)
    pair_part = lax.dynamic_slice_in_dim(pair_buf, core * slab_offsets * bs, width * bs, axis=2)
    right = jnp.concatenate([
        right[:lower_start], pair_part[:block_rows], right[below:below + block_rows],
        pair_part[block_rows:], right[upper_start + block_rows:],
    ], axis=0)
    right = right.reshape(total_rows * bs, width * bs)

    pattern_f = pattern.astype(jnp.float32)[:, None, :, None]

    def product(left_band):
        left = skew_rows(left_band.reshape(block_rows, bs, offsets * bs), block_rows - 1)
        left = left.reshape(rows_dev, total_rows * bs)
        dense = jnp.dot(left, right, preferred_element_type=jnp.float32)
        dense = dense.reshape(block_rows, bs, width * bs)
        out = jnp.stack(
            [dense[i, :, i * bs: (i + slab_offsets) * bs] for i in range(block_rows)], axis=0
        )
        return out.reshape(block_rows, bs, slab_offsets, bs) * pattern_f

    square = product(own_band).astype(jnp.bfloat16)
    square_full = layer_gather(sizes, square.reshape(rows_dev, slab_cols), 1)
    cubic = product(square_full)
    purified = 3.0 * square.astype(jnp.float32) - 2.0 * cubic
    return purified.reshape(rows_dev, slab_cols)


def solution(mesh):
    placed = (P("row", "layer"), P("row", "layer"))
    return jax.shard_map(
        body, mesh=mesh, in_specs=placed, out_specs=P("row", "layer"), check_vma=False
    )
```

```python
import jax
import jax.numpy as jnp
from jax import lax
from jax.sharding import PartitionSpec as P
from jax.experimental import pallas as pl
from jax.experimental.pallas import tpu as pltpu

MESH_AXES = ("layer", "row")


def _peer(sizes, layer_shift, row_shift):
    layer = lax.axis_index("layer")
    row = lax.axis_index("row")
    return (
        lax.rem(layer + layer_shift + sizes[0], sizes[0]),
        lax.rem(row + row_shift + sizes[1], sizes[1]),
    )


def _greet(sizes, shifts):
    barrier = pltpu.get_barrier_semaphore()
    for layer_shift, row_shift in shifts:
        pl.semaphore_signal(barrier, inc=1, device_id=_peer(sizes, layer_shift, row_shift),
                            device_id_type=pl.DeviceIdType.MESH)
    pl.semaphore_wait(barrier, len(shifts))


def _row_exchange_kernel(sizes, plan, *refs):
    (slab_offsets, block_rows, pad_l, width, pair_width, far, own_start,
     steps, pair_steps, pair_dest) = plan
    band_ref, out_ref, pair_ref = refs[:3]
    send_sem, recv_sem, pair_send, pair_recv, fwd_send, fwd_recv, local_sem = refs[3:]
    me = lax.axis_index("layer")
    core = lax.rem(me, 2)
    core_shift = 1 - 2 * core
    half_rows = block_rows // 2
    shifts = [(0, shift) for shift, _, _, _ in steps]
    shifts += [(far, shift) for shift, _ in pair_steps]
    _greet(sizes, shifts + [(core_shift, 0)])
    mesh = pl.DeviceIdType.MESH

    bs = band_ref.shape[2]

    def window(j, start, count):
        odd = lax.rem(start, 2)
        first = pl.multiple_of((start - odd) * bs, 2 * bs)
        return band_ref.at[odd, j, :, pl.ds(first, count * bs)]

    def row_copy(j, start, count, dst, send, recv, target):
        return pltpu.make_async_remote_copy(
            src_ref=window(j, start, count), dst_ref=dst,
            send_sem=send, recv_sem=recv, device_id=target, device_id_type=mesh,
        )

    def group(dst_rows, count, send, recv, target):
        return pltpu.make_async_remote_copy(
            src_ref=band_ref.at[0, pl.ds(0, dst_rows.shape[0]), :, pl.ds(0, count * bs)],
            dst_ref=dst_rows, send_sem=send, recv_sem=recv, device_id=target,
            device_id_type=mesh,
        )

    waits = []
    for k, (shift, first, last, row_start) in enumerate(steps):
        target = _peer(sizes, 0, shift)
        for j in range(first, last):
            start = me * slab_offsets + block_rows * shift - j + pad_l
            row_copy(j, start, width, out_ref.at[row_start + j - first],
                     send_sem.at[k], recv_sem.at[k], target).start()
        waits.append(group(out_ref.at[pl.ds(row_start, last - first)], width,
                           send_sem.at[k], recv_sem.at[k], target))
    pair_groups = []
    pair_base = (lax.rem(me + far, sizes[0]) - core) * slab_offsets
    for k, (shift, pair_start) in enumerate(pair_steps):
        target = _peer(sizes, far, shift)
        for jj in range(half_rows):
            j = core * half_rows + jj
            start = pair_base + block_rows * shift - j + pad_l
            row_copy(j, start, pair_width, pair_ref.at[pair_start + j],
                     pair_send.at[k], pair_recv.at[k], target).start()
        held = pair_ref.at[pl.ds(pair_start + core * half_rows, half_rows)]
        pair_groups.append((held, group(held, pair_width, pair_send.at[k], pair_recv.at[k], target)))
    for j in range(block_rows):
        start = me * slab_offsets - j + pad_l
        pltpu.make_async_copy(window(j, start, width),
                              out_ref.at[own_start + j], local_sem.at[0]).start()
    forwards = []
    for k, (held, grp) in enumerate(pair_groups):
        grp.wait_recv()
        forward = pltpu.make_async_remote_copy(
            src_ref=held, dst_ref=held, send_sem=fwd_send.at[k], recv_sem=fwd_recv.at[k],
            device_id=_peer(sizes, core_shift, 0), device_id_type=mesh,
        )
        forward.start()
        forwards.append(forward)
    pltpu.make_async_copy(band_ref.at[0, pl.ds(0, block_rows), :, pl.ds(0, width * bs)],
                          out_ref.at[pl.ds(own_start, block_rows)], local_sem.at[0]).wait()
    for grp in waits:
        grp.wait()
    for k, (held, grp) in enumerate(pair_groups):
        grp.wait_send()
        forwards[k].wait()
    pair_rows = 2 * half_rows
    cols = pl.ds(pl.multiple_of(core * slab_offsets * bs, 2 * bs), width * bs)
    for k, (shift, pair_start) in enumerate(pair_steps):
        pltpu.make_async_copy(pair_ref.at[pl.ds(pair_start, pair_rows), :, cols],
                              out_ref.at[pl.ds(pair_dest[k], pair_rows)], local_sem.at[0]).start()
    for k in range(len(pair_steps)):
        pltpu.make_async_copy(pair_ref.at[pl.ds(0, pair_rows), :, cols],
                              out_ref.at[pl.ds(pair_dest[k], pair_rows)], local_sem.at[0]).wait()


def row_exchange(sizes, plan, total_rows, pair_rows, band):
    (slab_offsets, block_rows, pad_l, width, pair_width, far, own_start,
     steps, pair_steps, pair_dest) = plan
    bs = band.shape[2]
    any_spec = pl.BlockSpec(memory_space=pl.ANY)
    n, m = len(steps), len(pair_steps)
    return pl.pallas_call(
        lambda *refs: _row_exchange_kernel(sizes, plan, *refs),
        out_shape=(jax.ShapeDtypeStruct((total_rows, bs, width * bs), band.dtype),
                   jax.ShapeDtypeStruct((pair_rows, bs, pair_width * bs), band.dtype)),
        in_specs=[any_spec],
        out_specs=(any_spec, any_spec),
        scratch_shapes=[
            pltpu.SemaphoreType.DMA((n,)),
            pltpu.SemaphoreType.DMA((n,)),
            pltpu.SemaphoreType.DMA((m,)),
            pltpu.SemaphoreType.DMA((m,)),
            pltpu.SemaphoreType.DMA((m,)),
            pltpu.SemaphoreType.DMA((m,)),
            pltpu.SemaphoreType.DMA((1,)),
        ],
        compiler_params=pltpu.CompilerParams(collective_id=0, has_side_effects=True),
        name="row_exchange",
    )(band)


def _layer_gather_kernel(sizes, *refs):
    src_ref, out_ref, send_sem, recv_sem, local_sem = refs
    count = sizes[0]
    me = lax.axis_index("layer")
    width = src_ref.shape[1]
    core_shift = 1 - 2 * lax.rem(me, 2)
    far = count // 2
    _greet(sizes, [(far, 0), (core_shift, 0)])

    def cols(layer):
        return out_ref.at[:, pl.ds(pl.multiple_of(layer * width, width), width)]

    mine = cols(me)
    to_far = pltpu.make_async_remote_copy(
        src_ref=src_ref, dst_ref=mine, send_sem=send_sem.at[0], recv_sem=recv_sem.at[0],
        device_id=_peer(sizes, far, 0), device_id_type=pl.DeviceIdType.MESH,
    )
    to_core = pltpu.make_async_remote_copy(
        src_ref=src_ref, dst_ref=mine, send_sem=send_sem.at[1], recv_sem=recv_sem.at[1],
        device_id=_peer(sizes, core_shift, 0), device_id_type=pl.DeviceIdType.MESH,
    )
    to_far.start()
    to_core.start()
    local = pltpu.make_async_copy(src_ref, mine, local_sem.at[0])
    local.start()
    far_layer = lax.rem(me + far, count)
    to_far.wait_recv()
    forward = pltpu.make_async_remote_copy(
        src_ref=cols(far_layer), dst_ref=cols(far_layer), send_sem=send_sem.at[2],
        recv_sem=recv_sem.at[2], device_id=_peer(sizes, core_shift, 0),
        device_id_type=pl.DeviceIdType.MESH,
    )
    forward.start()
    local.wait()
    to_far.wait_send()
    to_core.wait()
    forward.wait()


def layer_gather(sizes, slab, collective_id):
    count = sizes[0]
    any_spec = pl.BlockSpec(memory_space=pl.ANY)
    return pl.pallas_call(
        lambda *refs: _layer_gather_kernel(sizes, *refs),
        out_shape=jax.ShapeDtypeStruct((slab.shape[0], slab.shape[1] * count), slab.dtype),
        in_specs=[any_spec],
        out_specs=any_spec,
        scratch_shapes=[
            pltpu.SemaphoreType.DMA((3,)),
            pltpu.SemaphoreType.DMA((3,)),
            pltpu.SemaphoreType.DMA((1,)),
        ],
        compiler_params=pltpu.CompilerParams(collective_id=collective_id, has_side_effects=True),
        name="layer_gather",
    )(slab)


def shifted(value, axis, steps):
    count = lax.axis_size(axis)
    pairs = [(source, (source + steps) % count) for source in range(count)]
    return lax.ppermute(value, axis, pairs)


def skew_rows(band, shift_total):
    n, bs, width = band.shape
    pieces = [
        jnp.pad(band[i], ((0, 0), (i * bs, (shift_total - i) * bs))) for i in range(n)
    ]
    return jnp.stack(pieces, axis=0)


def body(density, pattern):
    rows_dev, slab_cols = density.shape
    block_rows, slab_offsets = pattern.shape
    bs = rows_dev // block_rows
    layers = lax.axis_size("layer")
    offsets = slab_offsets * layers
    half = offsets // 2
    layer_id = lax.axis_index("layer")
    sizes = tuple(lax.axis_size(name) for name in MESH_AXES)

    keep = pattern.astype(jnp.bfloat16)[:, None, :, None]
    masked = (density.reshape(block_rows, bs, slab_offsets, bs) * keep).reshape(rows_dev, slab_cols)
    own_band = layer_gather(sizes, masked, 1)

    total_rows = block_rows + offsets - 1
    width = slab_offsets + block_rows - 1
    pad_l = total_rows - 1 - half
    far = layers // 2
    width = width + width % 2
    pair_width = width + slab_offsets
    span = pad_l + 2 * block_rows + pair_width + 2
    total_blocks = slab_offsets * (layers - 1) + span
    total_blocks += total_blocks % 2
    pad_r = total_blocks - offsets - pad_l
    band = jnp.pad(own_band.reshape(block_rows, bs, offsets * bs),
                   ((0, 0), (0, 0), (pad_l * bs, pad_r * bs)))
    moved = jnp.pad(band[:, :, bs:], ((0, 0), (0, 0), (0, bs)))
    band = jnp.stack([band, moved], axis=0)
    core = lax.rem(layer_id, 2)

    below = half
    above = total_rows - half - block_rows
    steps = []
    dist, need = 1, below
    while need > 0:
        take = min(block_rows, need)
        if dist == 1:
            lower_start = need - take
        else:
            steps.append((dist, block_rows - take, block_rows, need - take))
        need -= take
        dist += 1
    dist, need = 1, above
    while need > 0:
        take = min(block_rows, need)
        if dist == 1:
            upper_start = below + block_rows
        else:
            steps.append((-dist, 0, take, below + block_rows + (above - need)))
        need -= take
        dist += 1
    pair_steps = ((1, 0), (-1, block_rows))
    plan = (slab_offsets, block_rows, pad_l, width, pair_width, far, below,
            tuple(steps), pair_steps, (lower_start, upper_start))
    right, pair_buf = row_exchange(sizes, plan, total_rows, 2 * block_rows, band)
    right = right.reshape(total_rows * bs, width * bs)

    pattern_f = pattern.astype(jnp.float32)[:, None, :, None]

    def product(left_band):
        left = skew_rows(left_band.reshape(block_rows, bs, offsets * bs), block_rows - 1)
        left = left.reshape(rows_dev, total_rows * bs)
        dense = jnp.dot(left, right, preferred_element_type=jnp.float32)
        dense = dense.reshape(block_rows, bs, width * bs)
        out = jnp.stack(
            [dense[i, :, i * bs: (i + slab_offsets) * bs] for i in range(block_rows)], axis=0
        )
        return out.reshape(block_rows, bs, slab_offsets, bs) * pattern_f

    square = product(own_band).astype(jnp.bfloat16)
    square_full = layer_gather(sizes, square.reshape(rows_dev, slab_cols), 1)
    cubic = product(square_full)
    purified = 3.0 * square.astype(jnp.float32) - 2.0 * cubic
    return purified.reshape(rows_dev, slab_cols)


def solution(mesh):
    placed = (P("row", "layer"), P("row", "layer"))
    return jax.shard_map(
        body, mesh=mesh, in_specs=placed, out_specs=P("row", "layer"), check_vma=False
    )
```

```python
import jax
import jax.numpy as jnp
from jax import lax
from jax.sharding import PartitionSpec as P
from jax.experimental import pallas as pl
from jax.experimental.pallas import tpu as pltpu

MESH_AXES = ("layer", "row")


def _peer(sizes, layer_shift, row_shift):
    layer = lax.axis_index("layer")
    row = lax.axis_index("row")
    return (
        lax.rem(layer + layer_shift + sizes[0], sizes[0]),
        lax.rem(row + row_shift + sizes[1], sizes[1]),
    )


def _greet(sizes, shifts):
    barrier = pltpu.get_barrier_semaphore()
    for layer_shift, row_shift in shifts:
        pl.semaphore_signal(barrier, inc=1, device_id=_peer(sizes, layer_shift, row_shift),
                            device_id_type=pl.DeviceIdType.MESH)
    pl.semaphore_wait(barrier, len(shifts))


def _row_exchange_kernel(sizes, plan, *refs):
    (slab_offsets, block_rows, pad_l, width, pair_width, far, own_start,
     steps, pair_steps) = plan
    band_ref, out_ref, pair_ref = refs[:3]
    send_sem, recv_sem, pair_send, pair_recv, fwd_send, fwd_recv, local_sem, stage = refs[3:]
    me = lax.axis_index("layer")
    core = lax.rem(me, 2)
    core_shift = 1 - 2 * core
    half_rows = block_rows // 2
    shifts = [(0, shift) for shift, _, _, _ in steps]
    shifts += [(far, shift) for shift, _ in pair_steps]
    _greet(sizes, shifts + [(core_shift, 0)])
    mesh = pl.DeviceIdType.MESH

    bs = band_ref.shape[2]

    def window(j, start, count):
        odd = lax.rem(start, 2)
        first = pl.multiple_of((start - odd) * bs, 2 * bs)
        return band_ref.at[odd, j, :, pl.ds(first, count * bs)]

    def row_copy(j, start, count, dst, send, recv, target):
        return pltpu.make_async_remote_copy(
            src_ref=window(j, start, count), dst_ref=dst,
            send_sem=send, recv_sem=recv, device_id=target, device_id_type=mesh,
        )

    def group(dst_rows, count, send, recv, target):
        return pltpu.make_async_remote_copy(
            src_ref=band_ref.at[0, pl.ds(0, dst_rows.shape[0]), :, pl.ds(0, count * bs)],
            dst_ref=dst_rows, send_sem=send, recv_sem=recv, device_id=target,
            device_id_type=mesh,
        )

    waits = []
    for k, (shift, first, last, row_start) in enumerate(steps):
        target = _peer(sizes, 0, shift)
        for j in range(first, last):
            start = me * slab_offsets + block_rows * shift - j + pad_l
            row_copy(j, start, width, out_ref.at[row_start + j - first],
                     send_sem.at[k], recv_sem.at[k], target).start()
        waits.append(group(out_ref.at[pl.ds(row_start, last - first)], width,
                           send_sem.at[k], recv_sem.at[k], target))
    pair_groups = []
    pair_base = (lax.rem(me + far, sizes[0]) - core) * slab_offsets
    for k, (shift, pair_start) in enumerate(pair_steps):
        target = _peer(sizes, far, shift)
        for jj in range(half_rows):
            j = core * half_rows + jj
            start = pair_base + block_rows * shift - j + pad_l
            row_copy(j, start, pair_width, pair_ref.at[pair_start + j],
                     pair_send.at[k], pair_recv.at[k], target).start()
        held = pair_ref.at[pl.ds(pair_start + core * half_rows, half_rows)]
        pair_groups.append((held, group(held, pair_width, pair_send.at[k], pair_recv.at[k], target)))
    for j in range(block_rows):
        start = me * slab_offsets - j + pad_l
        pltpu.make_async_copy(window(j, start, width), stage.at[j], local_sem.at[0]).start()
    forwards = []
    for k, (held, grp) in enumerate(pair_groups):
        grp.wait_recv()
        forward = pltpu.make_async_remote_copy(
            src_ref=held, dst_ref=held, send_sem=fwd_send.at[k], recv_sem=fwd_recv.at[k],
            device_id=_peer(sizes, core_shift, 0), device_id_type=mesh,
        )
        forward.start()
        forwards.append(forward)
    pltpu.make_async_copy(band_ref.at[0, pl.ds(0, block_rows), :, pl.ds(0, width * bs)],
                          stage, local_sem.at[0]).wait()
    own_out = pltpu.make_async_copy(stage, out_ref.at[pl.ds(own_start, block_rows)],
                                    local_sem.at[1])
    own_out.start()
    for grp in waits:
        grp.wait()
    for k, (held, grp) in enumerate(pair_groups):
        grp.wait_send()
        forwards[k].wait()
    own_out.wait()


def row_exchange(sizes, plan, total_rows, pair_rows, band):
    (slab_offsets, block_rows, pad_l, width, pair_width, far, own_start,
     steps, pair_steps) = plan
    bs = band.shape[2]
    any_spec = pl.BlockSpec(memory_space=pl.ANY)
    n, m = len(steps), len(pair_steps)
    return pl.pallas_call(
        lambda *refs: _row_exchange_kernel(sizes, plan, *refs),
        out_shape=(jax.ShapeDtypeStruct((total_rows, bs, width * bs), band.dtype),
                   jax.ShapeDtypeStruct((pair_rows, bs, pair_width * bs), band.dtype)),
        in_specs=[any_spec],
        out_specs=(any_spec, any_spec),
        scratch_shapes=[
            pltpu.SemaphoreType.DMA((n,)),
            pltpu.SemaphoreType.DMA((n,)),
            pltpu.SemaphoreType.DMA((m,)),
            pltpu.SemaphoreType.DMA((m,)),
            pltpu.SemaphoreType.DMA((m,)),
            pltpu.SemaphoreType.DMA((m,)),
            pltpu.SemaphoreType.DMA((2,)),
            pltpu.VMEM((block_rows, bs, width * bs), band.dtype),
        ],
        compiler_params=pltpu.CompilerParams(collective_id=0, has_side_effects=True),
        name="row_exchange",
    )(band)


def _layer_gather_kernel(sizes, *refs):
    src_ref, out_ref, send_sem, recv_sem = refs
    count = sizes[0]
    me = lax.axis_index("layer")
    width = src_ref.shape[1]
    core_shift = 1 - 2 * lax.rem(me, 2)
    far = count // 2
    _greet(sizes, [(far, 0), (core_shift, 0)])

    def cols(layer):
        return out_ref.at[:, pl.ds(pl.multiple_of(layer * width, width), width)]

    mine = cols(me)
    to_far = pltpu.make_async_remote_copy(
        src_ref=src_ref, dst_ref=mine, send_sem=send_sem.at[0], recv_sem=recv_sem.at[0],
        device_id=_peer(sizes, far, 0), device_id_type=pl.DeviceIdType.MESH,
    )
    to_core = pltpu.make_async_remote_copy(
        src_ref=src_ref, dst_ref=mine, send_sem=send_sem.at[1], recv_sem=recv_sem.at[1],
        device_id=_peer(sizes, core_shift, 0), device_id_type=pl.DeviceIdType.MESH,
    )
    to_far.start()
    to_core.start()
    far_layer = lax.rem(me + far, count)
    to_far.wait_recv()
    forward = pltpu.make_async_remote_copy(
        src_ref=cols(far_layer), dst_ref=cols(far_layer), send_sem=send_sem.at[2],
        recv_sem=recv_sem.at[2], device_id=_peer(sizes, core_shift, 0),
        device_id_type=pl.DeviceIdType.MESH,
    )
    forward.start()
    to_far.wait_send()
    to_core.wait()
    forward.wait()


def layer_gather(sizes, slab, collective_id):
    count = sizes[0]
    any_spec = pl.BlockSpec(memory_space=pl.ANY)
    others = pl.pallas_call(
        lambda *refs: _layer_gather_kernel(sizes, *refs),
        out_shape=jax.ShapeDtypeStruct((slab.shape[0], slab.shape[1] * count), slab.dtype),
        in_specs=[any_spec],
        out_specs=any_spec,
        scratch_shapes=[
            pltpu.SemaphoreType.DMA((3,)),
            pltpu.SemaphoreType.DMA((3,)),
        ],
        compiler_params=pltpu.CompilerParams(collective_id=collective_id, has_side_effects=True),
        name="layer_gather",
    )(slab)
    me = lax.axis_index("layer")
    return lax.dynamic_update_slice_in_dim(others, slab, me * slab.shape[1], axis=1)


def shifted(value, axis, steps):
    count = lax.axis_size(axis)
    pairs = [(source, (source + steps) % count) for source in range(count)]
    return lax.ppermute(value, axis, pairs)


def skew_rows(band, shift_total):
    n, bs, width = band.shape
    pieces = [
        jnp.pad(band[i], ((0, 0), (i * bs, (shift_total - i) * bs))) for i in range(n)
    ]
    return jnp.stack(pieces, axis=0)


def body(density, pattern):
    rows_dev, slab_cols = density.shape
    block_rows, slab_offsets = pattern.shape
    bs = rows_dev // block_rows
    layers = lax.axis_size("layer")
    offsets = slab_offsets * layers
    half = offsets // 2
    layer_id = lax.axis_index("layer")
    sizes = tuple(lax.axis_size(name) for name in MESH_AXES)

    keep = pattern.astype(jnp.bfloat16)[:, None, :, None]
    masked = (density.reshape(block_rows, bs, slab_offsets, bs) * keep).reshape(rows_dev, slab_cols)
    own_band = layer_gather(sizes, masked, 1)

    total_rows = block_rows + offsets - 1
    width = slab_offsets + block_rows - 1
    pad_l = total_rows - 1 - half
    far = layers // 2
    width = width + width % 2
    pair_width = width + slab_offsets
    span = pad_l + 2 * block_rows + pair_width + 2
    total_blocks = slab_offsets * (layers - 1) + span
    total_blocks += total_blocks % 2
    pad_r = total_blocks - offsets - pad_l
    band = jnp.pad(own_band.reshape(block_rows, bs, offsets * bs),
                   ((0, 0), (0, 0), (pad_l * bs, pad_r * bs)))
    moved = jnp.pad(band[:, :, bs:], ((0, 0), (0, 0), (0, bs)))
    band = jnp.stack([band, moved], axis=0)
    core = lax.rem(layer_id, 2)

    below = half
    above = total_rows - half - block_rows
    steps = []
    dist, need = 1, below
    while need > 0:
        take = min(block_rows, need)
        if dist == 1:
            lower_start = need - take
        else:
            steps.append((dist, block_rows - take, block_rows, need - take))
        need -= take
        dist += 1
    dist, need = 1, above
    while need > 0:
        take = min(block_rows, need)
        if dist == 1:
            upper_start = below + block_rows
        else:
            steps.append((-dist, 0, take, below + block_rows + (above - need)))
        need -= take
        dist += 1
    pair_steps = ((1, 0), (-1, block_rows))
    plan = (slab_offsets, block_rows, pad_l, width, pair_width, far, below,
            tuple(steps), pair_steps)
    right, pair_buf = row_exchange(sizes, plan, total_rows, 2 * block_rows, band)
    pair_part = lax.dynamic_slice_in_dim(pair_buf, core * slab_offsets * bs, width * bs, axis=2)
    right = jnp.concatenate([
        right[:lower_start], pair_part[:block_rows], right[below:below + block_rows],
        pair_part[block_rows:], right[upper_start + block_rows:],
    ], axis=0)
    right = right.reshape(total_rows * bs, width * bs)

    pattern_f = pattern.astype(jnp.float32)[:, None, :, None]

    def product(left_band):
        left = skew_rows(left_band.reshape(block_rows, bs, offsets * bs), block_rows - 1)
        left = left.reshape(rows_dev, total_rows * bs)
        dense = jnp.dot(left, right, preferred_element_type=jnp.float32)
        dense = dense.reshape(block_rows, bs, width * bs)
        out = jnp.stack(
            [dense[i, :, i * bs: (i + slab_offsets) * bs] for i in range(block_rows)], axis=0
        )
        return out.reshape(block_rows, bs, slab_offsets, bs) * pattern_f

    square = product(own_band).astype(jnp.bfloat16)
    square_full = layer_gather(sizes, square.reshape(rows_dev, slab_cols), 1)
    cubic = product(square_full)
    purified = 3.0 * square.astype(jnp.float32) - 2.0 * cubic
    return purified.reshape(rows_dev, slab_cols)


def solution(mesh):
    placed = (P("row", "layer"), P("row", "layer"))
    return jax.shard_map(
        body, mesh=mesh, in_specs=placed, out_specs=P("row", "layer"), check_vma=False
    )
```

```python
import jax
import jax.numpy as jnp
from jax import lax
from jax.sharding import PartitionSpec as P
from jax.experimental import pallas as pl
from jax.experimental.pallas import tpu as pltpu

MESH_AXES = ("layer", "row")


def _peer(sizes, layer_shift, row_shift):
    layer = lax.axis_index("layer")
    row = lax.axis_index("row")
    return (
        lax.rem(layer + layer_shift + sizes[0], sizes[0]),
        lax.rem(row + row_shift + sizes[1], sizes[1]),
    )


def _greet(sizes, shifts):
    barrier = pltpu.get_barrier_semaphore()
    for layer_shift, row_shift in shifts:
        pl.semaphore_signal(barrier, inc=1, device_id=_peer(sizes, layer_shift, row_shift),
                            device_id_type=pl.DeviceIdType.MESH)
    pl.semaphore_wait(barrier, len(shifts))


def _row_exchange_kernel(sizes, plan, *refs):
    (slab_offsets, block_rows, pad_l, width, pair_width, far, own_start,
     steps, pair_steps) = plan
    band_ref, out_ref, pair_ref = refs[:3]
    send_sem, recv_sem, pair_send, pair_recv, fwd_send, fwd_recv, local_sem, stage = refs[3:]
    me = lax.axis_index("layer")
    core = lax.rem(me, 2)
    core_shift = 1 - 2 * core
    half_rows = block_rows // 2
    shifts = [(0, shift) for shift, _, _, _ in steps]
    shifts += [(far, shift) for shift, _ in pair_steps]
    _greet(sizes, shifts + [(core_shift, 0)])
    mesh = pl.DeviceIdType.MESH

    bs = band_ref.shape[2]

    def window(j, start, count):
        odd = lax.rem(start, 2)
        first = pl.multiple_of((start - odd) * bs, 2 * bs)
        return band_ref.at[odd, j, :, pl.ds(first, count * bs)]

    def row_copy(j, start, count, dst, send, recv, target):
        return pltpu.make_async_remote_copy(
            src_ref=window(j, start, count), dst_ref=dst,
            send_sem=send, recv_sem=recv, device_id=target, device_id_type=mesh,
        )

    def group(dst_rows, count, send, recv, target):
        return pltpu.make_async_remote_copy(
            src_ref=band_ref.at[0, pl.ds(0, dst_rows.shape[0]), :, pl.ds(0, count * bs)],
            dst_ref=dst_rows, send_sem=send, recv_sem=recv, device_id=target,
            device_id_type=mesh,
        )

    waits = []
    for k, (shift, first, last, row_start) in enumerate(steps):
        target = _peer(sizes, 0, shift)
        for j in range(first, last):
            start = me * slab_offsets + block_rows * shift - j + pad_l
            row_copy(j, start, width, out_ref.at[row_start + j - first],
                     send_sem.at[k], recv_sem.at[k], target).start()
        waits.append(group(out_ref.at[pl.ds(row_start, last - first)], width,
                           send_sem.at[k], recv_sem.at[k], target))
    x_me = me // far
    pair_base = (lax.rem(me + far, sizes[0]) - core) * slab_offsets
    offsets = slab_offsets * sizes[0]

    def rect(shift, half):
        lo, hi = pair_width, 0
        for j in range(block_rows):
            b = 2 * slab_offsets * half + block_rows * shift - j
            lo = min(lo, max(0, -b))
            hi = max(hi, min(pair_width, offsets - b))
        lo -= lo % 2
        hi = min(pair_width, hi + hi % 2)
        return lo, hi - lo

    def held_cols(pair_start, c0, cw):
        return pair_ref.at[pl.ds(pair_start + core * half_rows, half_rows), :, pl.ds(c0 * bs, cw * bs)]

    for k, (shift, pair_start) in enumerate(pair_steps):
        target = _peer(sizes, far, shift)
        for half in range(2):
            c0, cw = rect(shift, half)

            @pl.when(x_me == 1 - half)
            def _():
                for jj in range(half_rows):
                    j = core * half_rows + jj
                    start = pair_base + block_rows * shift - j + pad_l + c0
                    row_copy(j, start, cw, pair_ref.at[pair_start + j, :, pl.ds(c0 * bs, cw * bs)],
                             pair_send.at[k], pair_recv.at[k], target).start()
    for j in range(block_rows):
        start = me * slab_offsets - j + pad_l
        pltpu.make_async_copy(window(j, start, width), stage.at[j], local_sem.at[0]).start()
    def forward(k, held):
        return pltpu.make_async_remote_copy(
            src_ref=held, dst_ref=held, send_sem=fwd_send.at[k], recv_sem=fwd_recv.at[k],
            device_id=_peer(sizes, core_shift, 0), device_id_type=mesh,
        )

    for k, (shift, pair_start) in enumerate(pair_steps):
        target = _peer(sizes, far, shift)
        for half in range(2):
            c0, cw = rect(shift, half)

            @pl.when(x_me == half)
            def _():
                held = held_cols(pair_start, c0, cw)
                group(held, cw, pair_send.at[k], pair_recv.at[k], target).wait_recv()
                forward(k, held).start()
    pltpu.make_async_copy(band_ref.at[0, pl.ds(0, block_rows), :, pl.ds(0, width * bs)],
                          stage, local_sem.at[0]).wait()
    own_out = pltpu.make_async_copy(stage, out_ref.at[pl.ds(own_start, block_rows)],
                                    local_sem.at[1])
    own_out.start()
    for grp in waits:
        grp.wait()
    for k, (shift, pair_start) in enumerate(pair_steps):
        target = _peer(sizes, far, shift)
        for half in range(2):
            c0, cw = rect(shift, half)

            @pl.when(x_me == 1 - half)
            def _():
                group(held_cols(pair_start, c0, cw), cw, pair_send.at[k], pair_recv.at[k],
                      target).wait_send()

            @pl.when(x_me == half)
            def _():
                forward(k, held_cols(pair_start, c0, cw)).wait()
    own_out.wait()


def row_exchange(sizes, plan, total_rows, pair_rows, band):
    (slab_offsets, block_rows, pad_l, width, pair_width, far, own_start,
     steps, pair_steps) = plan
    bs = band.shape[2]
    any_spec = pl.BlockSpec(memory_space=pl.ANY)
    n, m = len(steps), len(pair_steps)
    return pl.pallas_call(
        lambda *refs: _row_exchange_kernel(sizes, plan, *refs),
        out_shape=(jax.ShapeDtypeStruct((total_rows, bs, width * bs), band.dtype),
                   jax.ShapeDtypeStruct((pair_rows, bs, pair_width * bs), band.dtype)),
        in_specs=[any_spec],
        out_specs=(any_spec, any_spec),
        scratch_shapes=[
            pltpu.SemaphoreType.DMA((n,)),
            pltpu.SemaphoreType.DMA((n,)),
            pltpu.SemaphoreType.DMA((m,)),
            pltpu.SemaphoreType.DMA((m,)),
            pltpu.SemaphoreType.DMA((m,)),
            pltpu.SemaphoreType.DMA((m,)),
            pltpu.SemaphoreType.DMA((2,)),
            pltpu.VMEM((block_rows, bs, width * bs), band.dtype),
        ],
        compiler_params=pltpu.CompilerParams(collective_id=0, has_side_effects=True),
        name="row_exchange",
    )(band)


def _layer_gather_kernel(sizes, *refs):
    src_ref, out_ref, send_sem, recv_sem = refs
    count = sizes[0]
    me = lax.axis_index("layer")
    width = src_ref.shape[1]
    core_shift = 1 - 2 * lax.rem(me, 2)
    far = count // 2
    _greet(sizes, [(far, 0), (core_shift, 0)])

    def cols(layer):
        return out_ref.at[:, pl.ds(pl.multiple_of(layer * width, width), width)]

    mine = cols(me)
    to_far = pltpu.make_async_remote_copy(
        src_ref=src_ref, dst_ref=mine, send_sem=send_sem.at[0], recv_sem=recv_sem.at[0],
        device_id=_peer(sizes, far, 0), device_id_type=pl.DeviceIdType.MESH,
    )
    to_core = pltpu.make_async_remote_copy(
        src_ref=src_ref, dst_ref=mine, send_sem=send_sem.at[1], recv_sem=recv_sem.at[1],
        device_id=_peer(sizes, core_shift, 0), device_id_type=pl.DeviceIdType.MESH,
    )
    to_far.start()
    to_core.start()
    far_layer = lax.rem(me + far, count)
    to_far.wait_recv()
    forward = pltpu.make_async_remote_copy(
        src_ref=cols(far_layer), dst_ref=cols(far_layer), send_sem=send_sem.at[2],
        recv_sem=recv_sem.at[2], device_id=_peer(sizes, core_shift, 0),
        device_id_type=pl.DeviceIdType.MESH,
    )
    forward.start()
    to_far.wait_send()
    to_core.wait()
    forward.wait()


def layer_gather(sizes, slab, collective_id):
    count = sizes[0]
    any_spec = pl.BlockSpec(memory_space=pl.ANY)
    others = pl.pallas_call(
        lambda *refs: _layer_gather_kernel(sizes, *refs),
        out_shape=jax.ShapeDtypeStruct((slab.shape[0], slab.shape[1] * count), slab.dtype),
        in_specs=[any_spec],
        out_specs=any_spec,
        scratch_shapes=[
            pltpu.SemaphoreType.DMA((3,)),
            pltpu.SemaphoreType.DMA((3,)),
        ],
        compiler_params=pltpu.CompilerParams(collective_id=collective_id, has_side_effects=True),
        name="layer_gather",
    )(slab)
    me = lax.axis_index("layer")
    return lax.dynamic_update_slice_in_dim(others, slab, me * slab.shape[1], axis=1)


def shifted(value, axis, steps):
    count = lax.axis_size(axis)
    pairs = [(source, (source + steps) % count) for source in range(count)]
    return lax.ppermute(value, axis, pairs)


def skew_rows(band, shift_total):
    n, bs, width = band.shape
    pieces = [
        jnp.pad(band[i], ((0, 0), (i * bs, (shift_total - i) * bs))) for i in range(n)
    ]
    return jnp.stack(pieces, axis=0)


def body(density, pattern):
    rows_dev, slab_cols = density.shape
    block_rows, slab_offsets = pattern.shape
    bs = rows_dev // block_rows
    layers = lax.axis_size("layer")
    offsets = slab_offsets * layers
    half = offsets // 2
    layer_id = lax.axis_index("layer")
    sizes = tuple(lax.axis_size(name) for name in MESH_AXES)

    keep = pattern.astype(jnp.bfloat16)[:, None, :, None]
    masked = (density.reshape(block_rows, bs, slab_offsets, bs) * keep).reshape(rows_dev, slab_cols)
    own_band = layer_gather(sizes, masked, 1)

    total_rows = block_rows + offsets - 1
    width = slab_offsets + block_rows - 1
    pad_l = total_rows - 1 - half
    far = layers // 2
    width = width + width % 2
    pair_width = width + slab_offsets
    span = pad_l + 2 * block_rows + pair_width + 2
    total_blocks = slab_offsets * (layers - 1) + span
    total_blocks += total_blocks % 2
    pad_r = total_blocks - offsets - pad_l
    band = jnp.pad(own_band.reshape(block_rows, bs, offsets * bs),
                   ((0, 0), (0, 0), (pad_l * bs, pad_r * bs)))
    moved = jnp.pad(band[:, :, bs:], ((0, 0), (0, 0), (0, bs)))
    band = jnp.stack([band, moved], axis=0)
    core = lax.rem(layer_id, 2)

    below = half
    above = total_rows - half - block_rows
    steps = []
    dist, need = 1, below
    while need > 0:
        take = min(block_rows, need)
        if dist == 1:
            lower_start = need - take
        else:
            steps.append((dist, block_rows - take, block_rows, need - take))
        need -= take
        dist += 1
    dist, need = 1, above
    while need > 0:
        take = min(block_rows, need)
        if dist == 1:
            upper_start = below + block_rows
        else:
            steps.append((-dist, 0, take, below + block_rows + (above - need)))
        need -= take
        dist += 1
    pair_steps = ((1, 0), (-1, block_rows))
    plan = (slab_offsets, block_rows, pad_l, width, pair_width, far, below,
            tuple(steps), pair_steps)
    right, pair_buf = row_exchange(sizes, plan, total_rows, 2 * block_rows, band)
    pair_part = lax.dynamic_slice_in_dim(pair_buf, core * slab_offsets * bs, width * bs, axis=2)
    right = jnp.concatenate([
        right[:lower_start], pair_part[:block_rows], right[below:below + block_rows],
        pair_part[block_rows:], right[upper_start + block_rows:],
    ], axis=0)
    t_ids = lax.broadcasted_iota(jnp.int32, (total_rows, 1, width, 1), 0)
    u_ids = lax.broadcasted_iota(jnp.int32, (total_rows, 1, width, 1), 2)
    b_ids = layer_id * slab_offsets + half + u_ids - t_ids
    inside = (b_ids >= 0) & (b_ids < offsets)
    right = jnp.where(inside, right.reshape(total_rows, bs, width, bs), jnp.zeros((), right.dtype))
    right = right.reshape(total_rows * bs, width * bs)

    pattern_f = pattern.astype(jnp.float32)[:, None, :, None]

    def product(left_band):
        left = skew_rows(left_band.reshape(block_rows, bs, offsets * bs), block_rows - 1)
        left = left.reshape(rows_dev, total_rows * bs)
        dense = jnp.dot(left, right, preferred_element_type=jnp.float32)
        dense = dense.reshape(block_rows, bs, width * bs)
        out = jnp.stack(
            [dense[i, :, i * bs: (i + slab_offsets) * bs] for i in range(block_rows)], axis=0
        )
        return out.reshape(block_rows, bs, slab_offsets, bs) * pattern_f

    square = product(own_band).astype(jnp.bfloat16)
    square_full = layer_gather(sizes, square.reshape(rows_dev, slab_cols), 1)
    cubic = product(square_full)
    purified = 3.0 * square.astype(jnp.float32) - 2.0 * cubic
    return purified.reshape(rows_dev, slab_cols)


def solution(mesh):
    placed = (P("row", "layer"), P("row", "layer"))
    return jax.shard_map(
        body, mesh=mesh, in_specs=placed, out_specs=P("row", "layer"), check_vma=False
    )
```

```python
import jax
import jax.numpy as jnp
from jax import lax
from jax.sharding import PartitionSpec as P
from jax.experimental import pallas as pl
from jax.experimental.pallas import tpu as pltpu

MESH_AXES = ("layer", "row")


def _peer(sizes, layer_shift, row_shift):
    layer = lax.axis_index("layer")
    row = lax.axis_index("row")
    return (
        lax.rem(layer + layer_shift + sizes[0], sizes[0]),
        lax.rem(row + row_shift + sizes[1], sizes[1]),
    )


def _greet(sizes, shifts):
    barrier = pltpu.get_barrier_semaphore()
    for layer_shift, row_shift in shifts:
        pl.semaphore_signal(barrier, inc=1, device_id=_peer(sizes, layer_shift, row_shift),
                            device_id_type=pl.DeviceIdType.MESH)
    pl.semaphore_wait(barrier, len(shifts))


def _row_exchange_kernel(sizes, plan, *refs):
    (slab_offsets, block_rows, pad_l, width, pair_width, far, own_start,
     steps, pair_steps) = plan
    band_ref, out_ref, pair_ref = refs[:3]
    send_sem, recv_sem, pair_send, pair_recv, fwd_send, fwd_recv, local_sem, stage = refs[3:]
    me = lax.axis_index("layer")
    core = lax.rem(me, 2)
    core_shift = 1 - 2 * core
    half_rows = block_rows // 2
    shifts = [(0, shift) for shift, _, _, _ in steps]
    shifts += [(far, shift) for shift, _ in pair_steps]
    _greet(sizes, shifts + [(core_shift, 0)])
    mesh = pl.DeviceIdType.MESH

    bs = band_ref.shape[2]

    def window(j, start, count):
        odd = lax.rem(start, 2)
        first = pl.multiple_of((start - odd) * bs, 2 * bs)
        return band_ref.at[odd, j, :, pl.ds(first, count * bs)]

    def row_copy(j, start, count, dst, send, recv, target):
        return pltpu.make_async_remote_copy(
            src_ref=window(j, start, count), dst_ref=dst,
            send_sem=send, recv_sem=recv, device_id=target, device_id_type=mesh,
        )

    def group(dst_rows, count, send, recv, target):
        return pltpu.make_async_remote_copy(
            src_ref=band_ref.at[0, pl.ds(0, dst_rows.shape[0]), :, pl.ds(0, count * bs)],
            dst_ref=dst_rows, send_sem=send, recv_sem=recv, device_id=target,
            device_id_type=mesh,
        )

    waits = []
    for k, (shift, first, last, row_start) in enumerate(steps):
        target = _peer(sizes, 0, shift)
        for j in range(first, last):
            start = me * slab_offsets + block_rows * shift - j + pad_l
            row_copy(j, start, width, out_ref.at[row_start + j - first],
                     send_sem.at[k], recv_sem.at[k], target).start()
        waits.append(group(out_ref.at[pl.ds(row_start, last - first)], width,
                           send_sem.at[k], recv_sem.at[k], target))
    pair_base = (lax.rem(me + far, sizes[0]) - core) * slab_offsets
    pair_rows = []
    for k, (shift, pair_start) in enumerate(pair_steps):
        target = _peer(sizes, far, shift)
        for jj in range(half_rows):
            j = core * half_rows + jj
            start = pair_base + block_rows * shift - j + pad_l
            copy = row_copy(j, start, pair_width, pair_ref.at[pair_start + j],
                            pair_send.at[k * half_rows + jj], pair_recv.at[k * half_rows + jj],
                            target)
            copy.start()
            pair_rows.append(copy)
    for j in range(block_rows):
        start = me * slab_offsets - j + pad_l
        pltpu.make_async_copy(window(j, start, width), stage.at[j], local_sem.at[0]).start()
    for jj in range(half_rows):
        for k, (shift, pair_start) in enumerate(pair_steps):
            pair_rows[k * half_rows + jj].wait_recv()
            held = pair_ref.at[pair_start + core * half_rows + jj]
            pltpu.make_async_remote_copy(
                src_ref=held, dst_ref=held, send_sem=fwd_send.at[k], recv_sem=fwd_recv.at[k],
                device_id=_peer(sizes, core_shift, 0), device_id_type=mesh,
            ).start()
    pltpu.make_async_copy(band_ref.at[0, pl.ds(0, block_rows), :, pl.ds(0, width * bs)],
                          stage, local_sem.at[0]).wait()
    own_out = pltpu.make_async_copy(stage, out_ref.at[pl.ds(own_start, block_rows)],
                                    local_sem.at[1])
    own_out.start()
    for grp in waits:
        grp.wait()
    for copy in pair_rows:
        copy.wait_send()
    for k, (shift, pair_start) in enumerate(pair_steps):
        held = pair_ref.at[pl.ds(pair_start + core * half_rows, half_rows)]
        group(held, pair_width, fwd_send.at[k], fwd_recv.at[k],
              _peer(sizes, core_shift, 0)).wait()
    own_out.wait()


def row_exchange(sizes, plan, total_rows, pair_rows, band):
    (slab_offsets, block_rows, pad_l, width, pair_width, far, own_start,
     steps, pair_steps) = plan
    bs = band.shape[2]
    any_spec = pl.BlockSpec(memory_space=pl.ANY)
    n, m = len(steps), len(pair_steps)
    return pl.pallas_call(
        lambda *refs: _row_exchange_kernel(sizes, plan, *refs),
        out_shape=(jax.ShapeDtypeStruct((total_rows, bs, width * bs), band.dtype),
                   jax.ShapeDtypeStruct((pair_rows, bs, pair_width * bs), band.dtype)),
        in_specs=[any_spec],
        out_specs=(any_spec, any_spec),
        scratch_shapes=[
            pltpu.SemaphoreType.DMA((n,)),
            pltpu.SemaphoreType.DMA((n,)),
            pltpu.SemaphoreType.DMA((m * (block_rows // 2),)),
            pltpu.SemaphoreType.DMA((m * (block_rows // 2),)),
            pltpu.SemaphoreType.DMA((m,)),
            pltpu.SemaphoreType.DMA((m,)),
            pltpu.SemaphoreType.DMA((2,)),
            pltpu.VMEM((block_rows, bs, width * bs), band.dtype),
        ],
        compiler_params=pltpu.CompilerParams(collective_id=0, has_side_effects=True),
        name="row_exchange",
    )(band)


def _layer_gather_kernel(sizes, *refs):
    src_ref, out_ref, send_sem, recv_sem = refs
    count = sizes[0]
    me = lax.axis_index("layer")
    width = src_ref.shape[1]
    core_shift = 1 - 2 * lax.rem(me, 2)
    far = count // 2
    _greet(sizes, [(far, 0), (core_shift, 0)])

    def cols(layer):
        return out_ref.at[:, pl.ds(pl.multiple_of(layer * width, width), width)]

    mine = cols(me)
    to_far = pltpu.make_async_remote_copy(
        src_ref=src_ref, dst_ref=mine, send_sem=send_sem.at[0], recv_sem=recv_sem.at[0],
        device_id=_peer(sizes, far, 0), device_id_type=pl.DeviceIdType.MESH,
    )
    to_core = pltpu.make_async_remote_copy(
        src_ref=src_ref, dst_ref=mine, send_sem=send_sem.at[1], recv_sem=recv_sem.at[1],
        device_id=_peer(sizes, core_shift, 0), device_id_type=pl.DeviceIdType.MESH,
    )
    to_far.start()
    to_core.start()
    far_layer = lax.rem(me + far, count)
    to_far.wait_recv()
    forward = pltpu.make_async_remote_copy(
        src_ref=cols(far_layer), dst_ref=cols(far_layer), send_sem=send_sem.at[2],
        recv_sem=recv_sem.at[2], device_id=_peer(sizes, core_shift, 0),
        device_id_type=pl.DeviceIdType.MESH,
    )
    forward.start()
    to_far.wait_send()
    to_core.wait()
    forward.wait()


def layer_gather(sizes, slab, collective_id):
    count = sizes[0]
    any_spec = pl.BlockSpec(memory_space=pl.ANY)
    others = pl.pallas_call(
        lambda *refs: _layer_gather_kernel(sizes, *refs),
        out_shape=jax.ShapeDtypeStruct((slab.shape[0], slab.shape[1] * count), slab.dtype),
        in_specs=[any_spec],
        out_specs=any_spec,
        scratch_shapes=[
            pltpu.SemaphoreType.DMA((3,)),
            pltpu.SemaphoreType.DMA((3,)),
        ],
        compiler_params=pltpu.CompilerParams(collective_id=collective_id, has_side_effects=True),
        name="layer_gather",
    )(slab)
    me = lax.axis_index("layer")
    return lax.dynamic_update_slice_in_dim(others, slab, me * slab.shape[1], axis=1)


def shifted(value, axis, steps):
    count = lax.axis_size(axis)
    pairs = [(source, (source + steps) % count) for source in range(count)]
    return lax.ppermute(value, axis, pairs)


def skew_rows(band, shift_total):
    n, bs, width = band.shape
    pieces = [
        jnp.pad(band[i], ((0, 0), (i * bs, (shift_total - i) * bs))) for i in range(n)
    ]
    return jnp.stack(pieces, axis=0)


def body(density, pattern):
    rows_dev, slab_cols = density.shape
    block_rows, slab_offsets = pattern.shape
    bs = rows_dev // block_rows
    layers = lax.axis_size("layer")
    offsets = slab_offsets * layers
    half = offsets // 2
    layer_id = lax.axis_index("layer")
    sizes = tuple(lax.axis_size(name) for name in MESH_AXES)

    keep = pattern.astype(jnp.bfloat16)[:, None, :, None]
    masked = (density.reshape(block_rows, bs, slab_offsets, bs) * keep).reshape(rows_dev, slab_cols)
    own_band = layer_gather(sizes, masked, 1)

    total_rows = block_rows + offsets - 1
    width = slab_offsets + block_rows - 1
    pad_l = total_rows - 1 - half
    far = layers // 2
    width = width + width % 2
    pair_width = width + slab_offsets
    span = pad_l + 2 * block_rows + pair_width + 2
    total_blocks = slab_offsets * (layers - 1) + span
    total_blocks += total_blocks % 2
    pad_r = total_blocks - offsets - pad_l
    band = jnp.pad(own_band.reshape(block_rows, bs, offsets * bs),
                   ((0, 0), (0, 0), (pad_l * bs, pad_r * bs)))
    moved = jnp.pad(band[:, :, bs:], ((0, 0), (0, 0), (0, bs)))
    band = jnp.stack([band, moved], axis=0)
    core = lax.rem(layer_id, 2)

    below = half
    above = total_rows - half - block_rows
    steps = []
    dist, need = 1, below
    while need > 0:
        take = min(block_rows, need)
        if dist == 1:
            lower_start = need - take
        else:
            steps.append((dist, block_rows - take, block_rows, need - take))
        need -= take
        dist += 1
    dist, need = 1, above
    while need > 0:
        take = min(block_rows, need)
        if dist == 1:
            upper_start = below + block_rows
        else:
            steps.append((-dist, 0, take, below + block_rows + (above - need)))
        need -= take
        dist += 1
    pair_steps = ((1, 0), (-1, block_rows))
    plan = (slab_offsets, block_rows, pad_l, width, pair_width, far, below,
            tuple(steps), pair_steps)
    right, pair_buf = row_exchange(sizes, plan, total_rows, 2 * block_rows, band)
    pair_part = lax.dynamic_slice_in_dim(pair_buf, core * slab_offsets * bs, width * bs, axis=2)
    right = jnp.concatenate([
        right[:lower_start], pair_part[:block_rows], right[below:below + block_rows],
        pair_part[block_rows:], right[upper_start + block_rows:],
    ], axis=0)
    right = right.reshape(total_rows * bs, width * bs)

    pattern_f = pattern.astype(jnp.float32)[:, None, :, None]

    def product(left_band):
        left = skew_rows(left_band.reshape(block_rows, bs, offsets * bs), block_rows - 1)
        left = left.reshape(rows_dev, total_rows * bs)
        dense = jnp.dot(left, right, preferred_element_type=jnp.float32)
        dense = dense.reshape(block_rows, bs, width * bs)
        out = jnp.stack(
            [dense[i, :, i * bs: (i + slab_offsets) * bs] for i in range(block_rows)], axis=0
        )
        return out.reshape(block_rows, bs, slab_offsets, bs) * pattern_f

    square = product(own_band).astype(jnp.bfloat16)
    square_full = layer_gather(sizes, square.reshape(rows_dev, slab_cols), 1)
    cubic = product(square_full)
    purified = 3.0 * square.astype(jnp.float32) - 2.0 * cubic
    return purified.reshape(rows_dev, slab_cols)


def solution(mesh):
    placed = (P("row", "layer"), P("row", "layer"))
    return jax.shard_map(
        body, mesh=mesh, in_specs=placed, out_specs=P("row", "layer"), check_vma=False
    )
```

```python
import jax
import jax.numpy as jnp
from jax import lax
from jax.sharding import PartitionSpec as P
from jax.experimental import pallas as pl
from jax.experimental.pallas import tpu as pltpu

MESH_AXES = ("layer", "row")


def _peer(sizes, layer_shift, row_shift):
    layer = lax.axis_index("layer")
    row = lax.axis_index("row")
    return (
        lax.rem(layer + layer_shift + sizes[0], sizes[0]),
        lax.rem(row + row_shift + sizes[1], sizes[1]),
    )


def _greet(sizes, shifts):
    barrier = pltpu.get_barrier_semaphore()
    for layer_shift, row_shift in shifts:
        pl.semaphore_signal(barrier, inc=1, device_id=_peer(sizes, layer_shift, row_shift),
                            device_id_type=pl.DeviceIdType.MESH)
    pl.semaphore_wait(barrier, len(shifts))


def _row_exchange_kernel(sizes, plan, *refs):
    (slab_offsets, block_rows, pad_l, width, pair_width, far, own_start,
     steps, pair_steps) = plan
    band_ref, out_ref, pair_ref = refs[:3]
    send_sem, recv_sem, pair_send, pair_recv, fwd_send, fwd_recv, local_sem, stage = refs[3:]
    me = lax.axis_index("layer")
    core = lax.rem(me, 2)
    core_shift = 1 - 2 * core
    half_rows = block_rows // 2
    shifts = [(0, shift) for shift, _, _, _ in steps]
    shifts += [(far, shift) for shift, _ in pair_steps]
    _greet(sizes, shifts + [(core_shift, 0)])
    mesh = pl.DeviceIdType.MESH

    bs = band_ref.shape[2]

    def window(j, start, count):
        odd = lax.rem(start, 2)
        first = pl.multiple_of((start - odd) * bs, 2 * bs)
        return band_ref.at[odd, j, :, pl.ds(first, count * bs)]

    def row_copy(j, start, count, dst, send, recv, target):
        return pltpu.make_async_remote_copy(
            src_ref=window(j, start, count), dst_ref=dst,
            send_sem=send, recv_sem=recv, device_id=target, device_id_type=mesh,
        )

    def group(dst_rows, count, send, recv, target):
        return pltpu.make_async_remote_copy(
            src_ref=band_ref.at[0, pl.ds(0, dst_rows.shape[0]), :, pl.ds(0, count * bs)],
            dst_ref=dst_rows, send_sem=send, recv_sem=recv, device_id=target,
            device_id_type=mesh,
        )

    waits = []
    for k, (shift, first, last, row_start) in enumerate(steps):
        target = _peer(sizes, 0, shift)
        for j in range(first, last):
            start = me * slab_offsets + block_rows * shift - j + pad_l
            row_copy(j, start, width, out_ref.at[row_start + j - first],
                     send_sem.at[k], recv_sem.at[k], target).start()
        waits.append(group(out_ref.at[pl.ds(row_start, last - first)], width,
                           send_sem.at[k], recv_sem.at[k], target))
    pair_base = (lax.rem(me + far, sizes[0]) - core) * slab_offsets
    pair_rows = []
    for k, (shift, pair_start) in enumerate(pair_steps):
        target = _peer(sizes, far, shift)
        for jj in range(half_rows):
            j = core * half_rows + jj
            start = pair_base + block_rows * shift - j + pad_l
            copy = row_copy(j, start, pair_width, pair_ref.at[pair_start + j],
                            pair_send.at[k * half_rows + jj], pair_recv.at[k * half_rows + jj],
                            target)
            copy.start()
            pair_rows.append(copy)
    for j in range(block_rows):
        start = me * slab_offsets - j + pad_l
        pltpu.make_async_copy(window(j, start, width), stage.at[j], local_sem.at[0]).start()
    for jj in range(half_rows):
        for k, (shift, pair_start) in enumerate(pair_steps):
            pair_rows[k * half_rows + jj].wait_recv()
            held = pair_ref.at[pair_start + core * half_rows + jj]
            pltpu.make_async_remote_copy(
                src_ref=held, dst_ref=held, send_sem=fwd_send.at[k], recv_sem=fwd_recv.at[k],
                device_id=_peer(sizes, core_shift, 0), device_id_type=mesh,
            ).start()
    pltpu.make_async_copy(band_ref.at[0, pl.ds(0, block_rows), :, pl.ds(0, width * bs)],
                          stage, local_sem.at[0]).wait()
    own_out = pltpu.make_async_copy(stage, out_ref.at[pl.ds(own_start, block_rows)],
                                    local_sem.at[1])
    own_out.start()
    for grp in waits:
        grp.wait()
    for copy in pair_rows:
        copy.wait_send()
    for k, (shift, pair_start) in enumerate(pair_steps):
        held = pair_ref.at[pl.ds(pair_start + core * half_rows, half_rows)]
        group(held, pair_width, fwd_send.at[k], fwd_recv.at[k],
              _peer(sizes, core_shift, 0)).wait()
    own_out.wait()


def row_exchange(sizes, plan, total_rows, pair_rows, band):
    (slab_offsets, block_rows, pad_l, width, pair_width, far, own_start,
     steps, pair_steps) = plan
    bs = band.shape[2]
    any_spec = pl.BlockSpec(memory_space=pl.ANY)
    n, m = len(steps), len(pair_steps)
    return pl.pallas_call(
        lambda *refs: _row_exchange_kernel(sizes, plan, *refs),
        out_shape=(jax.ShapeDtypeStruct((total_rows, bs, width * bs), band.dtype),
                   jax.ShapeDtypeStruct((pair_rows, bs, pair_width * bs), band.dtype)),
        in_specs=[any_spec],
        out_specs=(any_spec, any_spec),
        scratch_shapes=[
            pltpu.SemaphoreType.DMA((n,)),
            pltpu.SemaphoreType.DMA((n,)),
            pltpu.SemaphoreType.DMA((m * (block_rows // 2),)),
            pltpu.SemaphoreType.DMA((m * (block_rows // 2),)),
            pltpu.SemaphoreType.DMA((m,)),
            pltpu.SemaphoreType.DMA((m,)),
            pltpu.SemaphoreType.DMA((2,)),
            pltpu.VMEM((block_rows, bs, width * bs), band.dtype),
        ],
        compiler_params=pltpu.CompilerParams(collective_id=0, has_side_effects=True),
        name="row_exchange",
    )(band)


def _layer_gather_kernel(sizes, *refs):
    src_ref, out_ref, send_sem, recv_sem = refs
    count = sizes[0]
    me = lax.axis_index("layer")
    width = src_ref.shape[1]
    core_shift = 1 - 2 * lax.rem(me, 2)
    far = count // 2
    _greet(sizes, [(far, 0), (core_shift, 0)])

    def cols(layer):
        return out_ref.at[:, pl.ds(pl.multiple_of(layer * width, width), width)]

    mine = cols(me)
    to_far = pltpu.make_async_remote_copy(
        src_ref=src_ref, dst_ref=mine, send_sem=send_sem.at[0], recv_sem=recv_sem.at[0],
        device_id=_peer(sizes, far, 0), device_id_type=pl.DeviceIdType.MESH,
    )
    to_core = pltpu.make_async_remote_copy(
        src_ref=src_ref, dst_ref=mine, send_sem=send_sem.at[1], recv_sem=recv_sem.at[1],
        device_id=_peer(sizes, core_shift, 0), device_id_type=pl.DeviceIdType.MESH,
    )
    to_far.start()
    to_core.start()
    far_layer = lax.rem(me + far, count)
    to_far.wait_recv()
    forward = pltpu.make_async_remote_copy(
        src_ref=cols(far_layer), dst_ref=cols(far_layer), send_sem=send_sem.at[2],
        recv_sem=recv_sem.at[2], device_id=_peer(sizes, core_shift, 0),
        device_id_type=pl.DeviceIdType.MESH,
    )
    forward.start()
    to_far.wait_send()
    to_core.wait()
    forward.wait()


def layer_gather(sizes, slab, collective_id):
    count = sizes[0]
    any_spec = pl.BlockSpec(memory_space=pl.ANY)
    others = pl.pallas_call(
        lambda *refs: _layer_gather_kernel(sizes, *refs),
        out_shape=jax.ShapeDtypeStruct((slab.shape[0], slab.shape[1] * count), slab.dtype),
        in_specs=[any_spec],
        out_specs=any_spec,
        scratch_shapes=[
            pltpu.SemaphoreType.DMA((3,)),
            pltpu.SemaphoreType.DMA((3,)),
        ],
        compiler_params=pltpu.CompilerParams(collective_id=collective_id, has_side_effects=True),
        name="layer_gather",
    )(slab)
    me = lax.axis_index("layer")
    return lax.dynamic_update_slice_in_dim(others, slab, me * slab.shape[1], axis=1)


def shifted(value, axis, steps):
    count = lax.axis_size(axis)
    pairs = [(source, (source + steps) % count) for source in range(count)]
    return lax.ppermute(value, axis, pairs)


def skew_rows(band, shift_total):
    n, bs, width = band.shape
    pieces = [
        jnp.pad(band[i], ((0, 0), (i * bs, (shift_total - i) * bs))) for i in range(n)
    ]
    return jnp.stack(pieces, axis=0)


def body(density, pattern):
    rows_dev, slab_cols = density.shape
    block_rows, slab_offsets = pattern.shape
    bs = rows_dev // block_rows
    layers = lax.axis_size("layer")
    offsets = slab_offsets * layers
    half = offsets // 2
    layer_id = lax.axis_index("layer")
    sizes = tuple(lax.axis_size(name) for name in MESH_AXES)

    keep = pattern.astype(jnp.bfloat16)[:, None, :, None]
    masked = (density.reshape(block_rows, bs, slab_offsets, bs) * keep).reshape(rows_dev, slab_cols)
    own_band = layer_gather(sizes, masked, 1)

    total_rows = block_rows + offsets - 1
    width = slab_offsets + block_rows - 1
    pad_l = total_rows - 1 - half
    far = layers // 2
    width = width + width % 2
    pair_width = width + slab_offsets
    reach = (half + block_rows - 1) // block_rows
    total_blocks = max(
        slab_offsets * (layers - 1) + block_rows * reach + pad_l + width,
        slab_offsets * (layers - 2) + block_rows + pad_l + pair_width,
        pad_l + offsets,
    )
    total_blocks += total_blocks % 2
    pad_r = total_blocks - offsets - pad_l
    band = jnp.pad(own_band.reshape(block_rows, bs, offsets * bs),
                   ((0, 0), (0, 0), (pad_l * bs, pad_r * bs)))
    moved = jnp.pad(band[:, :, bs:], ((0, 0), (0, 0), (0, bs)))
    band = jnp.stack([band, moved], axis=0)
    core = lax.rem(layer_id, 2)

    below = half
    above = total_rows - half - block_rows
    steps = []
    dist, need = 1, below
    while need > 0:
        take = min(block_rows, need)
        if dist == 1:
            lower_start = need - take
        else:
            steps.append((dist, block_rows - take, block_rows, need - take))
        need -= take
        dist += 1
    dist, need = 1, above
    while need > 0:
        take = min(block_rows, need)
        if dist == 1:
            upper_start = below + block_rows
        else:
            steps.append((-dist, 0, take, below + block_rows + (above - need)))
        need -= take
        dist += 1
    pair_steps = ((1, 0), (-1, block_rows))
    plan = (slab_offsets, block_rows, pad_l, width, pair_width, far, below,
            tuple(steps), pair_steps)
    right, pair_buf = row_exchange(sizes, plan, total_rows, 2 * block_rows, band)
    pair_part = lax.dynamic_slice_in_dim(pair_buf, core * slab_offsets * bs, width * bs, axis=2)
    right = lax.dynamic_update_slice_in_dim(right, pair_part[:block_rows], lower_start, axis=0)
    right = lax.dynamic_update_slice_in_dim(right, pair_part[block_rows:], upper_start, axis=0)
    right = right.reshape(total_rows * bs, width * bs)

    pattern_f = pattern.astype(jnp.float32)[:, None, :, None]

    def product(left_band):
        left = skew_rows(left_band.reshape(block_rows, bs, offsets * bs), block_rows - 1)
        left = left.reshape(rows_dev, total_rows * bs)
        dense = jnp.dot(left, right, preferred_element_type=jnp.float32)
        dense = dense.reshape(block_rows, bs, width * bs)
        out = jnp.stack(
            [dense[i, :, i * bs: (i + slab_offsets) * bs] for i in range(block_rows)], axis=0
        )
        return out.reshape(block_rows, bs, slab_offsets, bs) * pattern_f

    square = product(own_band).astype(jnp.bfloat16)
    square_full = layer_gather(sizes, square.reshape(rows_dev, slab_cols), 1)
    cubic = product(square_full)
    purified = 3.0 * square.astype(jnp.float32) - 2.0 * cubic
    return purified.reshape(rows_dev, slab_cols)


def solution(mesh):
    placed = (P("row", "layer"), P("row", "layer"))
    return jax.shard_map(
        body, mesh=mesh, in_specs=placed, out_specs=P("row", "layer"), check_vma=False
    )
```

```python
import jax
import jax.numpy as jnp
from jax import lax
from jax.sharding import PartitionSpec as P
from jax.experimental import pallas as pl
from jax.experimental.pallas import tpu as pltpu

MESH_AXES = ("layer", "row")


def _peer(sizes, layer_shift, row_shift):
    layer = lax.axis_index("layer")
    row = lax.axis_index("row")
    return (
        lax.rem(layer + layer_shift + sizes[0], sizes[0]),
        lax.rem(row + row_shift + sizes[1], sizes[1]),
    )


def _greet(sizes, shifts):
    barrier = pltpu.get_barrier_semaphore()
    for layer_shift, row_shift in shifts:
        pl.semaphore_signal(barrier, inc=1, device_id=_peer(sizes, layer_shift, row_shift),
                            device_id_type=pl.DeviceIdType.MESH)
    pl.semaphore_wait(barrier, len(shifts))


def _row_exchange_kernel(sizes, plan, *refs):
    (slab_offsets, block_rows, pad_l, width, pair_width, far, own_start,
     steps, pair_steps) = plan
    band_ref, out_ref, pair_ref = refs[:3]
    send_sem, recv_sem, pair_send, pair_recv, fwd_send, fwd_recv, local_sem, stage = refs[3:]
    me = lax.axis_index("layer")
    core = lax.rem(me, 2)
    core_shift = 1 - 2 * core
    half_rows = block_rows // 2
    shifts = [(0, shift) for shift, _, _, _ in steps]
    shifts += [(far, shift) for shift, _ in pair_steps]
    _greet(sizes, shifts + [(core_shift, 0)])
    mesh = pl.DeviceIdType.MESH

    bs = band_ref.shape[2]

    def window(j, start, count):
        odd = lax.rem(start, 2)
        first = pl.multiple_of((start - odd) * bs, 2 * bs)
        return band_ref.at[odd, j, :, pl.ds(first, count * bs)]

    def row_copy(j, start, count, dst, send, recv, target):
        return pltpu.make_async_remote_copy(
            src_ref=window(j, start, count), dst_ref=dst,
            send_sem=send, recv_sem=recv, device_id=target, device_id_type=mesh,
        )

    def group(dst_rows, count, send, recv, target):
        return pltpu.make_async_remote_copy(
            src_ref=band_ref.at[0, pl.ds(0, dst_rows.shape[0]), :, pl.ds(0, count * bs)],
            dst_ref=dst_rows, send_sem=send, recv_sem=recv, device_id=target,
            device_id_type=mesh,
        )

    waits = []
    for k, (shift, first, last, row_start) in enumerate(steps):
        target = _peer(sizes, 0, shift)
        for j in range(first, last):
            start = me * slab_offsets + block_rows * shift - j + pad_l
            row_copy(j, start, width, out_ref.at[row_start + j - first],
                     send_sem.at[k], recv_sem.at[k], target).start()
        waits.append(group(out_ref.at[pl.ds(row_start, last - first)], width,
                           send_sem.at[k], recv_sem.at[k], target))
    pair_base = (lax.rem(me + far, sizes[0]) - core) * slab_offsets
    pair_rows = []
    for k, (shift, pair_start) in enumerate(pair_steps):
        target = _peer(sizes, far, shift)
        for jj in range(half_rows):
            j = core * half_rows + jj
            start = pair_base + block_rows * shift - j + pad_l
            copy = row_copy(j, start, pair_width, pair_ref.at[pair_start + j],
                            pair_send.at[k * half_rows + jj], pair_recv.at[k * half_rows + jj],
                            target)
            copy.start()
            pair_rows.append(copy)
    for j in range(block_rows):
        start = me * slab_offsets - j + pad_l
        pltpu.make_async_copy(window(j, start, width), stage.at[j], local_sem.at[0]).start()
    for jj in range(half_rows):
        for k, (shift, pair_start) in enumerate(pair_steps):
            pair_rows[k * half_rows + jj].wait_recv()
            held = pair_ref.at[pair_start + core * half_rows + jj]
            pltpu.make_async_remote_copy(
                src_ref=held, dst_ref=held, send_sem=fwd_send.at[k], recv_sem=fwd_recv.at[k],
                device_id=_peer(sizes, core_shift, 0), device_id_type=mesh,
            ).start()
    pltpu.make_async_copy(band_ref.at[0, pl.ds(0, block_rows), :, pl.ds(0, width * bs)],
                          stage, local_sem.at[0]).wait()
    own_out = pltpu.make_async_copy(stage, out_ref.at[pl.ds(own_start, block_rows)],
                                    local_sem.at[1])
    own_out.start()
    for grp in waits:
        grp.wait()
    for copy in pair_rows:
        copy.wait_send()
    for k, (shift, pair_start) in enumerate(pair_steps):
        held = pair_ref.at[pl.ds(pair_start + core * half_rows, half_rows)]
        group(held, pair_width, fwd_send.at[k], fwd_recv.at[k],
              _peer(sizes, core_shift, 0)).wait()
    own_out.wait()


def row_exchange(sizes, plan, total_rows, pair_rows, band):
    (slab_offsets, block_rows, pad_l, width, pair_width, far, own_start,
     steps, pair_steps) = plan
    bs = band.shape[2]
    any_spec = pl.BlockSpec(memory_space=pl.ANY)
    n, m = len(steps), len(pair_steps)
    return pl.pallas_call(
        lambda *refs: _row_exchange_kernel(sizes, plan, *refs),
        out_shape=(jax.ShapeDtypeStruct((total_rows, bs, width * bs), band.dtype),
                   jax.ShapeDtypeStruct((pair_rows, bs, pair_width * bs), band.dtype)),
        in_specs=[any_spec],
        out_specs=(any_spec, any_spec),
        scratch_shapes=[
            pltpu.SemaphoreType.DMA((n,)),
            pltpu.SemaphoreType.DMA((n,)),
            pltpu.SemaphoreType.DMA((m * (block_rows // 2),)),
            pltpu.SemaphoreType.DMA((m * (block_rows // 2),)),
            pltpu.SemaphoreType.DMA((m,)),
            pltpu.SemaphoreType.DMA((m,)),
            pltpu.SemaphoreType.DMA((2,)),
            pltpu.VMEM((block_rows, bs, width * bs), band.dtype),
        ],
        compiler_params=pltpu.CompilerParams(collective_id=0, has_side_effects=True),
        name="row_exchange",
    )(band)


def _layer_gather_kernel(sizes, *refs):
    src_ref, out_ref, send_sem, recv_sem = refs
    count = sizes[0]
    me = lax.axis_index("layer")
    width = src_ref.shape[1]
    core_shift = 1 - 2 * lax.rem(me, 2)
    far = count // 2
    _greet(sizes, [(far, 0), (core_shift, 0)])

    def cols(layer):
        return out_ref.at[:, pl.ds(pl.multiple_of(layer * width, width), width)]

    mine = cols(me)
    rows = src_ref.shape[0]
    chunks = 4 if rows % 32 == 0 else 1
    part = rows // chunks
    mesh = pl.DeviceIdType.MESH
    to_far = []
    for c in range(chunks):
        piece = pl.ds(c * part, part)
        copy = pltpu.make_async_remote_copy(
            src_ref=src_ref.at[piece], dst_ref=mine.at[piece], send_sem=send_sem.at[c],
            recv_sem=recv_sem.at[c], device_id=_peer(sizes, far, 0), device_id_type=mesh,
        )
        copy.start()
        to_far.append(copy)
    to_core = pltpu.make_async_remote_copy(
        src_ref=src_ref, dst_ref=mine, send_sem=send_sem.at[chunks],
        recv_sem=recv_sem.at[chunks], device_id=_peer(sizes, core_shift, 0),
        device_id_type=mesh,
    )
    to_core.start()
    far_cols = cols(lax.rem(me + far, count))
    for c in range(chunks):
        piece = pl.ds(c * part, part)
        to_far[c].wait_recv()
        pltpu.make_async_remote_copy(
            src_ref=far_cols.at[piece], dst_ref=far_cols.at[piece],
            send_sem=send_sem.at[chunks + 1], recv_sem=recv_sem.at[chunks + 1],
            device_id=_peer(sizes, core_shift, 0), device_id_type=mesh,
        ).start()
    for c in range(chunks):
        to_far[c].wait_send()
    to_core.wait()
    pltpu.make_async_remote_copy(
        src_ref=far_cols, dst_ref=far_cols, send_sem=send_sem.at[chunks + 1],
        recv_sem=recv_sem.at[chunks + 1], device_id=_peer(sizes, core_shift, 0),
        device_id_type=mesh,
    ).wait()


def layer_gather(sizes, slab, collective_id):
    count = sizes[0]
    any_spec = pl.BlockSpec(memory_space=pl.ANY)
    others = pl.pallas_call(
        lambda *refs: _layer_gather_kernel(sizes, *refs),
        out_shape=jax.ShapeDtypeStruct((slab.shape[0], slab.shape[1] * count), slab.dtype),
        in_specs=[any_spec],
        out_specs=any_spec,
        scratch_shapes=[
            pltpu.SemaphoreType.DMA((6,)),
            pltpu.SemaphoreType.DMA((6,)),
        ],
        compiler_params=pltpu.CompilerParams(collective_id=collective_id, has_side_effects=True),
        name="layer_gather",
    )(slab)
    me = lax.axis_index("layer")
    return lax.dynamic_update_slice_in_dim(others, slab, me * slab.shape[1], axis=1)


def shifted(value, axis, steps):
    count = lax.axis_size(axis)
    pairs = [(source, (source + steps) % count) for source in range(count)]
    return lax.ppermute(value, axis, pairs)


def skew_rows(band, shift_total):
    n, bs, width = band.shape
    pieces = [
        jnp.pad(band[i], ((0, 0), (i * bs, (shift_total - i) * bs))) for i in range(n)
    ]
    return jnp.stack(pieces, axis=0)


def body(density, pattern):
    rows_dev, slab_cols = density.shape
    block_rows, slab_offsets = pattern.shape
    bs = rows_dev // block_rows
    layers = lax.axis_size("layer")
    offsets = slab_offsets * layers
    half = offsets // 2
    layer_id = lax.axis_index("layer")
    sizes = tuple(lax.axis_size(name) for name in MESH_AXES)

    keep = pattern.astype(jnp.bfloat16)[:, None, :, None]
    masked = (density.reshape(block_rows, bs, slab_offsets, bs) * keep).reshape(rows_dev, slab_cols)
    own_band = layer_gather(sizes, masked, 1)

    total_rows = block_rows + offsets - 1
    width = slab_offsets + block_rows - 1
    pad_l = total_rows - 1 - half
    far = layers // 2
    width = width + width % 2
    pair_width = width + slab_offsets
    reach = (half + block_rows - 1) // block_rows
    total_blocks = max(
        slab_offsets * (layers - 1) + block_rows * reach + pad_l + width,
        slab_offsets * (layers - 2) + block_rows + pad_l + pair_width,
        pad_l + offsets,
    )
    total_blocks += total_blocks % 2
    pad_r = total_blocks - offsets - pad_l
    band = jnp.pad(own_band.reshape(block_rows, bs, offsets * bs),
                   ((0, 0), (0, 0), (pad_l * bs, pad_r * bs)))
    moved = jnp.pad(band[:, :, bs:], ((0, 0), (0, 0), (0, bs)))
    band = jnp.stack([band, moved], axis=0)
    core = lax.rem(layer_id, 2)

    below = half
    above = total_rows - half - block_rows
    steps = []
    dist, need = 1, below
    while need > 0:
        take = min(block_rows, need)
        if dist == 1:
            lower_start = need - take
        else:
            steps.append((dist, block_rows - take, block_rows, need - take))
        need -= take
        dist += 1
    dist, need = 1, above
    while need > 0:
        take = min(block_rows, need)
        if dist == 1:
            upper_start = below + block_rows
        else:
            steps.append((-dist, 0, take, below + block_rows + (above - need)))
        need -= take
        dist += 1
    pair_steps = ((1, 0), (-1, block_rows))
    plan = (slab_offsets, block_rows, pad_l, width, pair_width, far, below,
            tuple(steps), pair_steps)
    right, pair_buf = row_exchange(sizes, plan, total_rows, 2 * block_rows, band)
    pair_part = lax.dynamic_slice_in_dim(pair_buf, core * slab_offsets * bs, width * bs, axis=2)
    right = lax.dynamic_update_slice_in_dim(right, pair_part[:block_rows], lower_start, axis=0)
    right = lax.dynamic_update_slice_in_dim(right, pair_part[block_rows:], upper_start, axis=0)
    right = right.reshape(total_rows * bs, width * bs)

    pattern_f = pattern.astype(jnp.float32)[:, None, :, None]

    def product(left_band):
        left = skew_rows(left_band.reshape(block_rows, bs, offsets * bs), block_rows - 1)
        left = left.reshape(rows_dev, total_rows * bs)
        dense = jnp.dot(left, right, preferred_element_type=jnp.float32)
        dense = dense.reshape(block_rows, bs, width * bs)
        out = jnp.stack(
            [dense[i, :, i * bs: (i + slab_offsets) * bs] for i in range(block_rows)], axis=0
        )
        return out.reshape(block_rows, bs, slab_offsets, bs) * pattern_f

    square = product(own_band).astype(jnp.bfloat16)
    square_full = layer_gather(sizes, square.reshape(rows_dev, slab_cols), 1)
    cubic = product(square_full)
    purified = 3.0 * square.astype(jnp.float32) - 2.0 * cubic
    return purified.reshape(rows_dev, slab_cols)


def solution(mesh):
    placed = (P("row", "layer"), P("row", "layer"))
    return jax.shard_map(
        body, mesh=mesh, in_specs=placed, out_specs=P("row", "layer"), check_vma=False
    )
```

```python
import jax
import jax.numpy as jnp
from jax import lax
from jax.sharding import PartitionSpec as P
from jax.experimental import pallas as pl
from jax.experimental.pallas import tpu as pltpu

MESH_AXES = ("layer", "row")


def _peer(sizes, layer_shift, row_shift):
    layer = lax.axis_index("layer")
    row = lax.axis_index("row")
    return (
        lax.rem(layer + layer_shift + sizes[0], sizes[0]),
        lax.rem(row + row_shift + sizes[1], sizes[1]),
    )


def _greet(sizes, shifts):
    barrier = pltpu.get_barrier_semaphore()
    for layer_shift, row_shift in shifts:
        pl.semaphore_signal(barrier, inc=1, device_id=_peer(sizes, layer_shift, row_shift),
                            device_id_type=pl.DeviceIdType.MESH)
    pl.semaphore_wait(barrier, len(shifts))


def _row_exchange_kernel(sizes, plan, *refs):
    (slab_offsets, block_rows, pad_l, width, pair_width, far, own_start,
     steps, pair_steps) = plan
    band_ref, moved_ref, out_ref, pair_ref = refs[:4]
    send_sem, recv_sem, pair_send, pair_recv, fwd_send, fwd_recv, local_sem, stage = refs[4:]
    me = lax.axis_index("layer")
    core = lax.rem(me, 2)
    core_shift = 1 - 2 * core
    half_rows = block_rows // 2
    shifts = [(0, shift) for shift, _, _, _ in steps]
    shifts += [(far, shift) for shift, _ in pair_steps]
    _greet(sizes, shifts + [(core_shift, 0)])
    mesh = pl.DeviceIdType.MESH

    bs = band_ref.shape[1]

    def window(j, start, count, odd):
        first = pl.multiple_of((start - odd) * bs, 2 * bs)
        return (moved_ref if odd else band_ref).at[j, :, pl.ds(first, count * bs)]

    def row_copy(j, start, count, dst, send, recv, target, odd):
        return pltpu.make_async_remote_copy(
            src_ref=window(j, start, count, odd), dst_ref=dst,
            send_sem=send, recv_sem=recv, device_id=target, device_id_type=mesh,
        )

    def group(dst_rows, count, send, recv, target):
        return pltpu.make_async_remote_copy(
            src_ref=band_ref.at[pl.ds(0, dst_rows.shape[0]), :, pl.ds(0, count * bs)],
            dst_ref=dst_rows, send_sem=send, recv_sem=recv, device_id=target,
            device_id_type=mesh,
        )

    waits = []
    for k, (shift, first, last, row_start) in enumerate(steps):
        target = _peer(sizes, 0, shift)
        for j in range(first, last):
            start = me * slab_offsets + block_rows * shift - j + pad_l
            odd = (block_rows * shift - j + pad_l) % 2
            row_copy(j, start, width, out_ref.at[row_start + j - first],
                     send_sem.at[k], recv_sem.at[k], target, odd).start()
        waits.append(group(out_ref.at[pl.ds(row_start, last - first)], width,
                           send_sem.at[k], recv_sem.at[k], target))
    pair_base = (lax.rem(me + far, sizes[0]) - core) * slab_offsets
    pair_rows = []
    for k, (shift, pair_start) in enumerate(pair_steps):
        target = _peer(sizes, far, shift)
        for jj in range(half_rows):
            j = core * half_rows + jj
            start = pair_base + block_rows * shift - j + pad_l
            sems = (pair_send.at[k * half_rows + jj], pair_recv.at[k * half_rows + jj])
            for odd in (0, 1):
                @pl.when(lax.rem(block_rows * shift - j + pad_l, 2) == odd)
                def _():
                    row_copy(j, start, pair_width, pair_ref.at[pair_start + j],
                             *sems, target, odd).start()
            pair_rows.append(pltpu.make_async_remote_copy(
                src_ref=band_ref.at[j, :, pl.ds(0, pair_width * bs)],
                dst_ref=pair_ref.at[pair_start + j], send_sem=sems[0], recv_sem=sems[1],
                device_id=target, device_id_type=mesh,
            ))
    for j in range(block_rows):
        start = me * slab_offsets - j + pad_l
        odd = (pad_l - j) % 2
        pltpu.make_async_copy(window(j, start, width, odd), stage.at[j], local_sem.at[0]).start()
    for jj in range(half_rows):
        for k, (shift, pair_start) in enumerate(pair_steps):
            pair_rows[k * half_rows + jj].wait_recv()
            held = pair_ref.at[pair_start + core * half_rows + jj]
            pltpu.make_async_remote_copy(
                src_ref=held, dst_ref=held, send_sem=fwd_send.at[k], recv_sem=fwd_recv.at[k],
                device_id=_peer(sizes, core_shift, 0), device_id_type=mesh,
            ).start()
    pltpu.make_async_copy(band_ref.at[pl.ds(0, block_rows), :, pl.ds(0, width * bs)],
                          stage, local_sem.at[0]).wait()
    own_out = pltpu.make_async_copy(stage, out_ref.at[pl.ds(own_start, block_rows)],
                                    local_sem.at[1])
    own_out.start()
    for grp in waits:
        grp.wait()
    for copy in pair_rows:
        copy.wait_send()
    for k, (shift, pair_start) in enumerate(pair_steps):
        held = pair_ref.at[pl.ds(pair_start + core * half_rows, half_rows)]
        group(held, pair_width, fwd_send.at[k], fwd_recv.at[k],
              _peer(sizes, core_shift, 0)).wait()
    own_out.wait()


def row_exchange(sizes, plan, total_rows, pair_rows, band, moved):
    (slab_offsets, block_rows, pad_l, width, pair_width, far, own_start,
     steps, pair_steps) = plan
    bs = band.shape[1]
    any_spec = pl.BlockSpec(memory_space=pl.ANY)
    n, m = len(steps), len(pair_steps)
    return pl.pallas_call(
        lambda *refs: _row_exchange_kernel(sizes, plan, *refs),
        out_shape=(jax.ShapeDtypeStruct((total_rows, bs, width * bs), band.dtype),
                   jax.ShapeDtypeStruct((pair_rows, bs, pair_width * bs), band.dtype)),
        in_specs=[any_spec, any_spec],
        out_specs=(any_spec, any_spec),
        scratch_shapes=[
            pltpu.SemaphoreType.DMA((n,)),
            pltpu.SemaphoreType.DMA((n,)),
            pltpu.SemaphoreType.DMA((m * (block_rows // 2),)),
            pltpu.SemaphoreType.DMA((m * (block_rows // 2),)),
            pltpu.SemaphoreType.DMA((m,)),
            pltpu.SemaphoreType.DMA((m,)),
            pltpu.SemaphoreType.DMA((2,)),
            pltpu.VMEM((block_rows, bs, width * bs), band.dtype),
        ],
        compiler_params=pltpu.CompilerParams(collective_id=0, has_side_effects=True),
        name="row_exchange",
    )(band, moved)


def _layer_gather_kernel(sizes, *refs):
    src_ref, out_ref, send_sem, recv_sem = refs
    count = sizes[0]
    me = lax.axis_index("layer")
    width = src_ref.shape[1]
    core_shift = 1 - 2 * lax.rem(me, 2)
    far = count // 2
    _greet(sizes, [(far, 0), (core_shift, 0)])

    def cols(layer):
        return out_ref.at[:, pl.ds(pl.multiple_of(layer * width, width), width)]

    mine = cols(me)
    rows = src_ref.shape[0]
    chunks = 4 if rows % 32 == 0 else 1
    part = rows // chunks
    mesh = pl.DeviceIdType.MESH
    to_far = []
    for c in range(chunks):
        piece = pl.ds(c * part, part)
        copy = pltpu.make_async_remote_copy(
            src_ref=src_ref.at[piece], dst_ref=mine.at[piece], send_sem=send_sem.at[c],
            recv_sem=recv_sem.at[c], device_id=_peer(sizes, far, 0), device_id_type=mesh,
        )
        copy.start()
        to_far.append(copy)
    to_core = pltpu.make_async_remote_copy(
        src_ref=src_ref, dst_ref=mine, send_sem=send_sem.at[chunks],
        recv_sem=recv_sem.at[chunks], device_id=_peer(sizes, core_shift, 0),
        device_id_type=mesh,
    )
    to_core.start()
    far_cols = cols(lax.rem(me + far, count))
    for c in range(chunks):
        piece = pl.ds(c * part, part)
        to_far[c].wait_recv()
        pltpu.make_async_remote_copy(
            src_ref=far_cols.at[piece], dst_ref=far_cols.at[piece],
            send_sem=send_sem.at[chunks + 1], recv_sem=recv_sem.at[chunks + 1],
            device_id=_peer(sizes, core_shift, 0), device_id_type=mesh,
        ).start()
    for c in range(chunks):
        to_far[c].wait_send()
    to_core.wait()
    pltpu.make_async_remote_copy(
        src_ref=far_cols, dst_ref=far_cols, send_sem=send_sem.at[chunks + 1],
        recv_sem=recv_sem.at[chunks + 1], device_id=_peer(sizes, core_shift, 0),
        device_id_type=mesh,
    ).wait()


def layer_gather(sizes, slab, collective_id):
    count = sizes[0]
    any_spec = pl.BlockSpec(memory_space=pl.ANY)
    others = pl.pallas_call(
        lambda *refs: _layer_gather_kernel(sizes, *refs),
        out_shape=jax.ShapeDtypeStruct((slab.shape[0], slab.shape[1] * count), slab.dtype),
        in_specs=[any_spec],
        out_specs=any_spec,
        scratch_shapes=[
            pltpu.SemaphoreType.DMA((6,)),
            pltpu.SemaphoreType.DMA((6,)),
        ],
        compiler_params=pltpu.CompilerParams(collective_id=collective_id, has_side_effects=True),
        name="layer_gather",
    )(slab)
    me = lax.axis_index("layer")
    return lax.dynamic_update_slice_in_dim(others, slab, me * slab.shape[1], axis=1)


def shifted(value, axis, steps):
    count = lax.axis_size(axis)
    pairs = [(source, (source + steps) % count) for source in range(count)]
    return lax.ppermute(value, axis, pairs)


def skew_rows(band, shift_total):
    n, bs, width = band.shape
    pieces = [
        jnp.pad(band[i], ((0, 0), (i * bs, (shift_total - i) * bs))) for i in range(n)
    ]
    return jnp.stack(pieces, axis=0)


def body(density, pattern):
    rows_dev, slab_cols = density.shape
    block_rows, slab_offsets = pattern.shape
    bs = rows_dev // block_rows
    layers = lax.axis_size("layer")
    offsets = slab_offsets * layers
    half = offsets // 2
    layer_id = lax.axis_index("layer")
    sizes = tuple(lax.axis_size(name) for name in MESH_AXES)

    keep = pattern.astype(jnp.bfloat16)[:, None, :, None]
    masked = (density.reshape(block_rows, bs, slab_offsets, bs) * keep).reshape(rows_dev, slab_cols)
    own_band = layer_gather(sizes, masked, 1)

    total_rows = block_rows + offsets - 1
    width = slab_offsets + block_rows - 1
    pad_l = total_rows - 1 - half
    far = layers // 2
    width = width + width % 2
    pair_width = width + slab_offsets
    reach = (half + block_rows - 1) // block_rows
    total_blocks = max(
        slab_offsets * (layers - 1) + block_rows * reach + pad_l + width,
        slab_offsets * (layers - 2) + block_rows + pad_l + pair_width,
        pad_l + offsets,
    )
    total_blocks += total_blocks % 2
    pad_r = total_blocks - offsets - pad_l
    band = jnp.pad(own_band.reshape(block_rows, bs, offsets * bs),
                   ((0, 0), (0, 0), (pad_l * bs, pad_r * bs)))
    moved = jnp.pad(own_band.reshape(block_rows, bs, offsets * bs),
                    ((0, 0), (0, 0), ((pad_l - 1) * bs, (pad_r + 1) * bs)))
    core = lax.rem(layer_id, 2)

    below = half
    above = total_rows - half - block_rows
    steps = []
    dist, need = 1, below
    while need > 0:
        take = min(block_rows, need)
        if dist == 1:
            lower_start = need - take
        else:
            steps.append((dist, block_rows - take, block_rows, need - take))
        need -= take
        dist += 1
    dist, need = 1, above
    while need > 0:
        take = min(block_rows, need)
        if dist == 1:
            upper_start = below + block_rows
        else:
            steps.append((-dist, 0, take, below + block_rows + (above - need)))
        need -= take
        dist += 1
    pair_steps = ((1, 0), (-1, block_rows))
    plan = (slab_offsets, block_rows, pad_l, width, pair_width, far, below,
            tuple(steps), pair_steps)
    right, pair_buf = row_exchange(sizes, plan, total_rows, 2 * block_rows, band, moved)
    pair_part = lax.dynamic_slice_in_dim(pair_buf, core * slab_offsets * bs, width * bs, axis=2)
    right = lax.dynamic_update_slice_in_dim(right, pair_part[:block_rows], lower_start, axis=0)
    right = lax.dynamic_update_slice_in_dim(right, pair_part[block_rows:], upper_start, axis=0)
    right = right.reshape(total_rows * bs, width * bs)

    pattern_f = pattern.astype(jnp.float32)[:, None, :, None]

    def product(left_band):
        left = skew_rows(left_band.reshape(block_rows, bs, offsets * bs), block_rows - 1)
        left = left.reshape(rows_dev, total_rows * bs)
        dense = jnp.dot(left, right, preferred_element_type=jnp.float32)
        dense = dense.reshape(block_rows, bs, width * bs)
        out = jnp.stack(
            [dense[i, :, i * bs: (i + slab_offsets) * bs] for i in range(block_rows)], axis=0
        )
        return out.reshape(block_rows, bs, slab_offsets, bs) * pattern_f

    square = product(own_band).astype(jnp.bfloat16)
    square_full = layer_gather(sizes, square.reshape(rows_dev, slab_cols), 1)
    cubic = product(square_full)
    purified = 3.0 * square.astype(jnp.float32) - 2.0 * cubic
    return purified.reshape(rows_dev, slab_cols)


def solution(mesh):
    placed = (P("row", "layer"), P("row", "layer"))
    return jax.shard_map(
        body, mesh=mesh, in_specs=placed, out_specs=P("row", "layer"), check_vma=False
    )
```

```python
import jax
import jax.numpy as jnp
from jax import lax
from jax.sharding import PartitionSpec as P
from jax.experimental import pallas as pl
from jax.experimental.pallas import tpu as pltpu

MESH_AXES = ("layer", "row")


def _peer(sizes, layer_shift, row_shift):
    layer = lax.axis_index("layer")
    row = lax.axis_index("row")
    return (
        lax.rem(layer + layer_shift + sizes[0], sizes[0]),
        lax.rem(row + row_shift + sizes[1], sizes[1]),
    )


def _greet(sizes, shifts):
    barrier = pltpu.get_barrier_semaphore()
    for layer_shift, row_shift in shifts:
        pl.semaphore_signal(barrier, inc=1, device_id=_peer(sizes, layer_shift, row_shift),
                            device_id_type=pl.DeviceIdType.MESH)
    pl.semaphore_wait(barrier, len(shifts))


def _row_exchange_kernel(sizes, plan, *refs):
    (slab_offsets, block_rows, pad_l, width, pair_width, far, own_start,
     steps, pair_steps, pair_dest) = plan
    band_ref, moved_ref, out_ref, pair_ref = refs[:4]
    (send_sem, recv_sem, pair_send, pair_recv, fwd_send, fwd_recv, local_sem, stage,
     pair_stage) = refs[4:]
    me = lax.axis_index("layer")
    core = lax.rem(me, 2)
    core_shift = 1 - 2 * core
    half_rows = block_rows // 2
    shifts = [(0, shift) for shift, _, _, _ in steps]
    shifts += [(far, shift) for shift, _ in pair_steps]
    _greet(sizes, shifts + [(core_shift, 0)])
    mesh = pl.DeviceIdType.MESH

    bs = band_ref.shape[1]

    def window(j, start, count, odd):
        first = pl.multiple_of((start - odd) * bs, 2 * bs)
        return (moved_ref if odd else band_ref).at[j, :, pl.ds(first, count * bs)]

    def row_copy(j, start, count, dst, send, recv, target, odd):
        return pltpu.make_async_remote_copy(
            src_ref=window(j, start, count, odd), dst_ref=dst,
            send_sem=send, recv_sem=recv, device_id=target, device_id_type=mesh,
        )

    def group(dst_rows, count, send, recv, target):
        return pltpu.make_async_remote_copy(
            src_ref=band_ref.at[pl.ds(0, dst_rows.shape[0]), :, pl.ds(0, count * bs)],
            dst_ref=dst_rows, send_sem=send, recv_sem=recv, device_id=target,
            device_id_type=mesh,
        )

    waits = []
    for k, (shift, first, last, row_start) in enumerate(steps):
        target = _peer(sizes, 0, shift)
        for j in range(first, last):
            start = me * slab_offsets + block_rows * shift - j + pad_l
            odd = (block_rows * shift - j + pad_l) % 2
            row_copy(j, start, width, out_ref.at[row_start + j - first],
                     send_sem.at[k], recv_sem.at[k], target, odd).start()
        waits.append(group(out_ref.at[pl.ds(row_start, last - first)], width,
                           send_sem.at[k], recv_sem.at[k], target))
    pair_base = (lax.rem(me + far, sizes[0]) - core) * slab_offsets
    pair_rows = []
    for k, (shift, pair_start) in enumerate(pair_steps):
        target = _peer(sizes, far, shift)
        for jj in range(half_rows):
            j = core * half_rows + jj
            start = pair_base + block_rows * shift - j + pad_l
            sems = (pair_send.at[k * half_rows + jj], pair_recv.at[k * half_rows + jj])
            for odd in (0, 1):
                @pl.when(lax.rem(block_rows * shift - j + pad_l, 2) == odd)
                def _():
                    row_copy(j, start, pair_width, pair_ref.at[pair_start + j],
                             *sems, target, odd).start()
            pair_rows.append(pltpu.make_async_remote_copy(
                src_ref=band_ref.at[j, :, pl.ds(0, pair_width * bs)],
                dst_ref=pair_ref.at[pair_start + j], send_sem=sems[0], recv_sem=sems[1],
                device_id=target, device_id_type=mesh,
            ))
    for j in range(block_rows):
        start = me * slab_offsets - j + pad_l
        odd = (pad_l - j) % 2
        pltpu.make_async_copy(window(j, start, width, odd), stage.at[j], local_sem.at[0]).start()
    for jj in range(half_rows):
        for k, (shift, pair_start) in enumerate(pair_steps):
            pair_rows[k * half_rows + jj].wait_recv()
            held = pair_ref.at[pair_start + core * half_rows + jj]
            pltpu.make_async_remote_copy(
                src_ref=held, dst_ref=held, send_sem=fwd_send.at[k], recv_sem=fwd_recv.at[k],
                device_id=_peer(sizes, core_shift, 0), device_id_type=mesh,
            ).start()
    pltpu.make_async_copy(band_ref.at[pl.ds(0, block_rows), :, pl.ds(0, width * bs)],
                          stage, local_sem.at[0]).wait()
    own_out = pltpu.make_async_copy(stage, out_ref.at[pl.ds(own_start, block_rows)],
                                    local_sem.at[1])
    own_out.start()
    for grp in waits:
        grp.wait()
    for copy in pair_rows:
        copy.wait_send()
    for k, (shift, pair_start) in enumerate(pair_steps):
        held = pair_ref.at[pl.ds(pair_start + core * half_rows, half_rows)]
        group(held, pair_width, fwd_send.at[k], fwd_recv.at[k],
              _peer(sizes, core_shift, 0)).wait()
    cols = pl.ds(pl.multiple_of(core * slab_offsets * bs, 2 * bs), width * bs)
    pair_count = 2 * half_rows
    takes = []
    for k, (shift, pair_start) in enumerate(pair_steps):
        take = pltpu.make_async_copy(pair_ref.at[pl.ds(pair_start, pair_count), :, cols],
                                     pair_stage.at[k], local_sem.at[2 + k])
        take.start()
        takes.append(take)
    puts = []
    for k in range(len(pair_steps)):
        takes[k].wait()
        put = pltpu.make_async_copy(pair_stage.at[k],
                                    out_ref.at[pl.ds(pair_dest[k], pair_count)],
                                    local_sem.at[2 + k])
        put.start()
        puts.append(put)
    own_out.wait()
    for put in puts:
        put.wait()


def row_exchange(sizes, plan, total_rows, pair_rows, band, moved):
    (slab_offsets, block_rows, pad_l, width, pair_width, far, own_start,
     steps, pair_steps, pair_dest) = plan
    bs = band.shape[1]
    any_spec = pl.BlockSpec(memory_space=pl.ANY)
    n, m = len(steps), len(pair_steps)
    return pl.pallas_call(
        lambda *refs: _row_exchange_kernel(sizes, plan, *refs),
        out_shape=(jax.ShapeDtypeStruct((total_rows, bs, width * bs), band.dtype),
                   jax.ShapeDtypeStruct((pair_rows, bs, pair_width * bs), band.dtype)),
        in_specs=[any_spec, any_spec],
        out_specs=(any_spec, any_spec),
        scratch_shapes=[
            pltpu.SemaphoreType.DMA((n,)),
            pltpu.SemaphoreType.DMA((n,)),
            pltpu.SemaphoreType.DMA((m * (block_rows // 2),)),
            pltpu.SemaphoreType.DMA((m * (block_rows // 2),)),
            pltpu.SemaphoreType.DMA((m,)),
            pltpu.SemaphoreType.DMA((m,)),
            pltpu.SemaphoreType.DMA((2 + m,)),
            pltpu.VMEM((block_rows, bs, width * bs), band.dtype),
            pltpu.VMEM((m, 2 * (block_rows // 2), bs, width * bs), band.dtype),
        ],
        compiler_params=pltpu.CompilerParams(collective_id=0, has_side_effects=True),
        name="row_exchange",
    )(band, moved)


def _layer_gather_kernel(sizes, *refs):
    src_ref, out_ref, send_sem, recv_sem = refs
    count = sizes[0]
    me = lax.axis_index("layer")
    width = src_ref.shape[1]
    core_shift = 1 - 2 * lax.rem(me, 2)
    far = count // 2
    _greet(sizes, [(far, 0), (core_shift, 0)])

    def cols(layer):
        return out_ref.at[:, pl.ds(pl.multiple_of(layer * width, width), width)]

    mine = cols(me)
    rows = src_ref.shape[0]
    chunks = 4 if rows % 32 == 0 else 1
    part = rows // chunks
    mesh = pl.DeviceIdType.MESH
    to_far = []
    for c in range(chunks):
        piece = pl.ds(c * part, part)
        copy = pltpu.make_async_remote_copy(
            src_ref=src_ref.at[piece], dst_ref=mine.at[piece], send_sem=send_sem.at[c],
            recv_sem=recv_sem.at[c], device_id=_peer(sizes, far, 0), device_id_type=mesh,
        )
        copy.start()
        to_far.append(copy)
    to_core = pltpu.make_async_remote_copy(
        src_ref=src_ref, dst_ref=mine, send_sem=send_sem.at[chunks],
        recv_sem=recv_sem.at[chunks], device_id=_peer(sizes, core_shift, 0),
        device_id_type=mesh,
    )
    to_core.start()
    far_cols = cols(lax.rem(me + far, count))
    for c in range(chunks):
        piece = pl.ds(c * part, part)
        to_far[c].wait_recv()
        pltpu.make_async_remote_copy(
            src_ref=far_cols.at[piece], dst_ref=far_cols.at[piece],
            send_sem=send_sem.at[chunks + 1], recv_sem=recv_sem.at[chunks + 1],
            device_id=_peer(sizes, core_shift, 0), device_id_type=mesh,
        ).start()
    for c in range(chunks):
        to_far[c].wait_send()
    to_core.wait()
    pltpu.make_async_remote_copy(
        src_ref=far_cols, dst_ref=far_cols, send_sem=send_sem.at[chunks + 1],
        recv_sem=recv_sem.at[chunks + 1], device_id=_peer(sizes, core_shift, 0),
        device_id_type=mesh,
    ).wait()


def layer_gather(sizes, slab, collective_id):
    count = sizes[0]
    any_spec = pl.BlockSpec(memory_space=pl.ANY)
    others = pl.pallas_call(
        lambda *refs: _layer_gather_kernel(sizes, *refs),
        out_shape=jax.ShapeDtypeStruct((slab.shape[0], slab.shape[1] * count), slab.dtype),
        in_specs=[any_spec],
        out_specs=any_spec,
        scratch_shapes=[
            pltpu.SemaphoreType.DMA((6,)),
            pltpu.SemaphoreType.DMA((6,)),
        ],
        compiler_params=pltpu.CompilerParams(collective_id=collective_id, has_side_effects=True),
        name="layer_gather",
    )(slab)
    me = lax.axis_index("layer")
    return lax.dynamic_update_slice_in_dim(others, slab, me * slab.shape[1], axis=1)


def shifted(value, axis, steps):
    count = lax.axis_size(axis)
    pairs = [(source, (source + steps) % count) for source in range(count)]
    return lax.ppermute(value, axis, pairs)


def skew_rows(band, shift_total):
    n, bs, width = band.shape
    pieces = [
        jnp.pad(band[i], ((0, 0), (i * bs, (shift_total - i) * bs))) for i in range(n)
    ]
    return jnp.stack(pieces, axis=0)


def body(density, pattern):
    rows_dev, slab_cols = density.shape
    block_rows, slab_offsets = pattern.shape
    bs = rows_dev // block_rows
    layers = lax.axis_size("layer")
    offsets = slab_offsets * layers
    half = offsets // 2
    layer_id = lax.axis_index("layer")
    sizes = tuple(lax.axis_size(name) for name in MESH_AXES)

    keep = pattern.astype(jnp.bfloat16)[:, None, :, None]
    masked = (density.reshape(block_rows, bs, slab_offsets, bs) * keep).reshape(rows_dev, slab_cols)
    own_band = layer_gather(sizes, masked, 1)

    total_rows = block_rows + offsets - 1
    width = slab_offsets + block_rows - 1
    pad_l = total_rows - 1 - half
    far = layers // 2
    width = width + width % 2
    pair_width = width + slab_offsets
    reach = (half + block_rows - 1) // block_rows
    total_blocks = max(
        slab_offsets * (layers - 1) + block_rows * reach + pad_l + width,
        slab_offsets * (layers - 2) + block_rows + pad_l + pair_width,
        pad_l + offsets,
    )
    total_blocks += total_blocks % 2
    pad_r = total_blocks - offsets - pad_l
    band = jnp.pad(own_band.reshape(block_rows, bs, offsets * bs),
                   ((0, 0), (0, 0), (pad_l * bs, pad_r * bs)))
    moved = jnp.pad(own_band.reshape(block_rows, bs, offsets * bs),
                    ((0, 0), (0, 0), ((pad_l - 1) * bs, (pad_r + 1) * bs)))
    core = lax.rem(layer_id, 2)

    below = half
    above = total_rows - half - block_rows
    steps = []
    dist, need = 1, below
    while need > 0:
        take = min(block_rows, need)
        if dist == 1:
            lower_start = need - take
        else:
            steps.append((dist, block_rows - take, block_rows, need - take))
        need -= take
        dist += 1
    dist, need = 1, above
    while need > 0:
        take = min(block_rows, need)
        if dist == 1:
            upper_start = below + block_rows
        else:
            steps.append((-dist, 0, take, below + block_rows + (above - need)))
        need -= take
        dist += 1
    pair_steps = ((1, 0), (-1, block_rows))
    plan = (slab_offsets, block_rows, pad_l, width, pair_width, far, below,
            tuple(steps), pair_steps, (lower_start, upper_start))
    right, pair_buf = row_exchange(sizes, plan, total_rows, 2 * block_rows, band, moved)
    right = right.reshape(total_rows * bs, width * bs)

    pattern_f = pattern.astype(jnp.float32)[:, None, :, None]

    def product(left_band):
        left = skew_rows(left_band.reshape(block_rows, bs, offsets * bs), block_rows - 1)
        left = left.reshape(rows_dev, total_rows * bs)
        dense = jnp.dot(left, right, preferred_element_type=jnp.float32)
        dense = dense.reshape(block_rows, bs, width * bs)
        out = jnp.stack(
            [dense[i, :, i * bs: (i + slab_offsets) * bs] for i in range(block_rows)], axis=0
        )
        return out.reshape(block_rows, bs, slab_offsets, bs) * pattern_f

    square = product(own_band).astype(jnp.bfloat16)
    square_full = layer_gather(sizes, square.reshape(rows_dev, slab_cols), 1)
    cubic = product(square_full)
    purified = 3.0 * square.astype(jnp.float32) - 2.0 * cubic
    return purified.reshape(rows_dev, slab_cols)


def solution(mesh):
    placed = (P("row", "layer"), P("row", "layer"))
    return jax.shard_map(
        body, mesh=mesh, in_specs=placed, out_specs=P("row", "layer"), check_vma=False
    )
```

```python
import jax
import jax.numpy as jnp
from jax import lax
from jax.sharding import PartitionSpec as P
from jax.experimental import pallas as pl
from jax.experimental.pallas import tpu as pltpu

MESH_AXES = ("layer", "row")


def _peer(sizes, layer_shift, row_shift):
    layer = lax.axis_index("layer")
    row = lax.axis_index("row")
    return (
        lax.rem(layer + layer_shift + sizes[0], sizes[0]),
        lax.rem(row + row_shift + sizes[1], sizes[1]),
    )


def _greet(sizes, shifts):
    barrier = pltpu.get_barrier_semaphore()
    for layer_shift, row_shift in shifts:
        pl.semaphore_signal(barrier, inc=1, device_id=_peer(sizes, layer_shift, row_shift),
                            device_id_type=pl.DeviceIdType.MESH)
    pl.semaphore_wait(barrier, len(shifts))


def _row_exchange_kernel(sizes, plan, *refs):
    (slab_offsets, block_rows, pad_l, width, pair_width, far, own_start,
     steps, pair_steps) = plan
    band_ref, moved_ref, out_ref, pair_ref = refs[:4]
    send_sem, recv_sem, pair_send, pair_recv, fwd_send, fwd_recv, local_sem, stage = refs[4:]
    me = lax.axis_index("layer")
    core = lax.rem(me, 2)
    core_shift = 1 - 2 * core
    half_rows = block_rows // 2
    shifts = [(0, shift) for shift, _, _, _ in steps]
    shifts += [(far, shift) for shift, _ in pair_steps]
    _greet(sizes, shifts + [(core_shift, 0)])
    mesh = pl.DeviceIdType.MESH

    bs = band_ref.shape[1]

    def window(j, start, count, odd):
        first = pl.multiple_of((start - odd) * bs, 2 * bs)
        return (moved_ref if odd else band_ref).at[j, :, pl.ds(first, count * bs)]

    def row_copy(j, start, count, dst, send, recv, target, odd):
        return pltpu.make_async_remote_copy(
            src_ref=window(j, start, count, odd), dst_ref=dst,
            send_sem=send, recv_sem=recv, device_id=target, device_id_type=mesh,
        )

    def group(dst_rows, count, send, recv, target):
        return pltpu.make_async_remote_copy(
            src_ref=band_ref.at[pl.ds(0, dst_rows.shape[0]), :, pl.ds(0, count * bs)],
            dst_ref=dst_rows, send_sem=send, recv_sem=recv, device_id=target,
            device_id_type=mesh,
        )

    waits = []
    for k, (shift, first, last, row_start) in enumerate(steps):
        target = _peer(sizes, 0, shift)
        for j in range(first, last):
            start = me * slab_offsets + block_rows * shift - j + pad_l
            odd = (block_rows * shift - j + pad_l) % 2
            row_copy(j, start, width, out_ref.at[row_start + j - first],
                     send_sem.at[k], recv_sem.at[k], target, odd).start()
        waits.append(group(out_ref.at[pl.ds(row_start, last - first)], width,
                           send_sem.at[k], recv_sem.at[k], target))
    pair_base = (lax.rem(me + far, sizes[0]) - core) * slab_offsets
    pair_rows = []
    for k, (shift, pair_start) in enumerate(pair_steps):
        target = _peer(sizes, far, shift)
        for jj in range(half_rows):
            j = core * half_rows + jj
            start = pair_base + block_rows * shift - j + pad_l
            sems = (pair_send.at[k * half_rows + jj], pair_recv.at[k * half_rows + jj])
            for odd in (0, 1):
                @pl.when(lax.rem(block_rows * shift - j + pad_l, 2) == odd)
                def _():
                    row_copy(j, start, pair_width, pair_ref.at[pair_start + j],
                             *sems, target, odd).start()
            pair_rows.append(pltpu.make_async_remote_copy(
                src_ref=band_ref.at[j, :, pl.ds(0, pair_width * bs)],
                dst_ref=pair_ref.at[pair_start + j], send_sem=sems[0], recv_sem=sems[1],
                device_id=target, device_id_type=mesh,
            ))
    for j in range(block_rows):
        start = me * slab_offsets - j + pad_l
        odd = (pad_l - j) % 2
        pltpu.make_async_copy(window(j, start, width, odd), stage.at[j], local_sem.at[0]).start()
    for jj in range(half_rows):
        for k, (shift, pair_start) in enumerate(pair_steps):
            pair_rows[k * half_rows + jj].wait_recv()
            held = pair_ref.at[pair_start + core * half_rows + jj]
            pltpu.make_async_remote_copy(
                src_ref=held, dst_ref=held, send_sem=fwd_send.at[k], recv_sem=fwd_recv.at[k],
                device_id=_peer(sizes, core_shift, 0), device_id_type=mesh,
            ).start()
    pltpu.make_async_copy(band_ref.at[pl.ds(0, block_rows), :, pl.ds(0, width * bs)],
                          stage, local_sem.at[0]).wait()
    own_out = pltpu.make_async_copy(stage, out_ref.at[pl.ds(own_start, block_rows)],
                                    local_sem.at[1])
    own_out.start()
    for grp in waits:
        grp.wait()
    for copy in pair_rows:
        copy.wait_send()
    for k, (shift, pair_start) in enumerate(pair_steps):
        held = pair_ref.at[pl.ds(pair_start + core * half_rows, half_rows)]
        group(held, pair_width, fwd_send.at[k], fwd_recv.at[k],
              _peer(sizes, core_shift, 0)).wait()
    own_out.wait()


def row_exchange(sizes, plan, total_rows, pair_rows, band, moved):
    (slab_offsets, block_rows, pad_l, width, pair_width, far, own_start,
     steps, pair_steps) = plan
    bs = band.shape[1]
    any_spec = pl.BlockSpec(memory_space=pl.ANY)
    n, m = len(steps), len(pair_steps)
    return pl.pallas_call(
        lambda *refs: _row_exchange_kernel(sizes, plan, *refs),
        out_shape=(jax.ShapeDtypeStruct((total_rows, bs, width * bs), band.dtype),
                   jax.ShapeDtypeStruct((pair_rows, bs, pair_width * bs), band.dtype)),
        in_specs=[any_spec, any_spec],
        out_specs=(any_spec, any_spec),
        scratch_shapes=[
            pltpu.SemaphoreType.DMA((n,)),
            pltpu.SemaphoreType.DMA((n,)),
            pltpu.SemaphoreType.DMA((m * (block_rows // 2),)),
            pltpu.SemaphoreType.DMA((m * (block_rows // 2),)),
            pltpu.SemaphoreType.DMA((m,)),
            pltpu.SemaphoreType.DMA((m,)),
            pltpu.SemaphoreType.DMA((2,)),
            pltpu.VMEM((block_rows, bs, width * bs), band.dtype),
        ],
        compiler_params=pltpu.CompilerParams(collective_id=0, has_side_effects=True),
        name="row_exchange",
    )(band, moved)


def _layer_gather_kernel(sizes, *refs):
    src_ref, out_ref, send_sem, recv_sem = refs
    count = sizes[0]
    me = lax.axis_index("layer")
    width = src_ref.shape[1]
    core_shift = 1 - 2 * lax.rem(me, 2)
    far = count // 2
    _greet(sizes, [(far, 0), (core_shift, 0)])

    def cols(layer):
        return out_ref.at[:, pl.ds(pl.multiple_of(layer * width, width), width)]

    mine = cols(me)
    rows = src_ref.shape[0]
    chunks = 4 if rows % 32 == 0 else 1
    part = rows // chunks
    mesh = pl.DeviceIdType.MESH
    to_far = []
    for c in range(chunks):
        piece = pl.ds(c * part, part)
        copy = pltpu.make_async_remote_copy(
            src_ref=src_ref.at[piece], dst_ref=mine.at[piece], send_sem=send_sem.at[c],
            recv_sem=recv_sem.at[c], device_id=_peer(sizes, far, 0), device_id_type=mesh,
        )
        copy.start()
        to_far.append(copy)
    to_core = pltpu.make_async_remote_copy(
        src_ref=src_ref, dst_ref=mine, send_sem=send_sem.at[chunks],
        recv_sem=recv_sem.at[chunks], device_id=_peer(sizes, core_shift, 0),
        device_id_type=mesh,
    )
    to_core.start()
    far_cols = cols(lax.rem(me + far, count))
    for c in range(chunks):
        piece = pl.ds(c * part, part)
        to_far[c].wait_recv()
        pltpu.make_async_remote_copy(
            src_ref=far_cols.at[piece], dst_ref=far_cols.at[piece],
            send_sem=send_sem.at[chunks + 1], recv_sem=recv_sem.at[chunks + 1],
            device_id=_peer(sizes, core_shift, 0), device_id_type=mesh,
        ).start()
    for c in range(chunks):
        to_far[c].wait_send()
    to_core.wait()
    pltpu.make_async_remote_copy(
        src_ref=far_cols, dst_ref=far_cols, send_sem=send_sem.at[chunks + 1],
        recv_sem=recv_sem.at[chunks + 1], device_id=_peer(sizes, core_shift, 0),
        device_id_type=mesh,
    ).wait()


def layer_gather(sizes, slab, collective_id):
    count = sizes[0]
    any_spec = pl.BlockSpec(memory_space=pl.ANY)
    others = pl.pallas_call(
        lambda *refs: _layer_gather_kernel(sizes, *refs),
        out_shape=jax.ShapeDtypeStruct((slab.shape[0], slab.shape[1] * count), slab.dtype),
        in_specs=[any_spec],
        out_specs=any_spec,
        scratch_shapes=[
            pltpu.SemaphoreType.DMA((6,)),
            pltpu.SemaphoreType.DMA((6,)),
        ],
        compiler_params=pltpu.CompilerParams(collective_id=collective_id, has_side_effects=True),
        name="layer_gather",
    )(slab)
    me = lax.axis_index("layer")
    return lax.dynamic_update_slice_in_dim(others, slab, me * slab.shape[1], axis=1)


def shifted(value, axis, steps):
    count = lax.axis_size(axis)
    pairs = [(source, (source + steps) % count) for source in range(count)]
    return lax.ppermute(value, axis, pairs)


def skew_rows(band, shift_total):
    n, bs, width = band.shape
    pieces = [
        jnp.pad(band[i], ((0, 0), (i * bs, (shift_total - i) * bs))) for i in range(n)
    ]
    return jnp.stack(pieces, axis=0)


def body(density, pattern):
    rows_dev, slab_cols = density.shape
    block_rows, slab_offsets = pattern.shape
    bs = rows_dev // block_rows
    layers = lax.axis_size("layer")
    offsets = slab_offsets * layers
    half = offsets // 2
    layer_id = lax.axis_index("layer")
    sizes = tuple(lax.axis_size(name) for name in MESH_AXES)

    keep = pattern.astype(jnp.bfloat16)[:, None, :, None]
    masked = (density.reshape(block_rows, bs, slab_offsets, bs) * keep).reshape(rows_dev, slab_cols)
    own_band = layer_gather(sizes, masked, 1)

    total_rows = block_rows + offsets - 1
    width = slab_offsets + block_rows - 1
    pad_l = total_rows - 1 - half
    far = layers // 2
    width = width + width % 2
    pair_width = width + slab_offsets
    reach = (half + block_rows - 1) // block_rows
    total_blocks = max(
        slab_offsets * (layers - 1) + block_rows * reach + pad_l + width,
        slab_offsets * (layers - 2) + block_rows + pad_l + pair_width,
        pad_l + offsets,
    )
    total_blocks += total_blocks % 2
    pad_r = total_blocks - offsets - pad_l
    band = jnp.pad(own_band.reshape(block_rows, bs, offsets * bs),
                   ((0, 0), (0, 0), (pad_l * bs, pad_r * bs)))
    moved = jnp.pad(own_band.reshape(block_rows, bs, offsets * bs),
                    ((0, 0), (0, 0), ((pad_l - 1) * bs, (pad_r + 1) * bs)))
    core = lax.rem(layer_id, 2)

    below = half
    above = total_rows - half - block_rows
    steps = []
    dist, need = 1, below
    while need > 0:
        take = min(block_rows, need)
        if dist == 1:
            lower_start = need - take
        else:
            steps.append((dist, block_rows - take, block_rows, need - take))
        need -= take
        dist += 1
    dist, need = 1, above
    while need > 0:
        take = min(block_rows, need)
        if dist == 1:
            upper_start = below + block_rows
        else:
            steps.append((-dist, 0, take, below + block_rows + (above - need)))
        need -= take
        dist += 1
    pair_steps = ((1, 0), (-1, block_rows))
    plan = (slab_offsets, block_rows, pad_l, width, pair_width, far, below,
            tuple(steps), pair_steps)
    right, pair_buf = row_exchange(sizes, plan, total_rows, 2 * block_rows, band, moved)
    pair_part = lax.dynamic_slice_in_dim(pair_buf, core * slab_offsets * bs, width * bs, axis=2)
    right = lax.dynamic_update_slice_in_dim(right, pair_part[:block_rows], lower_start, axis=0)
    right = lax.dynamic_update_slice_in_dim(right, pair_part[block_rows:], upper_start, axis=0)
    right = right.reshape(total_rows * bs, width * bs)

    pattern_f = pattern.astype(jnp.float32)[:, None, :, None]

    def product(left_band):
        rows_band = left_band.reshape(block_rows, bs, offsets * bs)
        group = block_rows // 2
        k_blocks = group - 1 + offsets
        n_blocks = group + slab_offsets
        n_blocks += n_blocks % 2
        pieces = []
        for g in range(2):
            first = g * group
            col0 = min(first - first % 2, width - n_blocks)
            left = skew_rows(rows_band[first:first + group], group - 1)
            left = left.reshape(group * bs, k_blocks * bs)
            part = right[first * bs:(first + k_blocks) * bs, col0 * bs:(col0 + n_blocks) * bs]
            dense = jnp.dot(left, part, preferred_element_type=jnp.float32)
            dense = dense.reshape(group, bs, n_blocks * bs)
            for ii in range(group):
                c = first + ii - col0
                pieces.append(dense[ii, :, c * bs:(c + slab_offsets) * bs])
        out = jnp.stack(pieces, axis=0)
        return out.reshape(block_rows, bs, slab_offsets, bs) * pattern_f

    square = product(own_band).astype(jnp.bfloat16)
    square_full = layer_gather(sizes, square.reshape(rows_dev, slab_cols), 1)
    cubic = product(square_full)
    purified = 3.0 * square.astype(jnp.float32) - 2.0 * cubic
    return purified.reshape(rows_dev, slab_cols)


def solution(mesh):
    placed = (P("row", "layer"), P("row", "layer"))
    return jax.shard_map(
        body, mesh=mesh, in_specs=placed, out_specs=P("row", "layer"), check_vma=False
    )
```

```python
import jax
import jax.numpy as jnp
from jax import lax
from jax.sharding import PartitionSpec as P
from jax.experimental import pallas as pl
from jax.experimental.pallas import tpu as pltpu

MESH_AXES = ("layer", "row")


def _peer(sizes, layer_shift, row_shift):
    layer = lax.axis_index("layer")
    row = lax.axis_index("row")
    return (
        lax.rem(layer + layer_shift + sizes[0], sizes[0]),
        lax.rem(row + row_shift + sizes[1], sizes[1]),
    )


def _greet(sizes, shifts):
    barrier = pltpu.get_barrier_semaphore()
    for layer_shift, row_shift in shifts:
        pl.semaphore_signal(barrier, inc=1, device_id=_peer(sizes, layer_shift, row_shift),
                            device_id_type=pl.DeviceIdType.MESH)
    pl.semaphore_wait(barrier, len(shifts))


def _row_exchange_kernel(sizes, plan, *refs):
    (slab_offsets, block_rows, pad_l, width, pair_width, far, own_start,
     steps, pair_steps) = plan
    band_ref, moved_ref, out_ref, pair_ref = refs[:4]
    send_sem, recv_sem, pair_send, pair_recv, fwd_send, fwd_recv, local_sem, stage = refs[4:]
    me = lax.axis_index("layer")
    core = lax.rem(me, 2)
    core_shift = 1 - 2 * core
    half_rows = block_rows // 2
    shifts = [(0, shift) for shift, _, _, _ in steps]
    shifts += [(far, shift) for shift, _ in pair_steps]
    _greet(sizes, shifts + [(core_shift, 0)])
    mesh = pl.DeviceIdType.MESH

    bs = band_ref.shape[1]

    def window(j, start, count, odd):
        first = pl.multiple_of((start - odd) * bs, 2 * bs)
        return (moved_ref if odd else band_ref).at[j, :, pl.ds(first, count * bs)]

    def row_copy(j, start, count, dst, send, recv, target, odd):
        return pltpu.make_async_remote_copy(
            src_ref=window(j, start, count, odd), dst_ref=dst,
            send_sem=send, recv_sem=recv, device_id=target, device_id_type=mesh,
        )

    def group(dst_rows, count, send, recv, target):
        return pltpu.make_async_remote_copy(
            src_ref=band_ref.at[pl.ds(0, dst_rows.shape[0]), :, pl.ds(0, count * bs)],
            dst_ref=dst_rows, send_sem=send, recv_sem=recv, device_id=target,
            device_id_type=mesh,
        )

    waits = []
    for k, (shift, first, last, row_start) in enumerate(steps):
        target = _peer(sizes, 0, shift)
        for j in range(first, last):
            start = me * slab_offsets + block_rows * shift - j + pad_l
            odd = (block_rows * shift - j + pad_l) % 2
            row_copy(j, start, width, out_ref.at[row_start + j - first],
                     send_sem.at[k], recv_sem.at[k], target, odd).start()
        waits.append(group(out_ref.at[pl.ds(row_start, last - first)], width,
                           send_sem.at[k], recv_sem.at[k], target))
    pair_base = (lax.rem(me + far, sizes[0]) - core) * slab_offsets
    pair_rows = []
    for k, (shift, pair_start) in enumerate(pair_steps):
        target = _peer(sizes, far, shift)
        for jj in range(half_rows):
            j = core * half_rows + jj
            start = pair_base + block_rows * shift - j + pad_l
            sems = (pair_send.at[k * half_rows + jj], pair_recv.at[k * half_rows + jj])
            for odd in (0, 1):
                @pl.when(lax.rem(block_rows * shift - j + pad_l, 2) == odd)
                def _():
                    row_copy(j, start, pair_width, pair_ref.at[pair_start + j],
                             *sems, target, odd).start()
            pair_rows.append(pltpu.make_async_remote_copy(
                src_ref=band_ref.at[j, :, pl.ds(0, pair_width * bs)],
                dst_ref=pair_ref.at[pair_start + j], send_sem=sems[0], recv_sem=sems[1],
                device_id=target, device_id_type=mesh,
            ))
    for j in range(block_rows):
        start = me * slab_offsets - j + pad_l
        odd = (pad_l - j) % 2
        pltpu.make_async_copy(window(j, start, width, odd), stage.at[j], local_sem.at[0]).start()
    for jj in range(half_rows):
        for k, (shift, pair_start) in enumerate(pair_steps):
            pair_rows[k * half_rows + jj].wait_recv()
            held = pair_ref.at[pair_start + core * half_rows + jj]
            pltpu.make_async_remote_copy(
                src_ref=held, dst_ref=held, send_sem=fwd_send.at[k], recv_sem=fwd_recv.at[k],
                device_id=_peer(sizes, core_shift, 0), device_id_type=mesh,
            ).start()
    pltpu.make_async_copy(band_ref.at[pl.ds(0, block_rows), :, pl.ds(0, width * bs)],
                          stage, local_sem.at[0]).wait()
    own_out = pltpu.make_async_copy(stage, out_ref.at[pl.ds(own_start, block_rows)],
                                    local_sem.at[1])
    own_out.start()
    for grp in waits:
        grp.wait()
    for copy in pair_rows:
        copy.wait_send()
    for k, (shift, pair_start) in enumerate(pair_steps):
        held = pair_ref.at[pl.ds(pair_start + core * half_rows, half_rows)]
        group(held, pair_width, fwd_send.at[k], fwd_recv.at[k],
              _peer(sizes, core_shift, 0)).wait()
    own_out.wait()


def row_exchange(sizes, plan, total_rows, pair_rows, band, moved):
    (slab_offsets, block_rows, pad_l, width, pair_width, far, own_start,
     steps, pair_steps) = plan
    bs = band.shape[1]
    any_spec = pl.BlockSpec(memory_space=pl.ANY)
    n, m = len(steps), len(pair_steps)
    return pl.pallas_call(
        lambda *refs: _row_exchange_kernel(sizes, plan, *refs),
        out_shape=(jax.ShapeDtypeStruct((total_rows, bs, width * bs), band.dtype),
                   jax.ShapeDtypeStruct((pair_rows, bs, pair_width * bs), band.dtype)),
        in_specs=[any_spec, any_spec],
        out_specs=(any_spec, any_spec),
        scratch_shapes=[
            pltpu.SemaphoreType.DMA((n,)),
            pltpu.SemaphoreType.DMA((n,)),
            pltpu.SemaphoreType.DMA((m * (block_rows // 2),)),
            pltpu.SemaphoreType.DMA((m * (block_rows // 2),)),
            pltpu.SemaphoreType.DMA((m,)),
            pltpu.SemaphoreType.DMA((m,)),
            pltpu.SemaphoreType.DMA((2,)),
            pltpu.VMEM((block_rows, bs, width * bs), band.dtype),
        ],
        compiler_params=pltpu.CompilerParams(collective_id=0, has_side_effects=True),
        name="row_exchange",
    )(band, moved)


def _layer_gather_kernel(sizes, *refs):
    src_ref, out_ref, send_sem, recv_sem = refs
    count = sizes[0]
    me = lax.axis_index("layer")
    width = src_ref.shape[1]
    core_shift = 1 - 2 * lax.rem(me, 2)
    far = count // 2
    _greet(sizes, [(far, 0), (core_shift, 0)])

    def cols(layer):
        return out_ref.at[:, pl.ds(pl.multiple_of(layer * width, width), width)]

    mine = cols(me)
    rows = src_ref.shape[0]
    chunks = 4 if rows % 32 == 0 else 1
    part = rows // chunks
    mesh = pl.DeviceIdType.MESH
    to_far = []
    for c in range(chunks):
        piece = pl.ds(c * part, part)
        copy = pltpu.make_async_remote_copy(
            src_ref=src_ref.at[piece], dst_ref=mine.at[piece], send_sem=send_sem.at[c],
            recv_sem=recv_sem.at[c], device_id=_peer(sizes, far, 0), device_id_type=mesh,
        )
        copy.start()
        to_far.append(copy)
    to_core = pltpu.make_async_remote_copy(
        src_ref=src_ref, dst_ref=mine, send_sem=send_sem.at[chunks],
        recv_sem=recv_sem.at[chunks], device_id=_peer(sizes, core_shift, 0),
        device_id_type=mesh,
    )
    to_core.start()
    far_cols = cols(lax.rem(me + far, count))
    for c in range(chunks):
        piece = pl.ds(c * part, part)
        to_far[c].wait_recv()
        pltpu.make_async_remote_copy(
            src_ref=far_cols.at[piece], dst_ref=far_cols.at[piece],
            send_sem=send_sem.at[chunks + 1], recv_sem=recv_sem.at[chunks + 1],
            device_id=_peer(sizes, core_shift, 0), device_id_type=mesh,
        ).start()
    for c in range(chunks):
        to_far[c].wait_send()
    to_core.wait()
    pltpu.make_async_remote_copy(
        src_ref=far_cols, dst_ref=far_cols, send_sem=send_sem.at[chunks + 1],
        recv_sem=recv_sem.at[chunks + 1], device_id=_peer(sizes, core_shift, 0),
        device_id_type=mesh,
    ).wait()


def layer_gather(sizes, slab, collective_id):
    count = sizes[0]
    any_spec = pl.BlockSpec(memory_space=pl.ANY)
    others = pl.pallas_call(
        lambda *refs: _layer_gather_kernel(sizes, *refs),
        out_shape=jax.ShapeDtypeStruct((slab.shape[0], slab.shape[1] * count), slab.dtype),
        in_specs=[any_spec],
        out_specs=any_spec,
        scratch_shapes=[
            pltpu.SemaphoreType.DMA((6,)),
            pltpu.SemaphoreType.DMA((6,)),
        ],
        compiler_params=pltpu.CompilerParams(collective_id=collective_id, has_side_effects=True),
        name="layer_gather",
    )(slab)
    me = lax.axis_index("layer")
    return lax.dynamic_update_slice_in_dim(others, slab, me * slab.shape[1], axis=1)


def shifted(value, axis, steps):
    count = lax.axis_size(axis)
    pairs = [(source, (source + steps) % count) for source in range(count)]
    return lax.ppermute(value, axis, pairs)


def skew_rows(band, shift_total):
    n, bs, width = band.shape
    pieces = [
        jnp.pad(band[i], ((0, 0), (i * bs, (shift_total - i) * bs))) for i in range(n)
    ]
    return jnp.stack(pieces, axis=0)


def body(density, pattern):
    rows_dev, slab_cols = density.shape
    block_rows, slab_offsets = pattern.shape
    bs = rows_dev // block_rows
    layers = lax.axis_size("layer")
    offsets = slab_offsets * layers
    half = offsets // 2
    layer_id = lax.axis_index("layer")
    sizes = tuple(lax.axis_size(name) for name in MESH_AXES)

    keep = pattern.astype(jnp.bfloat16)[:, None, :, None]
    masked = (density.reshape(block_rows, bs, slab_offsets, bs) * keep).reshape(rows_dev, slab_cols)
    own_band = layer_gather(sizes, masked, 1)

    total_rows = block_rows + offsets - 1
    width = slab_offsets + block_rows - 1
    pad_l = total_rows - 1 - half
    far = layers // 2
    width = width + width % 2
    pair_width = width + slab_offsets
    reach = (half + block_rows - 1) // block_rows
    total_blocks = max(
        slab_offsets * (layers - 1) + block_rows * reach + pad_l + width,
        slab_offsets * (layers - 2) + block_rows + pad_l + pair_width,
        pad_l + offsets,
    )
    total_blocks += total_blocks % 2
    pad_r = total_blocks - offsets - pad_l
    band = jnp.pad(own_band.reshape(block_rows, bs, offsets * bs),
                   ((0, 0), (0, 0), (pad_l * bs, pad_r * bs)))
    moved = jnp.pad(own_band.reshape(block_rows, bs, offsets * bs),
                    ((0, 0), (0, 0), ((pad_l - 1) * bs, (pad_r + 1) * bs)))
    core = lax.rem(layer_id, 2)

    below = half
    above = total_rows - half - block_rows
    steps = []
    dist, need = 1, below
    while need > 0:
        take = min(block_rows, need)
        if dist == 1:
            lower_start = need - take
        else:
            steps.append((dist, block_rows - take, block_rows, need - take))
        need -= take
        dist += 1
    dist, need = 1, above
    while need > 0:
        take = min(block_rows, need)
        if dist == 1:
            upper_start = below + block_rows
        else:
            steps.append((-dist, 0, take, below + block_rows + (above - need)))
        need -= take
        dist += 1
    pair_steps = ((1, 0), (-1, block_rows))
    plan = (slab_offsets, block_rows, pad_l, width, pair_width, far, below,
            tuple(steps), pair_steps)
    right, pair_buf = row_exchange(sizes, plan, total_rows, 2 * block_rows, band, moved)
    pair_part = lax.dynamic_slice_in_dim(pair_buf, core * slab_offsets * bs, width * bs, axis=2)
    right = lax.dynamic_update_slice_in_dim(right, pair_part[:block_rows], lower_start, axis=0)
    right = lax.dynamic_update_slice_in_dim(right, pair_part[block_rows:], upper_start, axis=0)
    right = right.reshape(total_rows * bs, width * bs)

    pattern_f = pattern.astype(jnp.float32)[:, None, :, None]

    def product(left_band):
        rows_band = left_band.reshape(block_rows, bs, offsets * bs)
        group = 2 if block_rows % 2 == 0 else block_rows
        k_blocks = group - 1 + offsets
        n_blocks = group + slab_offsets
        n_blocks += n_blocks % 2
        pieces = []
        for g in range(block_rows // group):
            first = g * group
            col0 = min(first - first % 2, width - n_blocks)
            left = skew_rows(rows_band[first:first + group], group - 1)
            left = left.reshape(group * bs, k_blocks * bs)
            part = right[first * bs:(first + k_blocks) * bs, col0 * bs:(col0 + n_blocks) * bs]
            dense = jnp.dot(left, part, preferred_element_type=jnp.float32)
            dense = dense.reshape(group, bs, n_blocks * bs)
            for ii in range(group):
                c = first + ii - col0
                pieces.append(dense[ii, :, c * bs:(c + slab_offsets) * bs])
        out = jnp.stack(pieces, axis=0)
        return out.reshape(block_rows, bs, slab_offsets, bs) * pattern_f

    square = product(own_band).astype(jnp.bfloat16)
    square_full = layer_gather(sizes, square.reshape(rows_dev, slab_cols), 1)
    cubic = product(square_full)
    purified = 3.0 * square.astype(jnp.float32) - 2.0 * cubic
    return purified.reshape(rows_dev, slab_cols)


def solution(mesh):
    placed = (P("row", "layer"), P("row", "layer"))
    return jax.shard_map(
        body, mesh=mesh, in_specs=placed, out_specs=P("row", "layer"), check_vma=False
    )
```
